32 devices in a mesh: ri: 16 (over z, y, core), rj: 2 (over x).
Axes of the slice: x: 2, y: 2, z: 4, core: 2. Of those that a mesh axis runs over, the one named last changes fastest.
Arguments:
- pair: bfloat16 [64, 512, 512], P(None, 'ri', 'rj'), may hold values from -6 to 6
- conv1_weight: bfloat16 [3, 3, 64, 64], replicated, may hold values from -0.25 to 0.25
- conv1_bias: float32 [64], replicated, may hold values from -3 to 3
- conv2_weight: bfloat16 [3, 3, 64, 64], replicated, may hold values from -0.25 to 0.25
- conv2_bias: float32 [64], replicated, may hold values from -3 to 3
- head_weight: bfloat16 [64, 37], replicated, may hold values from -60 to 60, as said below
- head_bias: float32 [37], replicated, may hold values from -4 to 4
- bins: int32 [512, 512], P('ri', 'rj'), may hold values from 0 to 36
- mask: int32 [512], replicated, may hold values from 0 to 1, as said below
Outputs:
- grad_pair: bfloat16 [64, 512, 512], P(None, 'ri', 'rj')
- grad_conv1_weight: float32 [3, 3, 64, 64], replicated
- grad_conv1_bias: float32 [64], replicated
- grad_conv2_weight: float32 [3, 3, 64, 64], replicated
- grad_conv2_bias: float32 [64], replicated
- grad_head_weight: float32 [64, 37], replicated
- grad_head_bias: float32 [37], replicated
The draws below stay inside these ranges and needn't reach their ends.
Inputs may be any that keep to these rules, and one draw needn't show every extreme that they name: `mask`: residue 0 is always valid; all valid residues lie before some position that is at least 256. `head_weight`: some bins' weights may reach tens in magnitude, so that logits may reach hundreds.
All inputs are finite; a program needn't handle non-finite values.
Results may differ from the reference program's by a relative error of at most 0.012.
The reference program's roundings to bfloat16 on the way (of `inner_act`, `hidden`, `outer_half` and `inner_half`) count: a program that leaves them out, or rounds other values in their place, can miss the bound.
Values may be sent and summed in bfloat16 or wider, within the bound.
A program may use at most 128 MiB of HBM per device.

```python
import jax
import jax.numpy as jnp
from jax import lax

C = 64
NB = 37
KERNEL_TAPS = 3
DILATION_RATE = 8
L = 512


def draw_head_weight(key, part):
    base_key = jax.random.fold_in(key, 23)
    key_one = jax.random.fold_in(base_key, 0)
    spread_scale = C ** (-0.5)
    result = jnp.clip(jax.random.normal(key_one, (C, NB), jnp.float32), -4.0, 4.0) * spread_scale
    return result.astype(jnp.bfloat16)


def draw_mask(key, part):
    base_key = jax.random.fold_in(key, 11)
    key_length, key_keep = jax.random.split(base_key)
    length_cut = jax.random.randint(key_length, (), L // 2, L + 1)
    keeper = jax.random.randint(key_keep, (L,), 0, 10)
    position = jnp.arange(L, dtype=jnp.int32)
    valid = (position < length_cut) & (keeper > 0) | (position == 0)
    return valid.astype(jnp.int32)


def place_ends(values, rng, least, top_value):
    longest = values.shape.index(max(values.shape))
    spots = []
    for shift in (0, 1):
        where = [jax.random.randint(jax.random.fold_in(rng, axis), (), 0, length) for axis, length in enumerate(values.shape)]
        where[longest] = (where[longest] + shift) % values.shape[longest]
        spots.append(tuple(where))
    return values.at[spots[0]].set(least).at[spots[1]].set(top_value)


def shard_levels(rng, extent, pieces, least, high):
    gain, own = 1.0, jax.random.fold_in(rng, 6)
    for dim, parts in pieces:
        draws = jnp.exp(jax.random.uniform(jax.random.fold_in(own, dim), (parts,), jnp.float32, least / len(pieces), high / len(pieces)))
        gain = gain * jnp.repeat(draws, extent[dim] // parts).reshape([-1 if axis == dim else 1 for axis in range(len(extent))])
    return gain


def scatter_about(rng, extent, deviation, limit, cuts=(), kind=jnp.bfloat16):
    values = deviation * jax.random.normal(rng, extent, jnp.float32)
    if cuts:
        values = values * shard_levels(rng, extent, cuts, -0.22, 0.18)
    return jnp.clip(values, -limit, limit).astype(kind)


def setup_inputs(seed: int = 0) -> dict:
    seeds = jax.random.split(jax.random.key(seed), 10)
    return {
        "pair": scatter_about(seeds[0], (C, L, L), 1.0, 6.0, ((1, 16), (2, 2))),
        "conv1_weight": scatter_about(seeds[1], (KERNEL_TAPS, KERNEL_TAPS, C, C), (KERNEL_TAPS * KERNEL_TAPS * C) ** -0.5, 0.25),
        "conv1_bias": scatter_about(seeds[2], (C,), 0.5, 3.0, (), jnp.float32),
        "conv2_weight": scatter_about(seeds[3], (KERNEL_TAPS, KERNEL_TAPS, C, C), (KERNEL_TAPS * KERNEL_TAPS * C) ** -0.5, 0.25),
        "conv2_bias": scatter_about(seeds[4], (C,), 0.5, 3.0, (), jnp.float32),
        "head_weight": draw_head_weight(jax.random.fold_in(seeds[9], 71), 0),
        "head_bias": scatter_about(seeds[6], (NB,), 1.0, 4.0, (), jnp.float32),
        "bins": place_ends(jax.random.randint(seeds[7], (L, L), 0, NB), jax.random.fold_in(seeds[7], 1), 0, NB - 1).astype(jnp.int32),
        "mask": draw_mask(jax.random.fold_in(seeds[9], 71), 0),
    }


def activate(value):
    return jnp.where(value > 0, value, jnp.expm1(jnp.minimum(value, 0.0)))


def activate_slope(value):
    return jnp.where(value > 0, 1.0, jnp.exp(jnp.minimum(value, 0.0)))


def rounded(value):
    return lax.optimization_barrier(value.astype(jnp.bfloat16))


def padded_input(field):
    border_margin = DILATION_RATE * (KERNEL_TAPS // 2)
    return jnp.pad(field, ((0, 0), (border_margin, border_margin), (border_margin, border_margin)))


def dilated(padded_field, weight):
    return lax.conv_general_dilated(
        padded_field[None].astype(jnp.float32), weight.astype(jnp.float32), (1, 1), [(0, 0), (0, 0)],
        rhs_dilation=(DILATION_RATE, DILATION_RATE), dimension_numbers=("NCHW", "HWIO", "NCHW"),
        precision=lax.Precision.HIGHEST)[0]


def flipped(weight):
    return jnp.transpose(weight[::-1, ::-1], (0, 1, 3, 2))


def tap_sums(padded_field, grad):
    row_extent = grad.shape[1]
    column_extent = grad.shape[2]
    widened_field = padded_field.astype(jnp.float32)
    grad_wide = grad.astype(jnp.float32)
    tap_rows = []
    for row_stride in range(KERNEL_TAPS):
        across = []
        for column_stride in range(KERNEL_TAPS):
            sliding_window = widened_field[:, DILATION_RATE * row_stride:DILATION_RATE * row_stride + row_extent, DILATION_RATE * column_stride:DILATION_RATE * column_stride + column_extent]
            across.append(jnp.einsum("cij,dij->cd", sliding_window, grad_wide, precision=lax.Precision.HIGHEST))
        tap_rows.append(jnp.stack(across))
    return jnp.stack(tap_rows)


def project(weight_wide, field):
    return jnp.einsum("ck,cij->kij", weight_wide, field.astype(jnp.float32), precision=lax.Precision.HIGHEST)


def reference(pair, conv1_weight, conv1_bias, conv2_weight, conv2_bias, head_weight, head_bias, bins, mask):
    valid = mask.astype(jnp.float32)
    pair_mask = valid[:, None] * valid[None, :]
    n_valid = jnp.sum(valid)
    pair_pad = padded_input(pair)
    inner = dilated(pair_pad, conv1_weight) + conv1_bias[:, None, None]
    inner_act = rounded(activate(inner))
    act_pad = padded_input(inner_act)
    outer = dilated(act_pad, conv2_weight) + conv2_bias[:, None, None]
    summed = pair.astype(jnp.float32) + outer
    hidden = rounded(pair_mask[None] * activate(summed))
    mirrored = jnp.transpose(hidden, (0, 2, 1))
    weight_wide = head_weight.astype(jnp.float32)
    logits = 0.5 * (project(weight_wide, hidden) + project(weight_wide, mirrored)) + head_bias[:, None, None]
    peak_logit = jnp.max(logits, axis=0, keepdims=True)
    powered = jnp.exp(logits - peak_logit)
    chance = powered / jnp.sum(powered, axis=0, keepdims=True)
    onehot = (bins[None, :, :] == jnp.arange(NB, dtype=jnp.int32)[:, None, None]).astype(jnp.float32)
    error = pair_mask[None] * (chance - onehot)
    symmetric = 0.5 * (hidden.astype(jnp.float32) + mirrored.astype(jnp.float32))
    grad_head_weight = jnp.einsum("cij,kij->ck", symmetric, error, precision=lax.Precision.HIGHEST) / n_valid
    grad_head_bias = jnp.sum(error, axis=(1, 2)) / n_valid
    slope = jnp.einsum("ck,kij->cij", weight_wide, error, precision=lax.Precision.HIGHEST)
    outer_grad = 0.5 * (slope + jnp.transpose(slope, (0, 2, 1))) * pair_mask[None] * activate_slope(summed)
    outer_half = rounded(outer_grad)
    grad_conv2_weight = tap_sums(act_pad, outer_half) / n_valid
    grad_conv2_bias = jnp.sum(outer_grad, axis=(1, 2)) / n_valid
    inner_grad = dilated(padded_input(outer_half), flipped(conv2_weight)) * activate_slope(inner)
    inner_half = rounded(inner_grad)
    grad_conv1_weight = tap_sums(pair_pad, inner_half) / n_valid
    grad_conv1_bias = jnp.sum(inner_grad, axis=(1, 2)) / n_valid
    grad_pair = (outer_grad + dilated(padded_input(inner_half), flipped(conv1_weight))).astype(jnp.bfloat16)
    return (grad_pair, grad_conv1_weight, grad_conv1_bias, grad_conv2_weight, grad_conv2_bias,
            grad_head_weight, grad_head_bias)
```

```python
import functools

import jax
import jax.numpy as jnp
from jax import lax
from jax.experimental import pallas as pl
from jax.experimental.pallas import tpu as pltpu
from jax.sharding import PartitionSpec as P

TAPS = 3
STEP = 8
CHANS = 64
LANES = 128
BINS = 40
MESH = pl.DeviceIdType.MESH
F32 = jnp.float32
BF16 = jnp.bfloat16
PAIR, ACT, OUTER, INNER = range(4)
SIDES = ((-1, 0), (1, 0), (0, -1), (0, 1), (-1, -1), (-1, 1), (1, -1), (1, 1))
GROUP = 4
CONV_ROWS = TAPS * TAPS * CHANS // 2


def dot_nt(a, b):
    return lax.dot_general(a, b, (((1,), (1,)), ((), ())), preferred_element_type=F32)


def dot_tn(a, b):
    return lax.dot_general(a, b, (((0,), (0,)), ((), ())), preferred_element_type=F32)


def dot_nn(a, b):
    return jnp.dot(a, b, preferred_element_type=F32)


def halves_mask(shape):
    return lax.broadcasted_iota(jnp.int32, shape, len(shape) - 1) < CHANS


def chunk_rows(used, chunks):
    return -(-used // (8 * chunks)) * 8


def scratch_list(rows, cols, nrow, ncol):
    pairs = rows // 2
    count = cols // rows
    near = GROUP * ncol
    far = nrow // GROUP
    rows_a = chunk_rows(CONV_ROWS + 8, near)
    rows_b = chunk_rows(CONV_ROWS + BINS + 8, near)
    dma = pltpu.SemaphoreType.DMA
    items = dict(
        p32=pltpu.VMEM((cols // LANES, CHANS * rows, LANES), F32),
        qa=pltpu.VMEM((4, pairs + STEP, cols, LANES), BF16),
        qb=pltpu.VMEM((4, pairs + STEP, cols + 2 * STEP, LANES), BF16),
        up=pltpu.VMEM((4, STEP, cols // 2, LANES), BF16),
        down=pltpu.VMEM((4, STEP, cols // 2, LANES), BF16),
        left=pltpu.VMEM((4, pairs, 2 * STEP, LANES), BF16),
        right=pltpu.VMEM((4, pairs, 2 * STEP, LANES), BF16),
        rows_in=pltpu.VMEM((4, 2, STEP, cols // 2, LANES), BF16),
        cols_in=pltpu.VMEM((4, 2, pairs, 2 * STEP, LANES), BF16),
        corner_in=pltpu.VMEM((4, 4, STEP, 2 * STEP, LANES), BF16),
        xr=pltpu.VMEM((pairs, cols, LANES), BF16),
        sl1=pltpu.VMEM((pairs, cols, LANES), F32),
        sl2=pltpu.VMEM((pairs, cols, LANES), F32),
        og=pltpu.VMEM((pairs, cols, LANES), F32),
        hid=pltpu.VMEM((pairs, cols, LANES), BF16),
        hidp=pltpu.VMEM((pairs, cols, LANES), BF16),
        grad=pltpu.VMEM((pairs, cols, LANES), BF16),
        mirror=pltpu.VMEM((count, pairs, rows, LANES), BF16),
        m32=pltpu.VMEM((count, pairs * rows, LANES), F32),
        binsend=pltpu.VMEM((cols, LANES), BF16),
        bins_in=pltpu.VMEM((count, rows, LANES), BF16),
        binsp=pltpu.VMEM((2, rows, cols), F32),
        ww=pltpu.VMEM((4, TAPS * 2 * LANES, LANES), BF16),
        wb=pltpu.VMEM((2 * BINS, LANES), BF16),
        wb2=pltpu.VMEM((4 * BINS, LANES), BF16),
        hwp=pltpu.VMEM((CHANS, LANES), F32),
        small=pltpu.VMEM((8, LANES), F32),
        hbias=pltpu.VMEM((BINS, cols), F32),
        colm=pltpu.VMEM((cols, LANES), F32),
        colp=pltpu.VMEM((BINS, cols), F32),
        acc_t=pltpu.VMEM((2, LANES, TAPS * 2 * LANES), F32),
        acc_b=pltpu.VMEM((2, 8, LANES), F32),
        acc_h=pltpu.VMEM((4 * BINS, LANES), F32),
        acc_e=pltpu.VMEM((BINS, cols), F32),
        own_a=pltpu.VMEM((near * rows_a, LANES), F32),
        own_b=pltpu.VMEM((near * rows_b, LANES), F32),
        slots_a=pltpu.VMEM((near, rows_a, LANES), F32),
        slots_b=pltpu.VMEM((near, rows_b, LANES), F32),
        mid_a=pltpu.VMEM((far, rows_a, LANES), F32),
        mid_b=pltpu.VMEM((far, rows_b, LANES), F32),
        all_a=pltpu.VMEM((near, rows_a, LANES), F32),
        all_b=pltpu.VMEM((near, rows_b, LANES), F32),
        halo_send=dma((4, 8)),
        halo_recv=dma((4, 8)),
        mir_send=dma((count, 4)),
        mir_recv=dma((count, 4)),
        mir_own=dma((4,)),
        bin_send=dma((count,)),
        bin_recv=dma((count,)),
        near_send=dma((2, 2, near)),
        near_recv=dma((2, 2, near)),
        far_send=dma((2, far)),
        far_recv=dma((2, far)),
    )
    return items


def mega_kernel(
    names, nrow, ncol,
    pair, mask_s, mask_v, w1, b1, w2, b2, hw, hb, bins, out_pair, out_a, out_b, *scratch
):
    sc = dict(zip(names, scratch))
    rows, cols = bins.shape
    pairs = rows // 2
    groups = pairs // STEP
    count = cols // rows
    half = cols // 2
    near = GROUP * ncol
    far = nrow // GROUP
    row = lax.axis_index("ri")
    column = lax.axis_index("rj")
    slot = lax.rem(row, count)
    far_column = lax.div(row, count)
    own_group = far_column == column
    spot = lax.rem(row, GROUP) + GROUP * column
    tier = lax.div(row, GROUP)
    barrier = pltpu.get_barrier_semaphore()

    qa, qb = sc["qa"], sc["qb"]

    def near_device(place):
        return (tier * GROUP + lax.rem(place, GROUP), lax.div(place, GROUP))

    def far_device(level):
        return (level * GROUP + lax.rem(row, GROUP), column)

    def side_exists(side):
        dr, dc = side
        there = None
        for step, here, size in ((dr, row, nrow), (dc, column, ncol)):
            if step:
                one = here > 0 if step < 0 else here < size - 1
                there = one if there is None else jnp.logical_and(there, one)
        return there

    def side_device(side):
        return (row + side[0], column + side[1])

    def meets_self(block):
        return jnp.logical_and(own_group, slot == block)

    def partner(block):
        return (count * column + block, far_column)

    for ref in (sc["rows_in"], sc["cols_in"], sc["corner_in"]):
        lead = ref.shape[:3]

        @pl.loop(0, lead[0] * lead[1])
        def _(at):
            ref[at // lead[1], at % lead[1]] = jnp.zeros(ref.shape[2:], ref.dtype)

    def signal(device):
        pl.semaphore_signal(barrier, inc=1, device_id=device, device_id_type=MESH)

    for side in SIDES:

        @pl.when(side_exists(side))
        def _():
            signal(side_device(side))

    for block in range(count):

        @pl.when(jnp.logical_not(meets_self(block)))
        def _():
            signal(partner(block))

    @pl.loop(1, near)
    def _(step):
        signal(near_device(lax.rem(spot + step, near)))

    @pl.loop(1, far)
    def _(step):
        signal(far_device(lax.rem(tier + step, far)))

    @pl.loop(0, CHANS, unroll=4)
    def _(chan):
        for tile in range(cols // LANES):
            sc["p32"][tile, pl.ds(chan * rows, rows), :] = pair[
                chan, :, tile * LANES : (tile + 1) * LANES
            ].astype(F32)

    zero8 = jnp.zeros((STEP, LANES), F32)
    low = halves_mask((half, LANES))

    def publish(field, at, value):
        turned = pltpu.roll(value, CHANS, 1)
        plain = turned.astype(BF16)
        wide = jnp.concatenate([zero8, turned, zero8], axis=0).astype(BF16)
        qa[field, at, :, CHANS:] = plain[:, CHANS:]
        qa[field, at + STEP, :, :CHANS] = plain[:, :CHANS]
        qb[field, at, :, CHANS:] = wide[:, CHANS:]
        qb[field, at + STEP, :, :CHANS] = wide[:, :CHANS]
        sc["left"][field, at] = value[: 2 * STEP].astype(BF16)
        sc["right"][field, at] = value[cols - 2 * STEP :].astype(BF16)
        return turned

    def pack_up(field, at, value, turned):
        sc["up"][field, at] = jnp.where(low, value[:half], turned[half:]).astype(BF16)

    def pack_down(field, at, value, turned):
        sc["down"][field, at] = jnp.where(low, turned[:half], value[half:]).astype(BF16)

    last = slice((groups - 1) * STEP, groups * STEP)
    first = slice(0, STEP)

    def halo_source(field, side):
        dr, dc = side
        if dc == 0:
            return sc["up" if dr < 0 else "down"].at[field]
        edge = sc["left" if dc < 0 else "right"].at[field]
        if dr == 0:
            return edge
        return edge.at[first if dr < 0 else last]

    def halo_target(field, side):
        dr, dc = side
        if dc == 0:
            return sc["rows_in"].at[field, 0 if dr < 0 else 1]
        if dr == 0:
            return sc["cols_in"].at[field, 0 if dc < 0 else 1]
        return sc["corner_in"].at[field, (0 if dr < 0 else 2) + (0 if dc < 0 else 1)]

    def halo_copy(field, index):
        side = SIDES[index]
        back = (-side[0], -side[1])
        return pltpu.make_async_remote_copy(
            src_ref=halo_source(field, side),
            dst_ref=halo_target(field, back),
            send_sem=sc["halo_send"].at[field, index],
            recv_sem=sc["halo_recv"].at[field, SIDES.index(back)],
            device_id=side_device(side),
            device_id_type=MESH,
        )

    def halo_arrival(field, index):
        side = SIDES[index]
        return pltpu.make_async_remote_copy(
            src_ref=halo_source(field, side),
            dst_ref=halo_target(field, side),
            send_sem=sc["halo_send"].at[field, index],
            recv_sem=sc["halo_recv"].at[field, index],
            device_id=side_device(side),
            device_id_type=MESH,
        )

    def send_halo(field, wanted):
        for index, side in enumerate(SIDES):
            if side[0] in wanted:

                @pl.when(side_exists(side))
                def _():
                    halo_copy(field, index).start()

    def wait_halo(field):
        for index, side in enumerate(SIDES):

            @pl.when(side_exists(side))
            def _():
                halo_arrival(field, index).wait()

    def place_halo(field):
        @pl.loop(0, STEP)
        def _(at):
            above = sc["rows_in"][field, 0, at].astype(F32)
            wide = jnp.concatenate([above, pltpu.roll(above, CHANS, 1)], axis=0)
            qa[field, at, :, :CHANS] = wide.astype(BF16)[:, :CHANS]
            west = pltpu.roll(sc["corner_in"][field, 0, at].astype(F32), CHANS, 1)[STEP:]
            east = pltpu.roll(sc["corner_in"][field, 1, at].astype(F32), CHANS, 1)[:STEP]
            wide = jnp.concatenate([west, wide, east], axis=0).astype(BF16)
            qb[field, at, :, :CHANS] = wide[:, :CHANS]
            below = sc["rows_in"][field, 1, at].astype(F32)
            wide = jnp.concatenate([pltpu.roll(below, CHANS, 1), below], axis=0)
            qa[field, pairs + at, :, CHANS:] = wide.astype(BF16)[:, CHANS:]
            west = pltpu.roll(sc["corner_in"][field, 2, at].astype(F32), CHANS, 1)[STEP:]
            east = pltpu.roll(sc["corner_in"][field, 3, at].astype(F32), CHANS, 1)[:STEP]
            wide = jnp.concatenate([west, wide, east], axis=0).astype(BF16)
            qb[field, pairs + at, :, CHANS:] = wide[:, CHANS:]

        @pl.loop(0, pairs, unroll=2)
        def _(at):
            for edge, side in ((0, "left"), (1, "right")):
                own = sc[side][field, at].astype(F32)
                come = sc["cols_in"][field, edge, at].astype(F32)
                if edge == 0:
                    both = jnp.concatenate([come[STEP:], own[:STEP]], axis=0)
                    spots = slice(0, 2 * STEP)
                else:
                    both = jnp.concatenate([own[STEP:], come[:STEP]], axis=0)
                    spots = slice(cols, cols + 2 * STEP)
                both = pltpu.roll(both, CHANS, 1).astype(BF16)
                qb[field, at, spots, CHANS:] = both[:, CHANS:]
                qb[field, at + STEP, spots, :CHANS] = both[:, :CHANS]

    def taps(field, at):
        return jnp.concatenate(
            [
                qb[field, at, :cols, :],
                qb[field, at + STEP, :cols, :],
                qa[field, at],
                qa[field, at + STEP],
                qb[field, at, 2 * STEP :, :],
                qb[field, at + STEP, 2 * STEP :, :],
            ],
            axis=1,
        )

    def conv(field, which, at):
        return dot_nn(taps(field, at), sc["ww"][which])

    def add_taps(field, which):
        sc["acc_t"][which] = jnp.zeros(sc["acc_t"].shape[1:], F32)

        @pl.loop(0, pairs, unroll=2)
        def _(at):
            sc["acc_t"][which] += dot_tn(sc["grad"][at], taps(field, at))

    def row_of(group, at):
        return 2 * STEP * group + at

    def column_sums(value):
        total = value[:STEP]
        for start in range(STEP, cols, STEP):
            total = total + value[start : start + STEP]
        return total

    with jax.named_scope("publish_pair"):
        for group in range(groups):

            @pl.loop(0, STEP, unroll=2)
            def _(at):
                line = row_of(group, at)
                value = []
                for tile in range(cols // LANES):
                    one = sc["p32"][tile, pl.ds(line, CHANS, stride=rows), :]
                    two = sc["p32"][tile, pl.ds(line + STEP, CHANS, stride=rows), :]
                    value.append(jnp.transpose(jnp.concatenate([one, two], axis=0)))
                value = jnp.concatenate(value, axis=0)
                place = group * STEP + at
                sc["xr"][place] = value.astype(BF16)
                turned = publish(PAIR, place, value)
                if group == 0:
                    pack_up(PAIR, at, value, turned)
                if group == groups - 1:
                    pack_down(PAIR, at, value, turned)

    text = bins[...].astype(F32)
    text = jnp.concatenate([text, jnp.zeros((LANES - rows, cols), F32)], axis=0)
    sc["binsend"][...] = jnp.transpose(text).astype(BF16)

    def bins_source(block):
        return sc["binsend"].at[pl.ds(block * rows, rows)]

    def bins_copy(block, at):
        return pltpu.make_async_remote_copy(
            src_ref=bins_source(block),
            dst_ref=sc["bins_in"].at[at],
            send_sem=sc["bin_send"].at[block],
            recv_sem=sc["bin_recv"].at[at],
            device_id=partner(block),
            device_id_type=MESH,
        )

    wait_count = 0
    for side in SIDES:
        wait_count = wait_count + side_exists(side).astype(jnp.int32)
    wait_count = wait_count + count - own_group.astype(jnp.int32)
    pl.semaphore_wait(barrier, wait_count + (near - 1) + (far - 1))

    send_halo(PAIR, (-1, 0, 1))
    for block in range(count):

        @pl.when(jnp.logical_not(meets_self(block)))
        def _():
            bins_copy(block, slot).start()

        @pl.when(meets_self(block))
        def _():
            sc["bins_in"][block] = sc["binsend"][pl.ds(block * rows, rows), :]

    with jax.named_scope("weights"):
        sc["ww"][...] = jnp.zeros(sc["ww"].shape, BF16)
        for which, (weight, flip) in enumerate(((w1, False), (w2, False), (w2, True), (w1, True))):
            for across in range(TAPS):
                for down in range(TAPS):
                    if flip:
                        piece = weight[TAPS - 1 - down, TAPS - 1 - across].astype(F32)
                        piece = jnp.transpose(piece).astype(BF16)
                    else:
                        piece = weight[down, across]
                    for part in range(2):
                        start = across * 2 * LANES + (down + part) * CHANS
                        sc["ww"][
                            which, start : start + CHANS, part * CHANS : (part + 1) * CHANS
                        ] = piece
        nbins = hw.shape[1]
        sc["hwp"][...] = jnp.zeros(sc["hwp"].shape, F32)
        sc["hwp"][:, :nbins] = hw[...].astype(F32)
        flat = jnp.transpose(sc["hwp"][...])[:BINS]
        none = jnp.zeros_like(flat)
        both = jnp.concatenate(
            [jnp.concatenate([flat, none], axis=1), jnp.concatenate([none, flat], axis=1)], axis=0
        )
        sc["wb"][...] = (0.5 * both).astype(BF16)
        sc["wb2"][...] = jnp.concatenate([both, both], axis=0).astype(BF16)
        sc["small"][...] = jnp.full((8, LANES), -1e30, F32)
        sc["small"][0:1, :nbins] = hb[...]
        spread = jnp.broadcast_to(sc["small"][0:1, :], (LANES, LANES))
        spread = jnp.transpose(spread)[:BINS]
        for start in range(0, cols, LANES):
            sc["hbias"][:, start : start + LANES] = spread
        sc["small"][0:1, :CHANS] = b1[...]
        sc["small"][0:1, CHANS:] = b1[...]
        sc["small"][1:2, :CHANS] = b2[...]
        sc["small"][1:2, CHANS:] = b2[...]
        natural = lax.broadcasted_iota(jnp.int32, (cols, cols), 0)
        placed = lax.broadcasted_iota(jnp.int32, (cols, cols), 1)
        goal = ((natural >> 3) & 1) * half + (natural >> 4) * STEP + (natural & 7)
        move = jnp.where(placed == goal, 1.0, 0.0).astype(BF16)
        ones_row = mask_v[pl.ds(column, 1), :].astype(F32)
        top = lax.broadcasted_iota(jnp.int32, (2 * STEP, cols), 0) == 0
        ones_row = jnp.where(top, jnp.broadcast_to(ones_row, (2 * STEP, cols)), 0.0).astype(BF16)
        sc["colm"][...] = dot_tn(ones_row, jnp.ones((2 * STEP, LANES), BF16))
        sc["colp"][...] = jnp.broadcast_to(dot_nn(ones_row, move)[0:1], (BINS, cols))
        sc["binsp"][0] = dot_nn(bins[...].astype(F32).astype(BF16), move)
        for ref in (sc["acc_b"], sc["acc_h"], sc["acc_e"]):
            ref[...] = jnp.zeros(ref.shape, F32)
        for ref in (sc["own_a"], sc["own_b"]):
            ref[CONV_ROWS:, :] = jnp.zeros((ref.shape[0] - CONV_ROWS, LANES), F32)

    lane_low = halves_mask((1, LANES))

    def valid(line):
        return mask_s[row * rows + line].astype(F32)

    def pair_mask(group, at):
        line = row_of(group, at)
        return sc["colm"][...] * jnp.where(lane_low, valid(line), valid(line + STEP))

    with jax.named_scope("wait_pair"):
        wait_halo(PAIR)
        place_halo(PAIR)

    with jax.named_scope("conv1"):
        for group in range(groups):

            @pl.loop(0, STEP, unroll=2)
            def _(at):
                place = group * STEP + at
                inner = conv(PAIR, 0, place) + sc["small"][0:1, :]
                power = jnp.exp(jnp.minimum(inner, 0.0))
                value = jnp.where(inner > 0, inner, power - 1.0)
                sc["sl1"][place] = jnp.where(inner > 0, 1.0, power)
                turned = publish(ACT, place, value)
                if group == 0:
                    pack_up(ACT, at, value, turned)
                if group == groups - 1:
                    pack_down(ACT, at, value, turned)

            send_halo(ACT, (-1,) if group == 0 else (0, 1))

    with jax.named_scope("wait_act"):
        wait_halo(ACT)
        place_halo(ACT)

    def mirror_source(block, group, part):
        return sc["hid"].at[
            pl.ds(group * STEP, STEP), pl.ds(block * rows + part * 2 * STEP, 2 * STEP)
        ]

    def mirror_target(at, group, part):
        return sc["mirror"].at[at, pl.ds(group * STEP, STEP), pl.ds(part * 2 * STEP, 2 * STEP)]

    def mirror_copy(block, at, group, part):
        piece = 2 * group + part
        return pltpu.make_async_remote_copy(
            src_ref=mirror_source(block, group, part),
            dst_ref=mirror_target(at, group, part),
            send_sem=sc["mir_send"].at[block, piece],
            recv_sem=sc["mir_recv"].at[at, piece],
            device_id=partner(block),
            device_id_type=MESH,
        )

    def mirror_own(block, group, part):
        return pltpu.make_async_copy(
            mirror_source(block, group, part),
            mirror_target(block, group, part),
            sc["mir_own"].at[2 * group + part],
        )

    with jax.named_scope("conv2"):
        for group in range(groups):

            @pl.loop(0, STEP, unroll=2)
            def _(at):
                place = group * STEP + at
                outer = conv(ACT, 1, place) + sc["small"][1:2, :]
                total = sc["xr"][place].astype(F32) + outer
                power = jnp.exp(jnp.minimum(total, 0.0))
                keep = pair_mask(group, at)
                hidden = keep * jnp.where(total > 0, total, power - 1.0)
                sc["sl2"][place] = keep * jnp.where(total > 0, 1.0, power)
                sc["hid"][place] = hidden.astype(BF16)
                order = [hidden[16 * t : 16 * t + 8] for t in range(cols // 16)]
                order += [hidden[16 * t + 8 : 16 * t + 16] for t in range(cols // 16)]
                sc["hidp"][place] = jnp.concatenate(order, axis=0).astype(BF16)

            for part in range(2):
                for block in range(count):

                    @pl.when(jnp.logical_not(meets_self(block)))
                    def _():
                        mirror_copy(block, slot, group, part).start()

                    @pl.when(meets_self(block))
                    def _():
                        mirror_own(block, group, part).start()

    with jax.named_scope("bins"):
        total = jnp.zeros((rows, cols), F32)
        for block in range(count):

            @pl.when(jnp.logical_not(meets_self(block)))
            def _():
                bins_copy(block, block).wait()

            part = move[block * rows : (block + 1) * rows]
            total = total + dot_nn(sc["bins_in"][block][:, :rows], part)
        sc["binsp"][1] = total

    bin_ids = lax.broadcasted_iota(jnp.int32, (BINS, cols), 0).astype(F32)

    def mirrored(line):
        parts = [sc["m32"][block, pl.ds(line, pairs, stride=rows), :] for block in range(count)]
        return jnp.concatenate(parts, axis=0).astype(BF16)

    for group in range(groups):
        with jax.named_scope("wait_mirror"):
            for sender in range(groups):
                for block in range(count):

                    @pl.when(jnp.logical_not(meets_self(block)))
                    def _():
                        mirror_copy(block, block, sender, group).wait()

                    @pl.when(meets_self(block))
                    def _():
                        mirror_own(block, sender, group).wait()

            @pl.loop(0, pairs, unroll=2)
            def _(at):
                for block in range(count):
                    start = pl.multiple_of(at * rows + group * 2 * STEP, 2 * STEP)
                    sc["m32"][block, pl.ds(start, 2 * STEP), :] = sc["mirror"][
                        block, at, group * 2 * STEP : (group + 1) * 2 * STEP, :
                    ].astype(F32)

        with jax.named_scope("head"):

            @pl.loop(0, STEP, unroll=2)
            def _(at):
                place = group * STEP + at
                own = dot_nt(sc["wb"][...], sc["hidp"][place])
                errors = []
                for part in range(2):
                    line = row_of(group, at) + part * STEP
                    other = dot_nt(sc["wb"][...], mirrored(line))
                    other = jnp.concatenate([other[:BINS], other[BINS:]], axis=1)
                    logits = own[part * BINS : (part + 1) * BINS] + other + sc["hbias"][...]
                    peak = jnp.max(logits, axis=0, keepdims=True)
                    powered = jnp.exp(logits - peak)
                    scale = 1.0 / jnp.sum(powered, axis=0, keepdims=True)
                    hits = jnp.where(sc["binsp"][0, pl.ds(line, 1), :] == bin_ids, 0.5, 0.0)
                    hits += jnp.where(sc["binsp"][1, pl.ds(line, 1), :] == bin_ids, 0.5, 0.0)
                    errors.append(sc["colp"][...] * valid(line) * (powered * scale - hits))
                sc["acc_e"][...] += errors[0] + errors[1]
                error = jnp.concatenate(errors, axis=0)
                coarse = error.astype(BF16)
                fine = (error - coarse.astype(F32)).astype(BF16)
                stack = jnp.concatenate([coarse, fine], axis=0)
                sc["acc_h"][...] += dot_nn(stack, sc["hidp"][place])
                slope = dot_tn(stack, sc["wb2"][...])
                order = []
                for t in range(cols // 16):
                    order += [slope[8 * t : 8 * t + 8], slope[half + 8 * t : half + 8 * t + 8]]
                value = jnp.concatenate(order, axis=0) * sc["sl2"][place]
                sc["og"][place] = value
                sc["grad"][place] = value.astype(BF16)
                sc["acc_b"][1] += column_sums(value)
                turned = publish(OUTER, place, value)
                if group == 0:
                    pack_up(OUTER, at, value, turned)
                if group == groups - 1:
                    pack_down(OUTER, at, value, turned)

        send_halo(OUTER, (-1,) if group == 0 else (0, 1))

    def near_one(kind, tag, step):
        tall = sc["slots_" + tag].shape[1]
        peer = lax.rem(spot + step, near)
        return pltpu.make_async_remote_copy(
            src_ref=sc["own_" + tag].at[pl.ds(pl.multiple_of(peer * tall, 8), tall)],
            dst_ref=sc["slots_" + tag].at[step],
            send_sem=sc["near_send"].at[kind, 0, step],
            recv_sem=sc["near_recv"].at[kind, 0, step],
            device_id=near_device(peer),
            device_id_type=MESH,
        )

    def far_one(kind, tag, step):
        return pltpu.make_async_remote_copy(
            src_ref=sc["mid_" + tag].at[tier],
            dst_ref=sc["mid_" + tag].at[tier],
            send_sem=sc["far_send"].at[kind, step],
            recv_sem=sc["far_recv"].at[kind, step],
            device_id=far_device(lax.rem(tier + step, far)),
            device_id_type=MESH,
        )

    def near_two(kind, tag, step):
        return pltpu.make_async_remote_copy(
            src_ref=sc["all_" + tag].at[spot],
            dst_ref=sc["all_" + tag].at[spot],
            send_sem=sc["near_send"].at[kind, 1, step],
            recv_sem=sc["near_recv"].at[kind, 1, step],
            device_id=near_device(lax.rem(spot + step, near)),
            device_id_type=MESH,
        )

    def pack_taps(which, own):
        both = jnp.transpose(sc["acc_t"][which])
        for across in range(TAPS):
            for down in range(TAPS):
                at = across * 2 * LANES + down * CHANS
                one = both[at : at + CHANS]
                two = pltpu.roll(both[at + CHANS : at + 2 * CHANS], CHANS, 1)
                total = one + two
                packed = jnp.where(
                    halves_mask((CHANS // 2, LANES)),
                    total[: CHANS // 2],
                    pltpu.roll(total[CHANS // 2 :], CHANS, 1),
                )
                start = (down * TAPS + across) * (CHANS // 2)
                own[start : start + CHANS // 2, :] = packed

    def start_sum(kind, tag):
        for step in range(1, near):
            near_one(kind, tag, step).start()

    def middle_sum(kind, tag):
        for step in range(1, near):
            near_one(kind, tag, step).wait()
        tall = sc["slots_" + tag].shape[1]
        total = sc["own_" + tag][pl.ds(pl.multiple_of(spot * tall, 8), tall), :]
        for step in range(1, near):
            total = total + sc["slots_" + tag][step]
        sc["mid_" + tag][tier] = total
        for step in range(1, far):
            far_one(kind, tag, step).start()

    def late_sum(kind, tag):
        for step in range(1, far):
            far_one(kind, tag, step).wait()
        total = sc["mid_" + tag][0]
        for level in range(1, far):
            total = total + sc["mid_" + tag][level]
        sc["all_" + tag][spot] = total
        for step in range(1, near):
            near_two(kind, tag, step).start()

    def end_sum(kind, tag, out):
        for step in range(1, near):
            near_two(kind, tag, step).wait()
        out[...] = sc["all_" + tag][...]

    with jax.named_scope("taps2"):
        add_taps(ACT, 1)
        pack_taps(1, sc["own_b"])
        both = sc["acc_h"][: 2 * BINS, :] + sc["acc_h"][2 * BINS :, :]
        both = both[:BINS] + pltpu.roll(both[BINS:], CHANS, 1)
        tally = jnp.sum(sc["acc_e"][...], axis=1, keepdims=True)
        sc["own_b"][CONV_ROWS : CONV_ROWS + BINS, :] = jnp.where(
            halves_mask((BINS, LANES)), both, jnp.broadcast_to(tally, (BINS, LANES))
        )
        sc["own_b"][CONV_ROWS + BINS : CONV_ROWS + BINS + 8, :] = sc["acc_b"][1]
        start_sum(1, "b")

    with jax.named_scope("wait_outer"):
        wait_halo(OUTER)
        place_halo(OUTER)

    with jax.named_scope("convt2"):
        for group in range(groups):

            @pl.loop(0, STEP, unroll=2)
            def _(at):
                place = group * STEP + at
                value = conv(OUTER, 2, place) * sc["sl1"][place]
                sc["grad"][place] = value.astype(BF16)
                sc["acc_b"][0] += column_sums(value)
                turned = publish(INNER, place, value)
                if group == 0:
                    pack_up(INNER, at, value, turned)
                if group == groups - 1:
                    pack_down(INNER, at, value, turned)

            send_halo(INNER, (-1,) if group == 0 else (0, 1))

    middle_sum(1, "b")

    with jax.named_scope("taps1"):
        add_taps(PAIR, 0)
        pack_taps(0, sc["own_a"])
        sc["own_a"][CONV_ROWS : CONV_ROWS + 8, :] = sc["acc_b"][0]
        start_sum(0, "a")
    late_sum(1, "b")

    with jax.named_scope("wait_inner"):
        wait_halo(INNER)
        place_halo(INNER)

    middle_sum(0, "a")
    with jax.named_scope("convt1"):
        for group in range(groups):

            @pl.loop(0, STEP, unroll=2)
            def _(at):
                place = group * STEP + at
                line = row_of(group, at)
                value = sc["og"][place] + conv(INNER, 3, place)
                for tile in range(cols // LANES):
                    turned = jnp.transpose(value[tile * LANES : (tile + 1) * LANES])
                    sc["p32"][tile, pl.ds(line, CHANS, stride=rows), :] = turned[:CHANS]
                    sc["p32"][tile, pl.ds(line + STEP, CHANS, stride=rows), :] = turned[CHANS:]

            if group == 0:
                late_sum(0, "a")

        @pl.loop(0, CHANS, unroll=4)
        def _(chan):
            for tile in range(cols // LANES):
                out_pair[chan, :, tile * LANES : (tile + 1) * LANES] = sc["p32"][
                    tile, pl.ds(chan * rows, rows), :
                ].astype(BF16)

    with jax.named_scope("end_sums"):
        end_sum(1, "b", out_b)
        end_sum(0, "a", out_a)


def finish_kernel(near, pair, sums_a, sums_b, mask_v, out_pair, c1w, c1b, c2w, c2b, hgw, hgb):
    out_pair[...] = pair[...]
    scale = 1.0 / jnp.sum(mask_v[...].astype(F32))
    for sums, weight, bias, extra in ((sums_a, c1w, c1b, 0), (sums_b, c2w, c2b, BINS)):
        for tap in range(TAPS * TAPS):
            start = tap * (CHANS // 2)
            value = sums[start : start + CHANS // 2, :] * scale
            weight[tap // TAPS, tap % TAPS, : CHANS // 2, :] = value[:, :CHANS]
            weight[tap // TAPS, tap % TAPS, CHANS // 2 :, :] = value[:, CHANS:]
        start = CONV_ROWS + extra
        total = jnp.sum(sums[start : start + 8, :], axis=0, keepdims=True) * scale
        bias[...] = total[:, :CHANS] + total[:, CHANS:]
    head = sums_b[CONV_ROWS : CONV_ROWS + BINS, :] * scale
    head = jnp.concatenate([head, jnp.zeros((LANES - BINS, LANES), F32)], axis=0)
    head = jnp.transpose(head)
    nbins = hgw.shape[1]
    hgw[...] = head[:CHANS, :nbins]
    hgb[...] = head[CHANS : CHANS + 1, :nbins]


def on_device(pair, w1, b1, w2, b2, hw, hb, bins, mask):
    nrow = lax.axis_size("ri")
    ncol = lax.axis_size("rj")
    rows, cols = bins.shape
    nbins = hw.shape[1]
    near = GROUP * ncol
    rows_a = chunk_rows(CONV_ROWS + 8, near)
    rows_b = chunk_rows(CONV_ROWS + BINS + 8, near)
    items = scratch_list(rows, cols, nrow, ncol)
    vmem = pl.BlockSpec(memory_space=pltpu.VMEM)
    smem = pl.BlockSpec(memory_space=pltpu.SMEM)
    mask_v = mask.reshape(ncol, cols)
    params = dict(vmem_limit_bytes=56 * 1024 * 1024)
    grad_pair, sums_a, sums_b = pl.pallas_call(
        functools.partial(mega_kernel, tuple(items), nrow, ncol),
        out_shape=[
            jax.ShapeDtypeStruct((CHANS, rows, cols), BF16),
            jax.ShapeDtypeStruct((near, rows_a, LANES), F32),
            jax.ShapeDtypeStruct((near, rows_b, LANES), F32),
        ],
        in_specs=[vmem, smem] + [vmem] * 8,
        out_specs=[vmem] * 3,
        scratch_shapes=list(items.values()),
        compiler_params=pltpu.CompilerParams(collective_id=0, has_side_effects=True, **params),
    )(
        pair, mask, mask_v, w1, b1.reshape(1, -1), w2, b2.reshape(1, -1), hw, hb.reshape(1, -1), bins
    )
    shape = (TAPS, TAPS, CHANS, CHANS)
    outs = pl.pallas_call(
        functools.partial(finish_kernel, near),
        out_shape=[
            jax.ShapeDtypeStruct((CHANS, rows, cols), BF16),
            jax.ShapeDtypeStruct(shape, F32),
            jax.ShapeDtypeStruct((1, CHANS), F32),
            jax.ShapeDtypeStruct(shape, F32),
            jax.ShapeDtypeStruct((1, CHANS), F32),
            jax.ShapeDtypeStruct((CHANS, nbins), F32),
            jax.ShapeDtypeStruct((1, nbins), F32),
        ],
        in_specs=[vmem] * 4,
        out_specs=[vmem] * 7,
        compiler_params=pltpu.CompilerParams(**params),
    )(grad_pair, sums_a.reshape(-1, LANES), sums_b.reshape(-1, LANES), mask_v)
    gp, c1w, c1b, c2w, c2b, hgw, hgb = outs
    return gp, c1w, c1b.reshape(-1), c2w, c2b.reshape(-1), hgw, hgb.reshape(-1)


def solution(mesh):
    return jax.shard_map(
        on_device,
        mesh=mesh,
        in_specs=(P(None, "ri", "rj"), P(), P(), P(), P(), P(), P(), P("ri", "rj"), P()),
        out_specs=(P(None, "ri", "rj"), P(), P(), P(), P(), P(), P()),
        check_vma=False,
    )
```

```python
import functools

import jax
import jax.numpy as jnp
from jax import lax
from jax.experimental import pallas as pl
from jax.experimental.pallas import tpu as pltpu
from jax.sharding import PartitionSpec as P

TAPS = 3
STEP = 8
CHANS = 64
LANES = 128
BINS = 40
MESH = pl.DeviceIdType.MESH
F32 = jnp.float32
BF16 = jnp.bfloat16
PAIR, ACT, OUTER, INNER = range(4)
SIDES = ((-1, 0), (1, 0), (0, -1), (0, 1), (-1, -1), (-1, 1), (1, -1), (1, 1))
GROUP = 4
CONV_ROWS = TAPS * TAPS * CHANS // 2


def dot_nt(a, b):
    return lax.dot_general(a, b, (((1,), (1,)), ((), ())), preferred_element_type=F32)


def dot_tn(a, b):
    return lax.dot_general(a, b, (((0,), (0,)), ((), ())), preferred_element_type=F32)


def dot_nn(a, b):
    return jnp.dot(a, b, preferred_element_type=F32)


def halves_mask(shape):
    return lax.broadcasted_iota(jnp.int32, shape, len(shape) - 1) < CHANS


def chunk_rows(used, chunks):
    return -(-used // (8 * chunks)) * 8


def scratch_list(rows, cols, nrow, ncol):
    pairs = rows // 2
    count = cols // rows
    near = GROUP * ncol
    far = nrow // GROUP
    rows_a = chunk_rows(CONV_ROWS + 8, near)
    rows_b = chunk_rows(CONV_ROWS + BINS + 8, near)
    dma = pltpu.SemaphoreType.DMA
    items = dict(
        p32=pltpu.VMEM((cols // LANES, CHANS * rows, LANES), F32),
        qa=pltpu.VMEM((4, pairs + STEP, cols, LANES), BF16),
        qb=pltpu.VMEM((4, pairs + STEP, cols + 2 * STEP, LANES), BF16),
        up=pltpu.VMEM((4, STEP, cols // 2, LANES), BF16),
        down=pltpu.VMEM((4, STEP, cols // 2, LANES), BF16),
        left=pltpu.VMEM((4, pairs, 2 * STEP, LANES), BF16),
        right=pltpu.VMEM((4, pairs, 2 * STEP, LANES), BF16),
        rows_in=pltpu.VMEM((4, 2, STEP, cols // 2, LANES), BF16),
        cols_in=pltpu.VMEM((4, 2, pairs, 2 * STEP, LANES), BF16),
        corner_in=pltpu.VMEM((4, 4, STEP, 2 * STEP, LANES), BF16),
        xr=pltpu.VMEM((pairs, cols, LANES), BF16),
        sl1=pltpu.VMEM((pairs, cols, LANES), F32),
        sl2=pltpu.VMEM((pairs, cols, LANES), F32),
        og=pltpu.VMEM((pairs, cols, LANES), F32),
        hid=pltpu.VMEM((pairs, cols, LANES), BF16),
        hidp=pltpu.VMEM((pairs, cols, LANES), BF16),
        grad=pltpu.VMEM((pairs, cols, LANES), BF16),
        mirror=pltpu.VMEM((count, pairs, rows, LANES), BF16),
        m32=pltpu.VMEM((count, pairs * rows, LANES), F32),
        binsend=pltpu.VMEM((cols, LANES), BF16),
        bins_in=pltpu.VMEM((count, rows, LANES), BF16),
        binsp=pltpu.VMEM((2, rows, cols), F32),
        ww=pltpu.VMEM((4, TAPS * 2 * LANES, LANES), BF16),
        wb=pltpu.VMEM((2 * BINS, LANES), BF16),
        wb2=pltpu.VMEM((4 * BINS, LANES), BF16),
        hwp=pltpu.VMEM((CHANS, LANES), F32),
        small=pltpu.VMEM((8, LANES), F32),
        hbias=pltpu.VMEM((BINS, cols), F32),
        colm=pltpu.VMEM((cols, LANES), F32),
        colp=pltpu.VMEM((BINS, cols), F32),
        acc_t=pltpu.VMEM((2, LANES, TAPS * 2 * LANES), F32),
        acc_b=pltpu.VMEM((2, 8, LANES), F32),
        acc_h=pltpu.VMEM((4 * BINS, LANES), F32),
        acc_e=pltpu.VMEM((BINS, cols), F32),
        own_a=pltpu.VMEM((near * rows_a, LANES), F32),
        own_b=pltpu.VMEM((near * rows_b, LANES), F32),
        slots_a=pltpu.VMEM((near, rows_a, LANES), F32),
        slots_b=pltpu.VMEM((near, rows_b, LANES), F32),
        mid_a=pltpu.VMEM((far, rows_a, LANES), F32),
        mid_b=pltpu.VMEM((far, rows_b, LANES), F32),
        all_a=pltpu.VMEM((near, rows_a, LANES), F32),
        all_b=pltpu.VMEM((near, rows_b, LANES), F32),
        halo_send=dma((4, 8)),
        halo_recv=dma((4, 8)),
        mir_send=dma((count, 4)),
        mir_recv=dma((count, 4)),
        mir_own=dma((4,)),
        relay=pltpu.VMEM((count, 2, STEP, 2 * STEP, LANES), BF16),
        relay_recv=dma((count, 2)),
        relay_send=dma((count, 2)),
        bin_send=dma((count,)),
        bin_recv=dma((count,)),
        near_send=dma((2, 2, near)),
        near_recv=dma((2, 2, near)),
        far_send=dma((2, far)),
        far_recv=dma((2, far)),
    )
    return items


def mega_kernel(
    names, nrow, ncol,
    pair, mask_s, mask_v, w1, b1, w2, b2, hw, hb, bins, out_pair, out_a, out_b, *scratch
):
    sc = dict(zip(names, scratch))
    rows, cols = bins.shape
    pairs = rows // 2
    groups = pairs // STEP
    count = cols // rows
    half = cols // 2
    near = GROUP * ncol
    far = nrow // GROUP
    row = lax.axis_index("ri")
    column = lax.axis_index("rj")
    slot = lax.rem(row, count)
    far_column = lax.div(row, count)
    own_group = far_column == column
    relays = ncol == 2
    spot = lax.rem(row, GROUP) + GROUP * column
    tier = lax.div(row, GROUP)
    barrier = pltpu.get_barrier_semaphore()

    qa, qb = sc["qa"], sc["qb"]

    def near_device(place):
        return (tier * GROUP + lax.rem(place, GROUP), lax.div(place, GROUP))

    def far_device(level):
        return (level * GROUP + lax.rem(row, GROUP), column)

    def side_exists(side):
        dr, dc = side
        there = None
        for step, here, size in ((dr, row, nrow), (dc, column, ncol)):
            if step:
                one = here > 0 if step < 0 else here < size - 1
                there = one if there is None else jnp.logical_and(there, one)
        return there

    def side_device(side):
        return (row + side[0], column + side[1])

    def meets_self(block):
        return jnp.logical_and(own_group, slot == block)

    def partner(block):
        return (count * column + block, far_column)

    for ref in (sc["rows_in"], sc["cols_in"], sc["corner_in"]):
        lead = ref.shape[:3]

        @pl.loop(0, lead[0] * lead[1])
        def _(at):
            ref[at // lead[1], at % lead[1]] = jnp.zeros(ref.shape[2:], ref.dtype)

    def signal(device):
        pl.semaphore_signal(barrier, inc=1, device_id=device, device_id_type=MESH)

    for side in SIDES:

        @pl.when(side_exists(side))
        def _():
            signal(side_device(side))

    for block in range(count):

        @pl.when(jnp.logical_not(meets_self(block)))
        def _():
            signal(partner(block))

    if relays:

        @pl.when(jnp.logical_not(own_group))
        def _():
            for block in range(count):
                signal((count * column + block, column))

    @pl.loop(1, near)
    def _(step):
        signal(near_device(lax.rem(spot + step, near)))

    @pl.loop(1, far)
    def _(step):
        signal(far_device(lax.rem(tier + step, far)))

    @pl.loop(0, CHANS, unroll=4)
    def _(chan):
        for tile in range(cols // LANES):
            sc["p32"][tile, pl.ds(chan * rows, rows), :] = pair[
                chan, :, tile * LANES : (tile + 1) * LANES
            ].astype(F32)

    zero8 = jnp.zeros((STEP, LANES), F32)
    low = halves_mask((half, LANES))

    def publish(field, at, value):
        turned = pltpu.roll(value, CHANS, 1)
        plain = turned.astype(BF16)
        wide = jnp.concatenate([zero8, turned, zero8], axis=0).astype(BF16)
        qa[field, at, :, CHANS:] = plain[:, CHANS:]
        qa[field, at + STEP, :, :CHANS] = plain[:, :CHANS]
        qb[field, at, :, CHANS:] = wide[:, CHANS:]
        qb[field, at + STEP, :, :CHANS] = wide[:, :CHANS]
        sc["left"][field, at] = value[: 2 * STEP].astype(BF16)
        sc["right"][field, at] = value[cols - 2 * STEP :].astype(BF16)
        return turned

    def pack_up(field, at, value, turned):
        sc["up"][field, at] = jnp.where(low, value[:half], turned[half:]).astype(BF16)

    def pack_down(field, at, value, turned):
        sc["down"][field, at] = jnp.where(low, turned[:half], value[half:]).astype(BF16)

    last = slice((groups - 1) * STEP, groups * STEP)
    first = slice(0, STEP)

    def halo_source(field, side):
        dr, dc = side
        if dc == 0:
            return sc["up" if dr < 0 else "down"].at[field]
        edge = sc["left" if dc < 0 else "right"].at[field]
        if dr == 0:
            return edge
        return edge.at[first if dr < 0 else last]

    def halo_target(field, side):
        dr, dc = side
        if dc == 0:
            return sc["rows_in"].at[field, 0 if dr < 0 else 1]
        if dr == 0:
            return sc["cols_in"].at[field, 0 if dc < 0 else 1]
        return sc["corner_in"].at[field, (0 if dr < 0 else 2) + (0 if dc < 0 else 1)]

    def halo_copy(field, index):
        side = SIDES[index]
        back = (-side[0], -side[1])
        return pltpu.make_async_remote_copy(
            src_ref=halo_source(field, side),
            dst_ref=halo_target(field, back),
            send_sem=sc["halo_send"].at[field, index],
            recv_sem=sc["halo_recv"].at[field, SIDES.index(back)],
            device_id=side_device(side),
            device_id_type=MESH,
        )

    def halo_arrival(field, index):
        side = SIDES[index]
        return pltpu.make_async_remote_copy(
            src_ref=halo_source(field, side),
            dst_ref=halo_target(field, side),
            send_sem=sc["halo_send"].at[field, index],
            recv_sem=sc["halo_recv"].at[field, index],
            device_id=side_device(side),
            device_id_type=MESH,
        )

    def send_halo(field, wanted):
        for index, side in enumerate(SIDES):
            if side[0] in wanted:

                @pl.when(side_exists(side))
                def _():
                    halo_copy(field, index).start()

    def wait_halo(field):
        for index, side in enumerate(SIDES):

            @pl.when(side_exists(side))
            def _():
                halo_arrival(field, index).wait()

    def place_halo(field):
        @pl.loop(0, STEP)
        def _(at):
            above = sc["rows_in"][field, 0, at].astype(F32)
            wide = jnp.concatenate([above, pltpu.roll(above, CHANS, 1)], axis=0)
            qa[field, at, :, :CHANS] = wide.astype(BF16)[:, :CHANS]
            west = pltpu.roll(sc["corner_in"][field, 0, at].astype(F32), CHANS, 1)[STEP:]
            east = pltpu.roll(sc["corner_in"][field, 1, at].astype(F32), CHANS, 1)[:STEP]
            wide = jnp.concatenate([west, wide, east], axis=0).astype(BF16)
            qb[field, at, :, :CHANS] = wide[:, :CHANS]
            below = sc["rows_in"][field, 1, at].astype(F32)
            wide = jnp.concatenate([pltpu.roll(below, CHANS, 1), below], axis=0)
            qa[field, pairs + at, :, CHANS:] = wide.astype(BF16)[:, CHANS:]
            west = pltpu.roll(sc["corner_in"][field, 2, at].astype(F32), CHANS, 1)[STEP:]
            east = pltpu.roll(sc["corner_in"][field, 3, at].astype(F32), CHANS, 1)[:STEP]
            wide = jnp.concatenate([west, wide, east], axis=0).astype(BF16)
            qb[field, pairs + at, :, CHANS:] = wide[:, CHANS:]

        @pl.loop(0, pairs, unroll=2)
        def _(at):
            for edge, side in ((0, "left"), (1, "right")):
                own = sc[side][field, at].astype(F32)
                come = sc["cols_in"][field, edge, at].astype(F32)
                if edge == 0:
                    both = jnp.concatenate([come[STEP:], own[:STEP]], axis=0)
                    spots = slice(0, 2 * STEP)
                else:
                    both = jnp.concatenate([own[STEP:], come[:STEP]], axis=0)
                    spots = slice(cols, cols + 2 * STEP)
                both = pltpu.roll(both, CHANS, 1).astype(BF16)
                qb[field, at, spots, CHANS:] = both[:, CHANS:]
                qb[field, at + STEP, spots, :CHANS] = both[:, :CHANS]

    def taps(field, at):
        return jnp.concatenate(
            [
                qb[field, at, :cols, :],
                qb[field, at + STEP, :cols, :],
                qa[field, at],
                qa[field, at + STEP],
                qb[field, at, 2 * STEP :, :],
                qb[field, at + STEP, 2 * STEP :, :],
            ],
            axis=1,
        )

    def conv(field, which, at):
        return dot_nn(taps(field, at), sc["ww"][which])

    def add_taps(field, which):
        sc["acc_t"][which] = jnp.zeros(sc["acc_t"].shape[1:], F32)

        @pl.loop(0, pairs, unroll=2)
        def _(at):
            sc["acc_t"][which] += dot_tn(sc["grad"][at], taps(field, at))

    def row_of(group, at):
        return 2 * STEP * group + at

    def column_sums(value):
        total = value[:STEP]
        for start in range(STEP, cols, STEP):
            total = total + value[start : start + STEP]
        return total

    with jax.named_scope("publish_pair"):
        for group in range(groups):

            @pl.loop(0, STEP, unroll=2)
            def _(at):
                line = row_of(group, at)
                value = []
                for tile in range(cols // LANES):
                    one = sc["p32"][tile, pl.ds(line, CHANS, stride=rows), :]
                    two = sc["p32"][tile, pl.ds(line + STEP, CHANS, stride=rows), :]
                    value.append(jnp.transpose(jnp.concatenate([one, two], axis=0)))
                value = jnp.concatenate(value, axis=0)
                place = group * STEP + at
                sc["xr"][place] = value.astype(BF16)
                turned = publish(PAIR, place, value)
                if group == 0:
                    pack_up(PAIR, at, value, turned)
                if group == groups - 1:
                    pack_down(PAIR, at, value, turned)

    text = bins[...].astype(F32)
    text = jnp.concatenate([text, jnp.zeros((LANES - rows, cols), F32)], axis=0)
    sc["binsend"][...] = jnp.transpose(text).astype(BF16)

    def bins_source(block):
        return sc["binsend"].at[pl.ds(block * rows, rows)]

    def bins_copy(block, at):
        return pltpu.make_async_remote_copy(
            src_ref=bins_source(block),
            dst_ref=sc["bins_in"].at[at],
            send_sem=sc["bin_send"].at[block],
            recv_sem=sc["bin_recv"].at[at],
            device_id=partner(block),
            device_id_type=MESH,
        )

    wait_count = 0
    for side in SIDES:
        wait_count = wait_count + side_exists(side).astype(jnp.int32)
    wait_count = wait_count + count - own_group.astype(jnp.int32)
    if relays:
        wait_count = wait_count + count * own_group.astype(jnp.int32)
    pl.semaphore_wait(barrier, wait_count + (near - 1) + (far - 1))

    send_halo(PAIR, (-1, 0, 1))
    for block in range(count):

        @pl.when(jnp.logical_not(meets_self(block)))
        def _():
            bins_copy(block, slot).start()

        @pl.when(meets_self(block))
        def _():
            sc["bins_in"][block] = sc["binsend"][pl.ds(block * rows, rows), :]

    with jax.named_scope("weights"):
        sc["ww"][...] = jnp.zeros(sc["ww"].shape, BF16)
        for which, (weight, flip) in enumerate(((w1, False), (w2, False), (w2, True), (w1, True))):
            for across in range(TAPS):
                for down in range(TAPS):
                    if flip:
                        piece = weight[TAPS - 1 - down, TAPS - 1 - across].astype(F32)
                        piece = jnp.transpose(piece).astype(BF16)
                    else:
                        piece = weight[down, across]
                    for part in range(2):
                        start = across * 2 * LANES + (down + part) * CHANS
                        sc["ww"][
                            which, start : start + CHANS, part * CHANS : (part + 1) * CHANS
                        ] = piece
        nbins = hw.shape[1]
        sc["hwp"][...] = jnp.zeros(sc["hwp"].shape, F32)
        sc["hwp"][:, :nbins] = hw[...].astype(F32)
        flat = jnp.transpose(sc["hwp"][...])[:BINS]
        none = jnp.zeros_like(flat)
        both = jnp.concatenate(
            [jnp.concatenate([flat, none], axis=1), jnp.concatenate([none, flat], axis=1)], axis=0
        )
        sc["wb"][...] = (0.5 * both).astype(BF16)
        sc["wb2"][...] = jnp.concatenate([both, both], axis=0).astype(BF16)
        sc["small"][...] = jnp.full((8, LANES), -1e30, F32)
        sc["small"][0:1, :nbins] = hb[...]
        spread = jnp.broadcast_to(sc["small"][0:1, :], (LANES, LANES))
        spread = jnp.transpose(spread)[:BINS]
        for start in range(0, cols, LANES):
            sc["hbias"][:, start : start + LANES] = spread
        sc["small"][0:1, :CHANS] = b1[...]
        sc["small"][0:1, CHANS:] = b1[...]
        sc["small"][1:2, :CHANS] = b2[...]
        sc["small"][1:2, CHANS:] = b2[...]
        natural = lax.broadcasted_iota(jnp.int32, (cols, cols), 0)
        placed = lax.broadcasted_iota(jnp.int32, (cols, cols), 1)
        goal = ((natural >> 3) & 1) * half + (natural >> 4) * STEP + (natural & 7)
        move = jnp.where(placed == goal, 1.0, 0.0).astype(BF16)
        ones_row = mask_v[pl.ds(column, 1), :].astype(F32)
        top = lax.broadcasted_iota(jnp.int32, (2 * STEP, cols), 0) == 0
        ones_row = jnp.where(top, jnp.broadcast_to(ones_row, (2 * STEP, cols)), 0.0).astype(BF16)
        sc["colm"][...] = dot_tn(ones_row, jnp.ones((2 * STEP, LANES), BF16))
        sc["colp"][...] = jnp.broadcast_to(dot_nn(ones_row, move)[0:1], (BINS, cols))
        sc["binsp"][0] = dot_nn(bins[...].astype(F32).astype(BF16), move)
        for ref in (sc["acc_b"], sc["acc_h"], sc["acc_e"]):
            ref[...] = jnp.zeros(ref.shape, F32)
        for ref in (sc["own_a"], sc["own_b"]):
            ref[CONV_ROWS:, :] = jnp.zeros((ref.shape[0] - CONV_ROWS, LANES), F32)

    lane_low = halves_mask((1, LANES))

    def valid(line):
        return mask_s[row * rows + line].astype(F32)

    def pair_mask(group, at):
        line = row_of(group, at)
        return sc["colm"][...] * jnp.where(lane_low, valid(line), valid(line + STEP))

    with jax.named_scope("wait_pair"):
        wait_halo(PAIR)
        place_halo(PAIR)

    with jax.named_scope("conv1"):
        for group in range(groups):

            @pl.loop(0, STEP, unroll=2)
            def _(at):
                place = group * STEP + at
                inner = conv(PAIR, 0, place) + sc["small"][0:1, :]
                power = jnp.exp(jnp.minimum(inner, 0.0))
                value = jnp.where(inner > 0, inner, power - 1.0)
                sc["sl1"][place] = jnp.where(inner > 0, 1.0, power)
                turned = publish(ACT, place, value)
                if group == 0:
                    pack_up(ACT, at, value, turned)
                if group == groups - 1:
                    pack_down(ACT, at, value, turned)

            send_halo(ACT, (-1,) if group == 0 else (0, 1))

    with jax.named_scope("wait_act"):
        wait_halo(ACT)
        place_halo(ACT)

    def mirror_source(block, group, part):
        return sc["hid"].at[
            pl.ds(group * STEP, STEP), pl.ds(block * rows + part * 2 * STEP, 2 * STEP)
        ]

    def mirror_target(at, group, part):
        return sc["mirror"].at[at, pl.ds(group * STEP, STEP), pl.ds(part * 2 * STEP, 2 * STEP)]

    def mirror_copy(block, at, group, part):
        piece = 2 * group + part
        return pltpu.make_async_remote_copy(
            src_ref=mirror_source(block, group, part),
            dst_ref=mirror_target(at, group, part),
            send_sem=sc["mir_send"].at[block, piece],
            recv_sem=sc["mir_recv"].at[at, piece],
            device_id=partner(block),
            device_id_type=MESH,
        )

    def mirror_own(block, group, part):
        return pltpu.make_async_copy(
            mirror_source(block, group, part),
            mirror_target(block, group, part),
            sc["mir_own"].at[2 * group + part],
        )

    def relayed(group, part):
        return relays and (group + part) % 2 == 1

    def relay_copy(block, group, part):
        return pltpu.make_async_remote_copy(
            src_ref=mirror_source(block, group, part),
            dst_ref=sc["relay"].at[block, group],
            send_sem=sc["mir_send"].at[block, 2 * group + part],
            recv_sem=sc["relay_recv"].at[block, group],
            device_id=(row, 1 - column),
            device_id_type=MESH,
        )

    def relay_forward(block, group, part):
        return pltpu.make_async_remote_copy(
            src_ref=sc["relay"].at[block, group],
            dst_ref=mirror_target(slot, group, part),
            send_sem=sc["relay_send"].at[block, group],
            recv_sem=sc["mir_recv"].at[slot, 2 * group + part],
            device_id=(count * (1 - column) + block, column),
            device_id_type=MESH,
        )

    with jax.named_scope("conv2"):
        for group in range(groups):

            @pl.loop(0, STEP, unroll=2)
            def _(at):
                place = group * STEP + at
                outer = conv(ACT, 1, place) + sc["small"][1:2, :]
                total = sc["xr"][place].astype(F32) + outer
                power = jnp.exp(jnp.minimum(total, 0.0))
                keep = pair_mask(group, at)
                hidden = keep * jnp.where(total > 0, total, power - 1.0)
                sc["sl2"][place] = keep * jnp.where(total > 0, 1.0, power)
                sc["hid"][place] = hidden.astype(BF16)
                order = [hidden[16 * t : 16 * t + 8] for t in range(cols // 16)]
                order += [hidden[16 * t + 8 : 16 * t + 16] for t in range(cols // 16)]
                sc["hidp"][place] = jnp.concatenate(order, axis=0).astype(BF16)

            for part in range(2):
                for block in range(count):

                    @pl.when(
                        own_group & (slot != block)
                        if relayed(group, part)
                        else jnp.logical_not(meets_self(block))
                    )
                    def _():
                        mirror_copy(block, slot, group, part).start()

                    if relayed(group, part):

                        @pl.when(jnp.logical_not(own_group))
                        def _():
                            relay_copy(block, group, part).start()

                    @pl.when(meets_self(block))
                    def _():
                        mirror_own(block, group, part).start()

    if relays:

        @pl.when(own_group)
        def _():
            for group in range(groups):
                part = 1 - group % 2
                for block in range(count):
                    relay_copy(block, group, part).wait_recv()
                    relay_forward(block, group, part).start()

    with jax.named_scope("bins"):
        total = jnp.zeros((rows, cols), F32)
        for block in range(count):

            @pl.when(jnp.logical_not(meets_self(block)))
            def _():
                bins_copy(block, block).wait()

            part = move[block * rows : (block + 1) * rows]
            total = total + dot_nn(sc["bins_in"][block][:, :rows], part)
        sc["binsp"][1] = total

    bin_ids = lax.broadcasted_iota(jnp.int32, (BINS, cols), 0).astype(F32)

    def mirrored(line):
        parts = [sc["m32"][block, pl.ds(line, pairs, stride=rows), :] for block in range(count)]
        return jnp.concatenate(parts, axis=0).astype(BF16)

    for group in range(groups):
        with jax.named_scope("wait_mirror"):
            for sender in range(groups):
                for block in range(count):

                    @pl.when(jnp.logical_not(meets_self(block)))
                    def _():
                        mirror_copy(block, block, sender, group).wait()

                    @pl.when(meets_self(block))
                    def _():
                        mirror_own(block, sender, group).wait()

            @pl.loop(0, pairs, unroll=2)
            def _(at):
                for block in range(count):
                    start = pl.multiple_of(at * rows + group * 2 * STEP, 2 * STEP)
                    sc["m32"][block, pl.ds(start, 2 * STEP), :] = sc["mirror"][
                        block, at, group * 2 * STEP : (group + 1) * 2 * STEP, :
                    ].astype(F32)

        with jax.named_scope("head"):

            @pl.loop(0, STEP, unroll=2)
            def _(at):
                place = group * STEP + at
                own = dot_nt(sc["wb"][...], sc["hidp"][place])
                errors = []
                for part in range(2):
                    line = row_of(group, at) + part * STEP
                    other = dot_nt(sc["wb"][...], mirrored(line))
                    other = jnp.concatenate([other[:BINS], other[BINS:]], axis=1)
                    logits = own[part * BINS : (part + 1) * BINS] + other + sc["hbias"][...]
                    peak = jnp.max(logits, axis=0, keepdims=True)
                    powered = jnp.exp(logits - peak)
                    scale = 1.0 / jnp.sum(powered, axis=0, keepdims=True)
                    hits = jnp.where(sc["binsp"][0, pl.ds(line, 1), :] == bin_ids, 0.5, 0.0)
                    hits += jnp.where(sc["binsp"][1, pl.ds(line, 1), :] == bin_ids, 0.5, 0.0)
                    errors.append(sc["colp"][...] * valid(line) * (powered * scale - hits))
                sc["acc_e"][...] += errors[0] + errors[1]
                error = jnp.concatenate(errors, axis=0)
                coarse = error.astype(BF16)
                fine = (error - coarse.astype(F32)).astype(BF16)
                stack = jnp.concatenate([coarse, fine], axis=0)
                sc["acc_h"][...] += dot_nn(stack, sc["hidp"][place])
                slope = dot_tn(stack, sc["wb2"][...])
                order = []
                for t in range(cols // 16):
                    order += [slope[8 * t : 8 * t + 8], slope[half + 8 * t : half + 8 * t + 8]]
                value = jnp.concatenate(order, axis=0) * sc["sl2"][place]
                sc["og"][place] = value
                sc["grad"][place] = value.astype(BF16)
                sc["acc_b"][1] += column_sums(value)
                turned = publish(OUTER, place, value)
                if group == 0:
                    pack_up(OUTER, at, value, turned)
                if group == groups - 1:
                    pack_down(OUTER, at, value, turned)

        send_halo(OUTER, (-1,) if group == 0 else (0, 1))

    def near_one(kind, tag, step):
        tall = sc["slots_" + tag].shape[1]
        peer = lax.rem(spot + step, near)
        return pltpu.make_async_remote_copy(
            src_ref=sc["own_" + tag].at[pl.ds(pl.multiple_of(peer * tall, 8), tall)],
            dst_ref=sc["slots_" + tag].at[step],
            send_sem=sc["near_send"].at[kind, 0, step],
            recv_sem=sc["near_recv"].at[kind, 0, step],
            device_id=near_device(peer),
            device_id_type=MESH,
        )

    def far_one(kind, tag, step):
        return pltpu.make_async_remote_copy(
            src_ref=sc["mid_" + tag].at[tier],
            dst_ref=sc["mid_" + tag].at[tier],
            send_sem=sc["far_send"].at[kind, step],
            recv_sem=sc["far_recv"].at[kind, step],
            device_id=far_device(lax.rem(tier + step, far)),
            device_id_type=MESH,
        )

    def near_two(kind, tag, step):
        return pltpu.make_async_remote_copy(
            src_ref=sc["all_" + tag].at[spot],
            dst_ref=sc["all_" + tag].at[spot],
            send_sem=sc["near_send"].at[kind, 1, step],
            recv_sem=sc["near_recv"].at[kind, 1, step],
            device_id=near_device(lax.rem(spot + step, near)),
            device_id_type=MESH,
        )

    def pack_taps(which, own):
        both = jnp.transpose(sc["acc_t"][which])
        for across in range(TAPS):
            for down in range(TAPS):
                at = across * 2 * LANES + down * CHANS
                one = both[at : at + CHANS]
                two = pltpu.roll(both[at + CHANS : at + 2 * CHANS], CHANS, 1)
                total = one + two
                packed = jnp.where(
                    halves_mask((CHANS // 2, LANES)),
                    total[: CHANS // 2],
                    pltpu.roll(total[CHANS // 2 :], CHANS, 1),
                )
                start = (down * TAPS + across) * (CHANS // 2)
                own[start : start + CHANS // 2, :] = packed

    def start_sum(kind, tag):
        for step in range(1, near):
            near_one(kind, tag, step).start()

    def middle_sum(kind, tag):
        for step in range(1, near):
            near_one(kind, tag, step).wait()
        tall = sc["slots_" + tag].shape[1]
        total = sc["own_" + tag][pl.ds(pl.multiple_of(spot * tall, 8), tall), :]
        for step in range(1, near):
            total = total + sc["slots_" + tag][step]
        sc["mid_" + tag][tier] = total
        for step in range(1, far):
            far_one(kind, tag, step).start()

    def late_sum(kind, tag):
        for step in range(1, far):
            far_one(kind, tag, step).wait()
        total = sc["mid_" + tag][0]
        for level in range(1, far):
            total = total + sc["mid_" + tag][level]
        sc["all_" + tag][spot] = total
        for step in range(1, near):
            near_two(kind, tag, step).start()

    def end_sum(kind, tag, out):
        for step in range(1, near):
            near_two(kind, tag, step).wait()
        out[...] = sc["all_" + tag][...]

    if relays:

        @pl.when(own_group)
        def _():
            for group in range(groups):
                for block in range(count):
                    relay_forward(block, group, 1 - group % 2).wait_send()

    with jax.named_scope("taps2"):
        add_taps(ACT, 1)
        pack_taps(1, sc["own_b"])
        both = sc["acc_h"][: 2 * BINS, :] + sc["acc_h"][2 * BINS :, :]
        both = both[:BINS] + pltpu.roll(both[BINS:], CHANS, 1)
        tally = jnp.sum(sc["acc_e"][...], axis=1, keepdims=True)
        sc["own_b"][CONV_ROWS : CONV_ROWS + BINS, :] = jnp.where(
            halves_mask((BINS, LANES)), both, jnp.broadcast_to(tally, (BINS, LANES))
        )
        sc["own_b"][CONV_ROWS + BINS : CONV_ROWS + BINS + 8, :] = sc["acc_b"][1]
        start_sum(1, "b")

    with jax.named_scope("wait_outer"):
        wait_halo(OUTER)
        place_halo(OUTER)

    with jax.named_scope("convt2"):
        for group in range(groups):

            @pl.loop(0, STEP, unroll=2)
            def _(at):
                place = group * STEP + at
                value = conv(OUTER, 2, place) * sc["sl1"][place]
                sc["grad"][place] = value.astype(BF16)
                sc["acc_b"][0] += column_sums(value)
                turned = publish(INNER, place, value)
                if group == 0:
                    pack_up(INNER, at, value, turned)
                if group == groups - 1:
                    pack_down(INNER, at, value, turned)

            send_halo(INNER, (-1,) if group == 0 else (0, 1))

    middle_sum(1, "b")

    with jax.named_scope("taps1"):
        add_taps(PAIR, 0)
        pack_taps(0, sc["own_a"])
        sc["own_a"][CONV_ROWS : CONV_ROWS + 8, :] = sc["acc_b"][0]
        start_sum(0, "a")
    late_sum(1, "b")

    with jax.named_scope("wait_inner"):
        wait_halo(INNER)
        place_halo(INNER)

    middle_sum(0, "a")
    with jax.named_scope("convt1"):
        for group in range(groups):

            @pl.loop(0, STEP, unroll=2)
            def _(at):
                place = group * STEP + at
                line = row_of(group, at)
                value = sc["og"][place] + conv(INNER, 3, place)
                for tile in range(cols // LANES):
                    turned = jnp.transpose(value[tile * LANES : (tile + 1) * LANES])
                    sc["p32"][tile, pl.ds(line, CHANS, stride=rows), :] = turned[:CHANS]
                    sc["p32"][tile, pl.ds(line + STEP, CHANS, stride=rows), :] = turned[CHANS:]

            if group == 0:
                late_sum(0, "a")

        @pl.loop(0, CHANS, unroll=4)
        def _(chan):
            for tile in range(cols // LANES):
                out_pair[chan, :, tile * LANES : (tile + 1) * LANES] = sc["p32"][
                    tile, pl.ds(chan * rows, rows), :
                ].astype(BF16)

    with jax.named_scope("end_sums"):
        end_sum(1, "b", out_b)
        end_sum(0, "a", out_a)


def finish_kernel(near, pair, sums_a, sums_b, mask_v, out_pair, c1w, c1b, c2w, c2b, hgw, hgb):
    out_pair[...] = pair[...]
    scale = 1.0 / jnp.sum(mask_v[...].astype(F32))
    for sums, weight, bias, extra in ((sums_a, c1w, c1b, 0), (sums_b, c2w, c2b, BINS)):
        for tap in range(TAPS * TAPS):
            start = tap * (CHANS // 2)
            value = sums[start : start + CHANS // 2, :] * scale
            weight[tap // TAPS, tap % TAPS, : CHANS // 2, :] = value[:, :CHANS]
            weight[tap // TAPS, tap % TAPS, CHANS // 2 :, :] = value[:, CHANS:]
        start = CONV_ROWS + extra
        total = jnp.sum(sums[start : start + 8, :], axis=0, keepdims=True) * scale
        bias[...] = total[:, :CHANS] + total[:, CHANS:]
    head = sums_b[CONV_ROWS : CONV_ROWS + BINS, :] * scale
    head = jnp.concatenate([head, jnp.zeros((LANES - BINS, LANES), F32)], axis=0)
    head = jnp.transpose(head)
    nbins = hgw.shape[1]
    hgw[...] = head[:CHANS, :nbins]
    hgb[...] = head[CHANS : CHANS + 1, :nbins]


def on_device(pair, w1, b1, w2, b2, hw, hb, bins, mask):
    nrow = lax.axis_size("ri")
    ncol = lax.axis_size("rj")
    rows, cols = bins.shape
    nbins = hw.shape[1]
    near = GROUP * ncol
    rows_a = chunk_rows(CONV_ROWS + 8, near)
    rows_b = chunk_rows(CONV_ROWS + BINS + 8, near)
    items = scratch_list(rows, cols, nrow, ncol)
    vmem = pl.BlockSpec(memory_space=pltpu.VMEM)
    smem = pl.BlockSpec(memory_space=pltpu.SMEM)
    mask_v = mask.reshape(ncol, cols)
    params = dict(vmem_limit_bytes=56 * 1024 * 1024)
    grad_pair, sums_a, sums_b = pl.pallas_call(
        functools.partial(mega_kernel, tuple(items), nrow, ncol),
        out_shape=[
            jax.ShapeDtypeStruct((CHANS, rows, cols), BF16),
            jax.ShapeDtypeStruct((near, rows_a, LANES), F32),
            jax.ShapeDtypeStruct((near, rows_b, LANES), F32),
        ],
        in_specs=[vmem, smem] + [vmem] * 8,
        out_specs=[vmem] * 3,
        scratch_shapes=list(items.values()),
        compiler_params=pltpu.CompilerParams(collective_id=0, has_side_effects=True, **params),
    )(
        pair, mask, mask_v, w1, b1.reshape(1, -1), w2, b2.reshape(1, -1), hw, hb.reshape(1, -1), bins
    )
    shape = (TAPS, TAPS, CHANS, CHANS)
    outs = pl.pallas_call(
        functools.partial(finish_kernel, near),
        out_shape=[
            jax.ShapeDtypeStruct((CHANS, rows, cols), BF16),
            jax.ShapeDtypeStruct(shape, F32),
            jax.ShapeDtypeStruct((1, CHANS), F32),
            jax.ShapeDtypeStruct(shape, F32),
            jax.ShapeDtypeStruct((1, CHANS), F32),
            jax.ShapeDtypeStruct((CHANS, nbins), F32),
            jax.ShapeDtypeStruct((1, nbins), F32),
        ],
        in_specs=[vmem] * 4,
        out_specs=[vmem] * 7,
        compiler_params=pltpu.CompilerParams(**params),
    )(grad_pair, sums_a.reshape(-1, LANES), sums_b.reshape(-1, LANES), mask_v)
    gp, c1w, c1b, c2w, c2b, hgw, hgb = outs
    return gp, c1w, c1b.reshape(-1), c2w, c2b.reshape(-1), hgw, hgb.reshape(-1)


def solution(mesh):
    return jax.shard_map(
        on_device,
        mesh=mesh,
        in_specs=(P(None, "ri", "rj"), P(), P(), P(), P(), P(), P(), P("ri", "rj"), P()),
        out_specs=(P(None, "ri", "rj"), P(), P(), P(), P(), P(), P()),
        check_vma=False,
    )
```

```python
import functools

import jax
import jax.numpy as jnp
from jax import lax
from jax.experimental import pallas as pl
from jax.experimental.pallas import tpu as pltpu
from jax.sharding import PartitionSpec as P

TAPS = 3
STEP = 8
CHANS = 64
LANES = 128
BINS = 40
MESH = pl.DeviceIdType.MESH
F32 = jnp.float32
BF16 = jnp.bfloat16
PAIR, ACT, OUTER, INNER = range(4)
SIDES = ((-1, 0), (1, 0), (0, -1), (0, 1), (-1, -1), (-1, 1), (1, -1), (1, 1))
MESSAGES = ((-1, 0, 0), (1, 0, 0), (-1, -1, 0), (-1, 1, 0), (1, -1, 0), (1, 1, 0)) + tuple(
    (0, step, kind) for kind in (0, 1) for step in (-1, 1)
)
EDGE, MIDDLE = 0, 1
OWN_BLOCKS = ((1, 4), (2, 3))
HALO_BLOCKS = (0, 5)
PLACES = (0, 3, 1, 2)
GROUP = 4
CONV_ROWS = TAPS * TAPS * CHANS // 2


def dot_nt(a, b):
    return lax.dot_general(a, b, (((1,), (1,)), ((), ())), preferred_element_type=F32)


def dot_tn(a, b):
    return lax.dot_general(a, b, (((0,), (0,)), ((), ())), preferred_element_type=F32)


def dot_nn(a, b):
    return jnp.dot(a, b, preferred_element_type=F32)


def halves_mask(shape):
    return lax.broadcasted_iota(jnp.int32, shape, len(shape) - 1) < CHANS


def chunk_rows(used, chunks):
    return -(-used // (8 * chunks)) * 8


def block_places(down, across):
    found = []
    for name, outs in (("edge", OWN_BLOCKS[EDGE]), ("middle", OWN_BLOCKS[MIDDLE])):
        for part, block in enumerate(outs):
            source = block + down - 1
            flat = OWN_BLOCKS[EDGE] + OWN_BLOCKS[MIDDLE]
            if source in flat:
                start = across * 2 * LANES + flat.index(source) * CHANS
            else:
                start = TAPS * 2 * LANES + across * LANES + HALO_BLOCKS.index(source) * CHANS
            found.append((name, start, part))
    return found


def scratch_list(rows, cols, nrow, ncol):
    pairs = rows // 2
    count = cols // rows
    near = GROUP * ncol
    far = nrow // GROUP
    rows_a = chunk_rows(CONV_ROWS + 8, near)
    rows_b = chunk_rows(CONV_ROWS + BINS + 8, near)
    dma = pltpu.SemaphoreType.DMA
    items = dict(
        p32=pltpu.VMEM((cols // LANES, CHANS * rows, LANES), F32),
        qa=pltpu.VMEM((4, pairs + STEP, cols, LANES), BF16),
        qb=pltpu.VMEM((4, pairs + STEP, cols + 2 * STEP, LANES), BF16),
        up=pltpu.VMEM((4, STEP, cols // 2, LANES), BF16),
        down=pltpu.VMEM((4, STEP, cols // 2, LANES), BF16),
        left=pltpu.VMEM((4, pairs, 2 * STEP, LANES), BF16),
        right=pltpu.VMEM((4, pairs, 2 * STEP, LANES), BF16),
        rows_in=pltpu.VMEM((4, 2, STEP, cols // 2, LANES), BF16),
        cols_in=pltpu.VMEM((4, 2, pairs, 2 * STEP, LANES), BF16),
        corner_in=pltpu.VMEM((4, 4, STEP, 2 * STEP, LANES), BF16),
        sl1=pltpu.VMEM((pairs, cols, LANES), F32),
        sl2=pltpu.VMEM((pairs, cols, LANES), F32),
        og=pltpu.VMEM((pairs, cols, LANES), F32),
        hid=pltpu.VMEM((pairs, cols, LANES), BF16),
        hidp=pltpu.VMEM((pairs, cols, LANES), BF16),
        grad=pltpu.VMEM((pairs, cols, LANES), BF16),
        mirror=pltpu.VMEM((count, pairs, rows, LANES), BF16),
        m32=pltpu.VMEM((count, pairs * rows, LANES), F32),
        binsend=pltpu.VMEM((cols, LANES), BF16),
        bins_in=pltpu.VMEM((count, rows, LANES), BF16),
        binsp=pltpu.VMEM((2, rows, cols), F32),
        w_edge=pltpu.VMEM((4, TAPS * 3 * LANES, LANES), BF16),
        w_middle=pltpu.VMEM((4, TAPS * 2 * LANES, LANES), BF16),
        wb=pltpu.VMEM((2 * BINS, LANES), BF16),
        wb2=pltpu.VMEM((4 * BINS, LANES), BF16),
        hwp=pltpu.VMEM((BINS, CHANS), F32),
        small=pltpu.VMEM((8, LANES), F32),
        hbias=pltpu.VMEM((BINS, cols), F32),
        colm=pltpu.VMEM((cols, LANES), F32),
        colp=pltpu.VMEM((BINS, cols), F32),
        t_edge=pltpu.VMEM((LANES, TAPS * 3 * LANES), F32),
        t_middle=pltpu.VMEM((LANES, TAPS * 2 * LANES), F32),
        acc_b=pltpu.VMEM((2, 8, LANES), F32),
        acc_h=pltpu.VMEM((4 * BINS, LANES), F32),
        acc_e=pltpu.VMEM((BINS, cols), F32),
        own_a=pltpu.VMEM((near * rows_a, LANES), F32),
        own_b=pltpu.VMEM((near * rows_b, LANES), F32),
        slots_a=pltpu.VMEM((near, rows_a, LANES), F32),
        slots_b=pltpu.VMEM((near, rows_b, LANES), F32),
        mid_a=pltpu.VMEM((far, rows_a, LANES), F32),
        mid_b=pltpu.VMEM((far, rows_b, LANES), F32),
        all_a=pltpu.VMEM((near, rows_a, LANES), F32),
        all_b=pltpu.VMEM((near, rows_b, LANES), F32),
        halo_send=dma((4, len(MESSAGES))),
        halo_recv=dma((4, len(MESSAGES))),
        mir_send=dma((count, 4)),
        mir_recv=dma((count, 4)),
        mir_own=dma((4,)),
        relay=pltpu.VMEM((count, 2, STEP, 2 * STEP, LANES), BF16),
        relay_recv=dma((count, 2)),
        relay_send=dma((count, 2)),
        bin_send=dma((count,)),
        bin_recv=dma((count,)),
        near_send=dma((2, 2, near)),
        near_recv=dma((2, 2, near)),
        far_send=dma((2, far)),
        far_recv=dma((2, far)),
    )
    return items


def mega_kernel(
    names, nrow, ncol,
    pair, mask_s, mask_v, w1, b1, w2, b2, hw, hb, bins, out_pair, out_a, out_b, *scratch
):
    sc = dict(zip(names, scratch))
    rows, cols = bins.shape
    pairs = rows // 2
    groups = pairs // STEP
    count = cols // rows
    half = cols // 2
    near = GROUP * ncol
    far = nrow // GROUP
    row = lax.axis_index("ri")
    column = lax.axis_index("rj")
    slot = lax.rem(row, count)
    far_column = lax.div(row, count)
    own_group = far_column == column
    relays = ncol == 2
    spot = lax.rem(row, GROUP) + GROUP * column
    tier = lax.div(row, GROUP)
    barrier = pltpu.get_barrier_semaphore()

    qa, qb = sc["qa"], sc["qb"]

    def near_device(place):
        return (tier * GROUP + lax.rem(place, GROUP), lax.div(place, GROUP))

    def far_device(level):
        return (level * GROUP + lax.rem(row, GROUP), column)

    def side_exists(side):
        dr, dc = side
        there = None
        for step, here, size in ((dr, row, nrow), (dc, column, ncol)):
            if step:
                one = here > 0 if step < 0 else here < size - 1
                there = one if there is None else jnp.logical_and(there, one)
        return there

    def side_device(side):
        return (row + side[0], column + side[1])

    def meets_self(block):
        return jnp.logical_and(own_group, slot == block)

    def partner(block):
        return (count * column + block, far_column)

    def signal(device):
        pl.semaphore_signal(barrier, inc=1, device_id=device, device_id_type=MESH)

    for side in SIDES:

        @pl.when(side_exists(side))
        def _():
            signal(side_device(side))

    for block in range(count):

        @pl.when(jnp.logical_not(meets_self(block)))
        def _():
            signal(partner(block))

    if relays:

        @pl.when(jnp.logical_not(own_group))
        def _():
            for block in range(count):
                signal((count * column + block, column))

    @pl.loop(1, near)
    def _(step):
        signal(near_device(lax.rem(spot + step, near)))

    @pl.loop(1, far)
    def _(step):
        signal(far_device(lax.rem(tier + step, far)))

    @pl.loop(0, CHANS, unroll=4)
    def _(chan):
        for tile in range(cols // LANES):
            sc["p32"][tile, pl.ds(chan * rows, rows), :] = pair[
                chan, :, tile * LANES : (tile + 1) * LANES
            ].astype(F32)

    lane_low = halves_mask((1, LANES))
    zero8 = jnp.zeros((STEP, LANES), F32)
    low = halves_mask((half, LANES))

    def publish(field, kind, at, value):
        place = kind * STEP + at
        qa[field, place] = value.astype(BF16)
        qb[field, place] = jnp.concatenate([zero8, value, zero8], axis=0).astype(BF16)
        sc["left"][field, place] = value[: 2 * STEP].astype(BF16)
        sc["right"][field, place] = value[cols - 2 * STEP :].astype(BF16)
        if kind == EDGE:
            turned = pltpu.roll(value, CHANS, 1)
            sc["up"][field, at] = jnp.where(low, value[:half], turned[half:]).astype(BF16)
            sc["down"][field, at] = jnp.where(low, turned[:half], value[half:]).astype(BF16)

    def halo_source(field, message):
        dr, dc, kind = message
        if dc == 0:
            return sc["up" if dr < 0 else "down"].at[field]
        return sc["left" if dc < 0 else "right"].at[field, pl.ds(kind * STEP, STEP)]

    def halo_target(field, message):
        dr, dc, kind = message
        if dc == 0:
            return sc["rows_in"].at[field, 0 if dr < 0 else 1]
        if dr == 0:
            return sc["cols_in"].at[field, 0 if dc < 0 else 1, pl.ds(kind * STEP, STEP)]
        return sc["corner_in"].at[field, (0 if dr < 0 else 2) + (0 if dc < 0 else 1)]

    def halo_copy(field, message):
        back = (-message[0], -message[1], message[2])
        return pltpu.make_async_remote_copy(
            src_ref=halo_source(field, message),
            dst_ref=halo_target(field, back),
            send_sem=sc["halo_send"].at[field, MESSAGES.index(message)],
            recv_sem=sc["halo_recv"].at[field, MESSAGES.index(back)],
            device_id=side_device(message[:2]),
            device_id_type=MESH,
        )

    def halo_arrival(field, message):
        index = MESSAGES.index(message)
        return pltpu.make_async_remote_copy(
            src_ref=halo_source(field, message),
            dst_ref=halo_target(field, message),
            send_sem=sc["halo_send"].at[field, index],
            recv_sem=sc["halo_recv"].at[field, index],
            device_id=side_device(message[:2]),
            device_id_type=MESH,
        )

    def send_halo(field, kind):
        for message in MESSAGES:
            if message[2] == kind:

                @pl.when(side_exists(message[:2]))
                def _():
                    halo_copy(field, message).start()

    def wait_halo(field, across):
        for message in MESSAGES:
            if (message[0] == 0) == across:

                @pl.when(side_exists(message[:2]))
                def _():
                    halo_arrival(field, message).wait()

    def place_rows(field):
        wait_halo(field, False)

        @pl.loop(0, STEP, unroll=2)
        def _(at):
            above = sc["rows_in"][field, 0, at].astype(F32)
            below = sc["rows_in"][field, 1, at].astype(F32)
            start = jnp.where(low, above, pltpu.roll(below, CHANS, 1))
            rest = jnp.where(low, pltpu.roll(above, CHANS, 1), below)
            wide = jnp.concatenate([start, rest], axis=0)
            qa[field, pairs + at] = wide.astype(BF16)
            edges = []
            for edge in (0, 1):
                upper = sc["corner_in"][field, edge, at].astype(F32)
                lower = sc["corner_in"][field, 2 + edge, at].astype(F32)
                both = pltpu.roll(jnp.where(lane_low, lower, upper), CHANS, 1)
                edges.append(both[STEP:] if edge == 0 else both[:STEP])
            wide = jnp.concatenate([edges[0], wide, edges[1]], axis=0)
            qb[field, pairs + at] = wide.astype(BF16)

    def place_cols(field):
        wait_halo(field, True)

        @pl.loop(0, pairs, unroll=4)
        def _(at):
            own = sc["left"][field, at].astype(F32)
            come = sc["cols_in"][field, 0, at].astype(F32)
            both = jnp.concatenate([come[STEP:], own[:STEP]], axis=0)
            qb[field, at, : 2 * STEP, :] = both.astype(BF16)
            own = sc["right"][field, at].astype(F32)
            come = sc["cols_in"][field, 1, at].astype(F32)
            both = jnp.concatenate([own[STEP:], come[:STEP]], axis=0)
            qb[field, at, cols:, :] = both.astype(BF16)

    def taps(field, kind, at):
        starts = (at, STEP + at)
        parts = [qb[field, start, :cols, :] for start in starts]
        parts += [qa[field, start] for start in starts]
        parts += [qb[field, start, 2 * STEP :, :] for start in starts]
        if kind == EDGE:
            start = pairs + at
            parts += [qb[field, start, :cols, :], qa[field, start], qb[field, start, 2 * STEP :, :]]
        return jnp.concatenate(parts, axis=1)

    def conv(field, which, kind, at):
        weight = sc["w_edge" if kind == EDGE else "w_middle"]
        return dot_nn(taps(field, kind, at), weight[which])

    def add_taps(field):
        for kind, name in ((MIDDLE, "t_middle"), (EDGE, "t_edge")):
            sc[name][...] = jnp.zeros(sc[name].shape, F32)

            @pl.loop(0, STEP, unroll=2)
            def _(at):
                sc[name][...] += dot_tn(sc["grad"][kind * STEP + at], taps(field, kind, at))

    def lines(kind, at):
        return (kind * STEP + at, rows - STEP * (kind + 1) + at)

    def column_sums(value):
        total = value[:STEP]
        for start in range(STEP, cols, STEP):
            total = total + value[start : start + STEP]
        return total

    def publish_pair(kind):
        @pl.loop(0, STEP, unroll=2)
        def _(at):
            one, two = lines(kind, at)
            value = []
            for tile in range(cols // LANES):
                upper = sc["p32"][tile, pl.ds(one, CHANS, stride=rows), :]
                lower = sc["p32"][tile, pl.ds(two, CHANS, stride=rows), :]
                value.append(jnp.transpose(jnp.concatenate([upper, lower], axis=0)))
            value = jnp.concatenate(value, axis=0)
            publish(PAIR, kind, at, value)

    for message in MESSAGES:

        @pl.when(jnp.logical_not(side_exists(message[:2])))
        def _():
            for field in range(4):
                ref = halo_target(field, message)
                ref[...] = jnp.zeros(ref.shape, ref.dtype)

    publish_pair(EDGE)
    wait_count = 0
    for side in SIDES:
        wait_count = wait_count + side_exists(side).astype(jnp.int32)
    wait_count = wait_count + count - own_group.astype(jnp.int32)
    if relays:
        wait_count = wait_count + count * own_group.astype(jnp.int32)
    pl.semaphore_wait(barrier, wait_count + (near - 1) + (far - 1))
    send_halo(PAIR, EDGE)
    publish_pair(MIDDLE)
    send_halo(PAIR, MIDDLE)

    text = bins[...].astype(F32)
    text = jnp.concatenate([text, jnp.zeros((LANES - rows, cols), F32)], axis=0)
    sc["binsend"][...] = jnp.transpose(text).astype(BF16)

    def bins_source(block):
        return sc["binsend"].at[pl.ds(block * rows, rows)]

    def bins_copy(block, at):
        return pltpu.make_async_remote_copy(
            src_ref=bins_source(block),
            dst_ref=sc["bins_in"].at[at],
            send_sem=sc["bin_send"].at[block],
            recv_sem=sc["bin_recv"].at[at],
            device_id=partner(block),
            device_id_type=MESH,
        )

    for block in range(count):

        @pl.when(jnp.logical_not(meets_self(block)))
        def _():
            bins_copy(block, slot).start()

        @pl.when(meets_self(block))
        def _():
            sc["bins_in"][block] = sc["binsend"][pl.ds(block * rows, rows), :]

    with jax.named_scope("weights"):
        for name in ("w_edge", "w_middle"):
            sc[name][...] = jnp.zeros(sc[name].shape, BF16)
        for which, (weight, flip) in enumerate(((w1, False), (w2, False), (w2, True), (w1, True))):
            for across in range(TAPS):
                for down in range(TAPS):
                    if flip:
                        piece = weight[TAPS - 1 - down, TAPS - 1 - across].astype(F32)
                        piece = jnp.transpose(piece).astype(BF16)
                    else:
                        piece = weight[down, across]
                    for name, start, part in block_places(down, across):
                        sc["w_" + name][
                            which, start : start + CHANS, part * CHANS : (part + 1) * CHANS
                        ] = piece
        nbins = hw.shape[0]
        sc["hwp"][...] = jnp.zeros(sc["hwp"].shape, F32)
        sc["hwp"][:nbins, :] = hw[...].astype(F32)
        flat = sc["hwp"][...]
        none = jnp.zeros_like(flat)
        both = jnp.concatenate(
            [jnp.concatenate([flat, none], axis=1), jnp.concatenate([none, flat], axis=1)], axis=0
        )
        sc["wb"][...] = (0.5 * both).astype(BF16)
        sc["wb2"][...] = jnp.concatenate([both, both], axis=0).astype(BF16)
        sc["small"][...] = jnp.full((8, LANES), -1e30, F32)
        sc["small"][0:1, :nbins] = hb[...]
        spread = jnp.broadcast_to(sc["small"][0:1, :], (LANES, LANES))
        spread = jnp.transpose(spread)[:BINS]
        for start in range(0, cols, LANES):
            sc["hbias"][:, start : start + LANES] = spread
        sc["small"][0:1, :CHANS] = b1[...]
        sc["small"][0:1, CHANS:] = b1[...]
        sc["small"][1:2, :CHANS] = b2[...]
        sc["small"][1:2, CHANS:] = b2[...]
        natural = lax.broadcasted_iota(jnp.int32, (cols, cols), 0)
        placed = lax.broadcasted_iota(jnp.int32, (cols, cols), 1)
        eighth = (natural >> 3) & 3
        upper = eighth >> 1
        goal = upper * half + (natural >> 5) * 2 * STEP + ((eighth ^ upper) & 1) * STEP
        goal = goal + (natural & 7)
        move = jnp.where(placed == goal, 1.0, 0.0).astype(BF16)
        tiles = cols // LANES
        ones_row = [mask_v[pl.ds(column * tiles + tile, 1), :] for tile in range(tiles)]
        ones_row = jnp.concatenate(ones_row, axis=1).astype(F32)
        top = lax.broadcasted_iota(jnp.int32, (2 * STEP, cols), 0) == 0
        ones_row = jnp.where(top, jnp.broadcast_to(ones_row, (2 * STEP, cols)), 0.0).astype(BF16)
        sc["colm"][...] = dot_tn(ones_row, jnp.ones((2 * STEP, LANES), BF16))
        sc["colp"][...] = jnp.broadcast_to(dot_nn(ones_row, move)[0:1], (BINS, cols))
        sc["binsp"][0] = dot_nn(bins[...].astype(F32).astype(BF16), move)
        for ref in (sc["acc_b"], sc["acc_h"], sc["acc_e"]):
            ref[...] = jnp.zeros(ref.shape, F32)
        for ref in (sc["own_a"], sc["own_b"]):
            ref[CONV_ROWS:, :] = jnp.zeros((ref.shape[0] - CONV_ROWS, LANES), F32)

    def valid(line):
        return mask_s[row * rows + line].astype(F32)

    def pair_mask(kind, at):
        one, two = lines(kind, at)
        return sc["colm"][...] * jnp.where(lane_low, valid(one), valid(two))

    def conv_step(field, kind, body):
        if kind == EDGE:
            place_rows(field)
        else:
            place_cols(field)

        @pl.loop(0, STEP, unroll=2)
        def _(at):
            body(at)

    with jax.named_scope("conv1"):
        for kind in (MIDDLE, EDGE):

            def body(at):
                place = kind * STEP + at
                inner = conv(PAIR, 0, kind, at) + sc["small"][0:1, :]
                power = jnp.exp(jnp.minimum(inner, 0.0))
                value = jnp.where(inner > 0, inner, power - 1.0)
                sc["sl1"][place] = jnp.where(inner > 0, 1.0, power)
                publish(ACT, kind, at, value)

            conv_step(PAIR, kind, body)
            send_halo(ACT, kind)

    def mirror_source(block, group, part):
        return sc["hid"].at[
            pl.ds(group * STEP, STEP), pl.ds(block * rows + part * 2 * STEP, 2 * STEP)
        ]

    def mirror_target(at, group, part):
        return sc["mirror"].at[at, pl.ds(group * STEP, STEP), pl.ds(part * 2 * STEP, 2 * STEP)]

    def mirror_copy(block, at, group, part):
        piece = 2 * group + part
        return pltpu.make_async_remote_copy(
            src_ref=mirror_source(block, group, part),
            dst_ref=mirror_target(at, group, part),
            send_sem=sc["mir_send"].at[block, piece],
            recv_sem=sc["mir_recv"].at[at, piece],
            device_id=partner(block),
            device_id_type=MESH,
        )

    def mirror_own(block, group, part):
        return pltpu.make_async_copy(
            mirror_source(block, group, part),
            mirror_target(block, group, part),
            sc["mir_own"].at[2 * group + part],
        )

    def relayed(group, part):
        return relays and (group + part) % 2 == 1

    def relay_copy(block, group, part):
        return pltpu.make_async_remote_copy(
            src_ref=mirror_source(block, group, part),
            dst_ref=sc["relay"].at[block, group],
            send_sem=sc["mir_send"].at[block, 2 * group + part],
            recv_sem=sc["relay_recv"].at[block, group],
            device_id=(row, 1 - column),
            device_id_type=MESH,
        )

    def relay_forward(block, group, part):
        return pltpu.make_async_remote_copy(
            src_ref=sc["relay"].at[block, group],
            dst_ref=mirror_target(slot, group, part),
            send_sem=sc["relay_send"].at[block, group],
            recv_sem=sc["mir_recv"].at[slot, 2 * group + part],
            device_id=(count * (1 - column) + block, column),
            device_id_type=MESH,
        )

    def row_groups(eighths):
        return [rows * block + STEP * at for block in range(count) for at in eighths]

    def gathered(value, starts):
        return jnp.concatenate([value[start : start + STEP] for start in starts], axis=0)

    with jax.named_scope("conv2"):
        for kind in (MIDDLE, EDGE):
            group = kind

            def body(at):
                place = kind * STEP + at
                outer = conv(ACT, 1, kind, at) + sc["small"][1:2, :]
                total = qa[PAIR, place].astype(F32) + outer
                power = jnp.exp(jnp.minimum(total, 0.0))
                keep = pair_mask(kind, at)
                hidden = keep * jnp.where(total > 0, total, power - 1.0)
                sc["sl2"][place] = keep * jnp.where(total > 0, 1.0, power)
                sc["hid"][place] = gathered(hidden, row_groups(PLACES)).astype(BF16)
                order = row_groups(PLACES[0:4:2]) + row_groups(PLACES[1:4:2])
                sc["hidp"][place] = gathered(hidden, order).astype(BF16)

            conv_step(ACT, kind, body)

            for part in range(2):
                for block in range(count):

                    @pl.when(
                        own_group & (slot != block)
                        if relayed(group, part)
                        else jnp.logical_not(meets_self(block))
                    )
                    def _():
                        mirror_copy(block, slot, group, part).start()

                    if relayed(group, part):

                        @pl.when(jnp.logical_not(own_group))
                        def _():
                            relay_copy(block, group, part).start()

                    @pl.when(meets_self(block))
                    def _():
                        mirror_own(block, group, part).start()

    if relays:

        @pl.when(own_group)
        def _():
            for group in (MIDDLE, EDGE):
                part = 1 - group % 2
                for block in range(count):
                    relay_copy(block, group, part).wait_recv()
                    relay_forward(block, group, part).start()

    with jax.named_scope("bins"):
        total = jnp.zeros((rows, cols), F32)
        for block in range(count):

            @pl.when(jnp.logical_not(meets_self(block)))
            def _():
                bins_copy(block, block).wait()

            part = move[block * rows : (block + 1) * rows]
            total = total + dot_nn(sc["bins_in"][block][:, :rows], part)
        sc["binsp"][1] = total

    bin_ids = lax.broadcasted_iota(jnp.int32, (BINS, cols), 0).astype(F32)

    def mirrored(line):
        parts = [sc["m32"][block, pl.ds(line, pairs, stride=rows), :] for block in range(count)]
        return jnp.concatenate(parts, axis=0).astype(BF16)

    for group in range(groups):
        with jax.named_scope("wait_mirror"):
            for sender in range(groups):
                for block in range(count):

                    @pl.when(jnp.logical_not(meets_self(block)))
                    def _():
                        mirror_copy(block, block, sender, group).wait()

                    @pl.when(meets_self(block))
                    def _():
                        mirror_own(block, sender, group).wait()

            @pl.loop(0, pairs, unroll=2)
            def _(at):
                for block in range(count):
                    start = pl.multiple_of(at * rows + group * 2 * STEP, 2 * STEP)
                    sc["m32"][block, pl.ds(start, 2 * STEP), :] = sc["mirror"][
                        block, at, group * 2 * STEP : (group + 1) * 2 * STEP, :
                    ].astype(F32)

        with jax.named_scope("head"):

            @pl.loop(0, STEP, unroll=2)
            def _(at):
                place = group * STEP + at
                own = dot_nt(sc["wb"][...], sc["hidp"][place])
                errors = []
                for part, line in enumerate(lines(group, at)):
                    other = dot_nt(sc["wb"][...], mirrored((2 * group + part) * STEP + at))
                    other = jnp.concatenate([other[:BINS], other[BINS:]], axis=1)
                    logits = own[part * BINS : (part + 1) * BINS] + other + sc["hbias"][...]
                    peak = jnp.max(logits, axis=0, keepdims=True)
                    powered = jnp.exp(logits - peak)
                    scale = 1.0 / jnp.sum(powered, axis=0, keepdims=True)
                    hits = jnp.where(sc["binsp"][0, pl.ds(line, 1), :] == bin_ids, 0.5, 0.0)
                    hits += jnp.where(sc["binsp"][1, pl.ds(line, 1), :] == bin_ids, 0.5, 0.0)
                    errors.append(sc["colp"][...] * valid(line) * (powered * scale - hits))
                sc["acc_e"][...] += errors[0] + errors[1]
                error = jnp.concatenate(errors, axis=0)
                coarse = error.astype(BF16)
                fine = (error - coarse.astype(F32)).astype(BF16)
                stack = jnp.concatenate([coarse, fine], axis=0)
                sc["acc_h"][...] += dot_nn(stack, sc["hidp"][place])
                slope = dot_tn(stack, sc["wb2"][...])
                order = []
                for block in range(count):
                    for eighth in range(4):
                        upper = eighth >> 1
                        first = (eighth ^ upper) & 1
                        order.append(upper * half + block * 2 * STEP + first * STEP)
                value = gathered(slope, order) * sc["sl2"][place]
                sc["og"][place] = value
                sc["grad"][place] = value.astype(BF16)
                sc["acc_b"][1] += column_sums(value)
                publish(OUTER, group, at, value)

        send_halo(OUTER, group)

    def near_one(kind, tag, step):
        tall = sc["slots_" + tag].shape[1]
        peer = lax.rem(spot + step, near)
        return pltpu.make_async_remote_copy(
            src_ref=sc["own_" + tag].at[pl.ds(pl.multiple_of(peer * tall, 8), tall)],
            dst_ref=sc["slots_" + tag].at[step],
            send_sem=sc["near_send"].at[kind, 0, step],
            recv_sem=sc["near_recv"].at[kind, 0, step],
            device_id=near_device(peer),
            device_id_type=MESH,
        )

    def far_one(kind, tag, step):
        return pltpu.make_async_remote_copy(
            src_ref=sc["mid_" + tag].at[tier],
            dst_ref=sc["mid_" + tag].at[tier],
            send_sem=sc["far_send"].at[kind, step],
            recv_sem=sc["far_recv"].at[kind, step],
            device_id=far_device(lax.rem(tier + step, far)),
            device_id_type=MESH,
        )

    def near_two(kind, tag, step):
        return pltpu.make_async_remote_copy(
            src_ref=sc["all_" + tag].at[spot],
            dst_ref=sc["all_" + tag].at[spot],
            send_sem=sc["near_send"].at[kind, 1, step],
            recv_sem=sc["near_recv"].at[kind, 1, step],
            device_id=near_device(lax.rem(spot + step, near)),
            device_id_type=MESH,
        )

    def pack_taps(own):
        turned = {name: jnp.transpose(sc["t_" + name][...]) for name in ("edge", "middle")}
        for across in range(TAPS):
            for down in range(TAPS):
                sides = [0.0, 0.0]
                for name, start, part in block_places(down, across):
                    sides[part] = sides[part] + turned[name][start : start + CHANS]
                total = sides[0] + pltpu.roll(sides[1], CHANS, 1)
                packed = jnp.where(
                    halves_mask((CHANS // 2, LANES)),
                    total[: CHANS // 2],
                    pltpu.roll(total[CHANS // 2 :], CHANS, 1),
                )
                start = (down * TAPS + across) * (CHANS // 2)
                own[start : start + CHANS // 2, :] = packed

    def start_sum(kind, tag):
        for step in range(1, near):
            near_one(kind, tag, step).start()

    def middle_sum(kind, tag):
        for step in range(1, near):
            near_one(kind, tag, step).wait()
        tall = sc["slots_" + tag].shape[1]
        total = sc["own_" + tag][pl.ds(pl.multiple_of(spot * tall, 8), tall), :]
        for step in range(1, near):
            total = total + sc["slots_" + tag][step]
        sc["mid_" + tag][tier] = total
        for step in range(1, far):
            far_one(kind, tag, step).start()

    def late_sum(kind, tag):
        for step in range(1, far):
            far_one(kind, tag, step).wait()
        total = sc["mid_" + tag][0]
        for level in range(1, far):
            total = total + sc["mid_" + tag][level]
        sc["all_" + tag][spot] = total
        for step in range(1, near):
            near_two(kind, tag, step).start()

    def end_sum(kind, tag, out):
        for step in range(1, near):
            near_two(kind, tag, step).wait()
        out[...] = sc["all_" + tag][...]

    if relays:

        @pl.when(own_group)
        def _():
            for group in range(groups):
                for block in range(count):
                    relay_forward(block, group, 1 - group % 2).wait_send()

    with jax.named_scope("taps2"):
        add_taps(ACT)
        pack_taps(sc["own_b"])
        both = sc["acc_h"][: 2 * BINS, :] + sc["acc_h"][2 * BINS :, :]
        both = both[:BINS] + pltpu.roll(both[BINS:], CHANS, 1)
        tally = jnp.sum(sc["acc_e"][...], axis=1, keepdims=True)
        sc["own_b"][CONV_ROWS : CONV_ROWS + BINS, :] = jnp.where(
            halves_mask((BINS, LANES)), both, jnp.broadcast_to(tally, (BINS, LANES))
        )
        sc["own_b"][CONV_ROWS + BINS : CONV_ROWS + BINS + 8, :] = sc["acc_b"][1]
        start_sum(1, "b")

    with jax.named_scope("convt2"):
        for kind in (MIDDLE, EDGE):

            def body(at):
                place = kind * STEP + at
                value = conv(OUTER, 2, kind, at) * sc["sl1"][place]
                sc["grad"][place] = value.astype(BF16)
                sc["acc_b"][0] += column_sums(value)
                publish(INNER, kind, at, value)

            conv_step(OUTER, kind, body)
            send_halo(INNER, kind)

    middle_sum(1, "b")

    with jax.named_scope("taps1"):
        add_taps(PAIR)
        pack_taps(sc["own_a"])
        sc["own_a"][CONV_ROWS : CONV_ROWS + 8, :] = sc["acc_b"][0]
        start_sum(0, "a")
    late_sum(1, "b")

    with jax.named_scope("convt1"):
        for kind in (MIDDLE, EDGE):

            def body(at):
                place = kind * STEP + at
                one, two = lines(kind, at)
                value = sc["og"][place] + conv(INNER, 3, kind, at)
                for tile in range(cols // LANES):
                    turned = jnp.transpose(value[tile * LANES : (tile + 1) * LANES])
                    sc["p32"][tile, pl.ds(one, CHANS, stride=rows), :] = turned[:CHANS]
                    sc["p32"][tile, pl.ds(two, CHANS, stride=rows), :] = turned[CHANS:]

            conv_step(INNER, kind, body)
            if kind == MIDDLE:
                middle_sum(0, "a")
        late_sum(0, "a")

        @pl.loop(0, CHANS, unroll=4)
        def _(chan):
            for tile in range(cols // LANES):
                out_pair[chan, :, tile * LANES : (tile + 1) * LANES] = sc["p32"][
                    tile, pl.ds(chan * rows, rows), :
                ].astype(BF16)

    with jax.named_scope("end_sums"):
        end_sum(1, "b", out_b)
        end_sum(0, "a", out_a)


def finish_kernel(near, pair, sums_a, sums_b, mask_v, out_pair, c1w, c1b, c2w, c2b, hgw, hgb):
    out_pair[...] = pair[...]
    scale = 1.0 / jnp.sum(mask_v[...].astype(F32))
    for sums, weight, bias, extra in ((sums_a, c1w, c1b, 0), (sums_b, c2w, c2b, BINS)):
        for tap in range(TAPS * TAPS):
            start = tap * (CHANS // 2)
            value = sums[start : start + CHANS // 2, :] * scale
            weight[tap // TAPS, tap % TAPS, : CHANS // 2, :] = value[:, :CHANS]
            weight[tap // TAPS, tap % TAPS, CHANS // 2 :, :] = value[:, CHANS:]
        start = CONV_ROWS + extra
        total = jnp.sum(sums[start : start + 8, :], axis=0, keepdims=True) * scale
        bias[...] = total[:, :CHANS] + total[:, CHANS:]
    head = sums_b[CONV_ROWS : CONV_ROWS + BINS, :] * scale
    nbins = hgw.shape[0]
    hgw[...] = head[:nbins, :CHANS]
    head = jnp.concatenate([head, jnp.zeros((LANES - BINS, LANES), F32)], axis=0)
    hgb[...] = jnp.transpose(head)[CHANS : CHANS + 1, :nbins]


def on_device(pair, w1, b1, w2, b2, hw, hb, bins, mask):
    nrow = lax.axis_size("ri")
    ncol = lax.axis_size("rj")
    rows, cols = bins.shape
    nbins = hw.shape[1]
    near = GROUP * ncol
    rows_a = chunk_rows(CONV_ROWS + 8, near)
    rows_b = chunk_rows(CONV_ROWS + BINS + 8, near)
    items = scratch_list(rows, cols, nrow, ncol)
    vmem = pl.BlockSpec(memory_space=pltpu.VMEM)
    smem = pl.BlockSpec(memory_space=pltpu.SMEM)
    mask_v = mask.reshape(-1, LANES)
    params = dict(vmem_limit_bytes=56 * 1024 * 1024)
    grad_pair, sums_a, sums_b = pl.pallas_call(
        functools.partial(mega_kernel, tuple(items), nrow, ncol),
        out_shape=[
            jax.ShapeDtypeStruct((CHANS, rows, cols), BF16),
            jax.ShapeDtypeStruct((near, rows_a, LANES), F32),
            jax.ShapeDtypeStruct((near, rows_b, LANES), F32),
        ],
        in_specs=[vmem, smem] + [vmem] * 8,
        out_specs=[vmem] * 3,
        scratch_shapes=list(items.values()),
        compiler_params=pltpu.CompilerParams(collective_id=0, has_side_effects=True, **params),
    )(
        pair, mask, mask_v, w1, b1.reshape(1, -1), w2, b2.reshape(1, -1), hw.T, hb.reshape(1, -1), bins
    )
    shape = (TAPS, TAPS, CHANS, CHANS)
    outs = pl.pallas_call(
        functools.partial(finish_kernel, near),
        out_shape=[
            jax.ShapeDtypeStruct((CHANS, rows, cols), BF16),
            jax.ShapeDtypeStruct(shape, F32),
            jax.ShapeDtypeStruct((1, CHANS), F32),
            jax.ShapeDtypeStruct(shape, F32),
            jax.ShapeDtypeStruct((1, CHANS), F32),
            jax.ShapeDtypeStruct((nbins, CHANS), F32),
            jax.ShapeDtypeStruct((1, nbins), F32),
        ],
        in_specs=[vmem] * 4,
        out_specs=[vmem] * 7,
        compiler_params=pltpu.CompilerParams(**params),
    )(grad_pair, sums_a.reshape(-1, LANES), sums_b.reshape(-1, LANES), mask_v)
    gp, c1w, c1b, c2w, c2b, hgw, hgb = outs
    return gp, c1w, c1b.reshape(-1), c2w, c2b.reshape(-1), hgw.T, hgb.reshape(-1)


def solution(mesh):
    return jax.shard_map(
        on_device,
        mesh=mesh,
        in_specs=(P(None, "ri", "rj"), P(), P(), P(), P(), P(), P(), P("ri", "rj"), P()),
        out_specs=(P(None, "ri", "rj"), P(), P(), P(), P(), P(), P()),
        check_vma=False,
    )
```

```python
import functools

import jax
import jax.numpy as jnp
from jax import lax
from jax.experimental import pallas as pl
from jax.experimental.pallas import tpu as pltpu
from jax.sharding import PartitionSpec as P

TAPS = 3
STEP = 8
CHANS = 64
LANES = 128
BINS = 40
MESH = pl.DeviceIdType.MESH
F32 = jnp.float32
BF16 = jnp.bfloat16
PAIR, ACT, OUTER, INNER = range(4)
EDGE_PARTS = ((0, 4), (4, 8))
MIDDLE_PART = (8, 16)
SIDES = ((-1, 0), (1, 0), (-1, -1), (-1, 1), (1, -1), (1, 1), (0, -1), (0, 1))
MESSAGES = tuple((side, part) for part in EDGE_PARTS for side in SIDES) + tuple(
    (side, MIDDLE_PART) for side in SIDES if side[0] == 0
)
EDGE, MIDDLE = 0, 1
OWN_BLOCKS = ((1, 4), (2, 3))
HALO_BLOCKS = (0, 5)
PLACES = (0, 3, 1, 2)
GROUP = 2
CONV_ROWS = TAPS * TAPS * CHANS // 2


def dot_nt(a, b):
    return lax.dot_general(a, b, (((1,), (1,)), ((), ())), preferred_element_type=F32)


def dot_tn(a, b):
    return lax.dot_general(a, b, (((0,), (0,)), ((), ())), preferred_element_type=F32)


def dot_nn(a, b):
    return jnp.dot(a, b, preferred_element_type=F32)


def halves_mask(shape):
    return lax.broadcasted_iota(jnp.int32, shape, len(shape) - 1) < CHANS


def chunk_rows(used, chunks):
    return -(-used // (16 * chunks)) * 16


def block_places(down, across):
    found = []
    for name, outs in (("edge", OWN_BLOCKS[EDGE]), ("middle", OWN_BLOCKS[MIDDLE])):
        for part, block in enumerate(outs):
            source = block + down - 1
            flat = OWN_BLOCKS[EDGE] + OWN_BLOCKS[MIDDLE]
            if source in flat:
                start = across * 2 * LANES + flat.index(source) * CHANS
            else:
                start = TAPS * 2 * LANES + across * LANES + HALO_BLOCKS.index(source) * CHANS
            found.append((name, start, part))
    return found


def scratch_list(rows, cols, nrow, ncol):
    pairs = rows // 2
    count = cols // rows
    near = GROUP * ncol
    far = nrow // GROUP
    rows_a = chunk_rows(CONV_ROWS + 16, near)
    rows_b = chunk_rows(CONV_ROWS + BINS + 24, near)
    dma = pltpu.SemaphoreType.DMA
    items = dict(
        p32=pltpu.VMEM((cols // LANES, CHANS * rows, LANES), F32),
        qa=pltpu.VMEM((4, pairs + STEP, cols, LANES), BF16),
        qb=pltpu.VMEM((4, pairs + STEP, cols + 2 * STEP, LANES), BF16),
        up=pltpu.VMEM((4, STEP, cols // 2, LANES), BF16),
        down=pltpu.VMEM((4, STEP, cols // 2, LANES), BF16),
        left=pltpu.VMEM((4, pairs, 2 * STEP, LANES), BF16),
        right=pltpu.VMEM((4, pairs, 2 * STEP, LANES), BF16),
        rows_in=pltpu.VMEM((4, 2, STEP, cols // 2, LANES), BF16),
        cols_in=pltpu.VMEM((4, 2, pairs, 2 * STEP, LANES), BF16),
        corner_in=pltpu.VMEM((4, 4, STEP, 2 * STEP, LANES), BF16),
        sl1=pltpu.VMEM((pairs, cols, LANES), F32),
        sl2=pltpu.VMEM((pairs, cols, LANES), F32),
        og=pltpu.VMEM((pairs, cols, LANES), F32),
        hid=pltpu.VMEM((pairs, cols, LANES), BF16),
        hidp=pltpu.VMEM((pairs, cols, LANES), BF16),
        grad=pltpu.VMEM((pairs, cols, LANES), BF16),
        mirror=pltpu.VMEM((count, pairs, rows, LANES), BF16),
        m32=pltpu.VMEM((count, pairs * rows, LANES), F32),
        binsend=pltpu.VMEM((cols, LANES), BF16),
        bins_in=pltpu.VMEM((count, rows, LANES), BF16),
        binsp=pltpu.VMEM((2, rows, cols), F32),
        w_edge=pltpu.VMEM((4, TAPS * 3 * LANES, LANES), BF16),
        w_middle=pltpu.VMEM((4, TAPS * 2 * LANES, LANES), BF16),
        wb=pltpu.VMEM((2 * BINS, LANES), BF16),
        wb2=pltpu.VMEM((4 * BINS, LANES), BF16),
        hwp=pltpu.VMEM((BINS, CHANS), F32),
        small=pltpu.VMEM((8, LANES), F32),
        hbias=pltpu.VMEM((BINS, cols), F32),
        colm=pltpu.VMEM((cols, LANES), F32),
        colp=pltpu.VMEM((BINS, cols), F32),
        t_edge=pltpu.VMEM((LANES, TAPS * 3 * LANES), F32),
        t_middle=pltpu.VMEM((LANES, TAPS * 2 * LANES), F32),
        acc_b=pltpu.VMEM((2, 8, LANES), F32),
        acc_h=pltpu.VMEM((4 * BINS, LANES), F32),
        acc_e=pltpu.VMEM((BINS, cols), F32),
        own_a=pltpu.VMEM((near * rows_a, LANES), BF16),
        own_b=pltpu.VMEM((near * rows_b, LANES), BF16),
        slots_a=pltpu.VMEM((near, rows_a, LANES), BF16),
        slots_b=pltpu.VMEM((near, rows_b, LANES), BF16),
        mid_a=pltpu.VMEM((far, rows_a, LANES), BF16),
        mid_b=pltpu.VMEM((far, rows_b, LANES), BF16),
        all_a=pltpu.VMEM((near, rows_a, LANES), BF16),
        all_b=pltpu.VMEM((near, rows_b, LANES), BF16),
        halo_send=dma((4, len(MESSAGES))),
        halo_recv=dma((4, len(MESSAGES))),
        mir_send=dma((count, 4)),
        mir_recv=dma((count, 4)),
        mir_own=dma((4,)),
        relay=pltpu.VMEM((count, 2, STEP, 2 * STEP, LANES), BF16),
        relay_recv=dma((count, 2)),
        relay_send=dma((count, 2)),
        bin_send=dma((count,)),
        bin_recv=dma((count,)),
        near_send=dma((2, 2, near)),
        near_recv=dma((2, 2, near)),
        far_send=dma((2, far)),
        far_recv=dma((2, far)),
    )
    return items


def mega_kernel(
    names, nrow, ncol,
    pair, mask_s, mask_v, w1, b1, w2, b2, hw, hb, bins, out_pair, out_a, out_b, *scratch
):
    sc = dict(zip(names, scratch))
    rows, cols = bins.shape
    pairs = rows // 2
    groups = pairs // STEP
    count = cols // rows
    half = cols // 2
    near = GROUP * ncol
    far = nrow // GROUP
    row = lax.axis_index("ri")
    column = lax.axis_index("rj")
    slot = lax.rem(row, count)
    far_column = lax.div(row, count)
    own_group = far_column == column
    relays = ncol == 2
    spot = lax.rem(row, GROUP) + GROUP * column
    tier = lax.div(row, GROUP)
    barrier = pltpu.get_barrier_semaphore()

    qa, qb = sc["qa"], sc["qb"]

    def near_device(place):
        return (tier * GROUP + lax.rem(place, GROUP), lax.div(place, GROUP))

    def far_device(level):
        return (level * GROUP + lax.rem(row, GROUP), column)

    def side_exists(side):
        dr, dc = side
        there = None
        for step, here, size in ((dr, row, nrow), (dc, column, ncol)):
            if step:
                one = here > 0 if step < 0 else here < size - 1
                there = one if there is None else jnp.logical_and(there, one)
        return there

    def side_device(side):
        return (row + side[0], column + side[1])

    def meets_self(block):
        return jnp.logical_and(own_group, slot == block)

    def partner(block):
        return (count * column + block, far_column)

    def signal(device):
        pl.semaphore_signal(barrier, inc=1, device_id=device, device_id_type=MESH)

    for side in SIDES:

        @pl.when(side_exists(side))
        def _():
            signal(side_device(side))

    for block in range(count):

        @pl.when(jnp.logical_not(meets_self(block)))
        def _():
            signal(partner(block))

    if relays:

        @pl.when(jnp.logical_not(own_group))
        def _():
            for block in range(count):
                signal((count * column + block, column))

    @pl.loop(1, near)
    def _(step):
        signal(near_device(lax.rem(spot + step, near)))

    @pl.loop(1, far)
    def _(step):
        signal(far_device(lax.rem(tier + step, far)))

    @pl.loop(0, CHANS, unroll=4)
    def _(chan):
        for tile in range(cols // LANES):
            sc["p32"][tile, pl.ds(chan * rows, rows), :] = pair[
                chan, :, tile * LANES : (tile + 1) * LANES
            ].astype(F32)

    lane_low = halves_mask((1, LANES))
    zero8 = jnp.zeros((STEP, LANES), F32)
    low = halves_mask((half, LANES))

    def publish(field, kind, at, value):
        place = kind * STEP + at
        qa[field, place] = value.astype(BF16)
        qb[field, place] = jnp.concatenate([zero8, value, zero8], axis=0).astype(BF16)
        sc["left"][field, place] = value[: 2 * STEP].astype(BF16)
        sc["right"][field, place] = value[cols - 2 * STEP :].astype(BF16)
        if kind == EDGE:
            turned = pltpu.roll(value, CHANS, 1)
            sc["up"][field, at] = jnp.where(low, value[:half], turned[half:]).astype(BF16)
            sc["down"][field, at] = jnp.where(low, turned[:half], value[half:]).astype(BF16)

    def halo_source(field, message):
        (dr, dc), (start, stop) = message
        if dc == 0:
            return sc["up" if dr < 0 else "down"].at[field, pl.ds(start, stop - start)]
        return sc["left" if dc < 0 else "right"].at[field, pl.ds(start, stop - start)]

    def halo_target(field, message):
        (dr, dc), (start, stop) = message
        if dc == 0:
            name, index = "rows_in", 0 if dr < 0 else 1
        elif dr == 0:
            name, index = "cols_in", 0 if dc < 0 else 1
        else:
            name, index = "corner_in", (0 if dr < 0 else 2) + (0 if dc < 0 else 1)
        return sc[name].at[field, index, pl.ds(start, stop - start)]

    def halo_copy(field, message):
        (dr, dc), part = message
        back = ((-dr, -dc), part)
        return pltpu.make_async_remote_copy(
            src_ref=halo_source(field, message),
            dst_ref=halo_target(field, back),
            send_sem=sc["halo_send"].at[field, MESSAGES.index(message)],
            recv_sem=sc["halo_recv"].at[field, MESSAGES.index(back)],
            device_id=side_device((dr, dc)),
            device_id_type=MESH,
        )

    def halo_arrival(field, message):
        index = MESSAGES.index(message)
        return pltpu.make_async_remote_copy(
            src_ref=halo_source(field, message),
            dst_ref=halo_target(field, message),
            send_sem=sc["halo_send"].at[field, index],
            recv_sem=sc["halo_recv"].at[field, index],
            device_id=side_device(message[0]),
            device_id_type=MESH,
        )

    def send_halo(field, part):
        for message in MESSAGES:
            if message[1] == part:

                @pl.when(side_exists(message[0]))
                def _():
                    halo_copy(field, message).start()

    def wait_halo(field, messages):
        for message in messages:

            @pl.when(side_exists(message[0]))
            def _():
                halo_arrival(field, message).wait()

    def place_rows(field, part):
        wait_halo(field, [m for m in MESSAGES if m[1] == part and m[0][0] != 0])

        @pl.loop(*part, unroll=4)
        def _(at):
            above = sc["rows_in"][field, 0, at].astype(F32)
            below = sc["rows_in"][field, 1, at].astype(F32)
            start = jnp.where(low, above, pltpu.roll(below, CHANS, 1))
            rest = jnp.where(low, pltpu.roll(above, CHANS, 1), below)
            wide = jnp.concatenate([start, rest], axis=0)
            qa[field, pairs + at] = wide.astype(BF16)
            edges = []
            for edge in (0, 1):
                upper = sc["corner_in"][field, edge, at].astype(F32)
                lower = sc["corner_in"][field, 2 + edge, at].astype(F32)
                both = pltpu.roll(jnp.where(lane_low, lower, upper), CHANS, 1)
                edges.append(both[STEP:] if edge == 0 else both[:STEP])
            wide = jnp.concatenate([edges[0], wide, edges[1]], axis=0)
            qb[field, pairs + at] = wide.astype(BF16)

    def place_cols(field, parts, starts):
        wait_halo(field, [m for m in MESSAGES if m[0][0] == 0 and m[1] in parts])
        for start in starts:

            @pl.loop(start, start + 4, unroll=4)
            def _(at):
                own = sc["left"][field, at].astype(F32)
                come = sc["cols_in"][field, 0, at].astype(F32)
                both = jnp.concatenate([come[STEP:], own[:STEP]], axis=0)
                qb[field, at, : 2 * STEP, :] = both.astype(BF16)
                own = sc["right"][field, at].astype(F32)
                come = sc["cols_in"][field, 1, at].astype(F32)
                both = jnp.concatenate([own[STEP:], come[:STEP]], axis=0)
                qb[field, at, cols:, :] = both.astype(BF16)

    def taps(field, kind, at):
        starts = (at, STEP + at)
        parts = [qb[field, start, :cols, :] for start in starts]
        parts += [qa[field, start] for start in starts]
        parts += [qb[field, start, 2 * STEP :, :] for start in starts]
        if kind == EDGE:
            start = pairs + at
            parts += [qb[field, start, :cols, :], qa[field, start], qb[field, start, 2 * STEP :, :]]
        return jnp.concatenate(parts, axis=1)

    def conv(field, which, kind, at):
        weight = sc["w_edge" if kind == EDGE else "w_middle"]
        return dot_nn(taps(field, kind, at), weight[which])

    def add_taps(field, kind):
        name = "t_edge" if kind == EDGE else "t_middle"
        sc[name][...] = jnp.zeros(sc[name].shape, F32)

        @pl.loop(0, STEP, unroll=8)
        def _(at):
            sc[name][...] += dot_tn(sc["grad"][kind * STEP + at], taps(field, kind, at))

    def lines(kind, at):
        return (kind * STEP + at, rows - STEP * (kind + 1) + at)

    def column_sums(value):
        total = value[:STEP]
        for start in range(STEP, cols, STEP):
            total = total + value[start : start + STEP]
        return total

    def publish_pair(kind):
        @pl.loop(0, STEP, unroll=2)
        def _(at):
            one, two = lines(kind, at)
            value = []
            for tile in range(cols // LANES):
                upper = sc["p32"][tile, pl.ds(one, CHANS, stride=rows), :]
                lower = sc["p32"][tile, pl.ds(two, CHANS, stride=rows), :]
                value.append(jnp.transpose(jnp.concatenate([upper, lower], axis=0)))
            value = jnp.concatenate(value, axis=0)
            publish(PAIR, kind, at, value)

    for message in MESSAGES:

        @pl.when(jnp.logical_not(side_exists(message[0])))
        def _():
            for field in range(4):
                ref = halo_target(field, message)
                ref[...] = jnp.zeros(ref.shape, ref.dtype)

    publish_pair(EDGE)
    wait_count = 0
    for side in SIDES:
        wait_count = wait_count + side_exists(side).astype(jnp.int32)
    wait_count = wait_count + count - own_group.astype(jnp.int32)
    if relays:
        wait_count = wait_count + count * own_group.astype(jnp.int32)
    pl.semaphore_wait(barrier, wait_count + (near - 1) + (far - 1))
    for part in EDGE_PARTS:
        send_halo(PAIR, part)
    publish_pair(MIDDLE)
    send_halo(PAIR, MIDDLE_PART)

    text = bins[...].astype(F32)
    text = jnp.concatenate([text, jnp.zeros((LANES - rows, cols), F32)], axis=0)
    sc["binsend"][...] = jnp.transpose(text).astype(BF16)

    def bins_source(block):
        return sc["binsend"].at[pl.ds(block * rows, rows)]

    def bins_copy(block, at):
        return pltpu.make_async_remote_copy(
            src_ref=bins_source(block),
            dst_ref=sc["bins_in"].at[at],
            send_sem=sc["bin_send"].at[block],
            recv_sem=sc["bin_recv"].at[at],
            device_id=partner(block),
            device_id_type=MESH,
        )

    for block in range(count):

        @pl.when(jnp.logical_not(meets_self(block)))
        def _():
            bins_copy(block, slot).start()

        @pl.when(meets_self(block))
        def _():
            sc["bins_in"][block] = sc["binsend"][pl.ds(block * rows, rows), :]

    with jax.named_scope("weights"):
        for name in ("w_edge", "w_middle"):
            sc[name][...] = jnp.zeros(sc[name].shape, BF16)
        for which, (weight, flip) in enumerate(((w1, False), (w2, False), (w2, True), (w1, True))):
            for across in range(TAPS):
                for down in range(TAPS):
                    if flip:
                        piece = weight[TAPS - 1 - down, TAPS - 1 - across].astype(F32)
                        piece = jnp.transpose(piece).astype(BF16)
                    else:
                        piece = weight[down, across]
                    for name, start, part in block_places(down, across):
                        sc["w_" + name][
                            which, start : start + CHANS, part * CHANS : (part + 1) * CHANS
                        ] = piece
        nbins = hw.shape[0]
        sc["hwp"][...] = jnp.zeros(sc["hwp"].shape, F32)
        sc["hwp"][:nbins, :] = hw[...].astype(F32)
        flat = sc["hwp"][...]
        none = jnp.zeros_like(flat)
        both = jnp.concatenate(
            [jnp.concatenate([flat, none], axis=1), jnp.concatenate([none, flat], axis=1)], axis=0
        )
        sc["wb"][...] = (0.5 * both).astype(BF16)
        sc["wb2"][...] = jnp.concatenate([both, both], axis=0).astype(BF16)
        sc["small"][...] = jnp.full((8, LANES), -1e30, F32)
        sc["small"][0:1, :nbins] = hb[...]
        spread = jnp.broadcast_to(sc["small"][0:1, :], (LANES, LANES))
        spread = jnp.transpose(spread)[:BINS]
        for start in range(0, cols, LANES):
            sc["hbias"][:, start : start + LANES] = spread
        sc["small"][0:1, :CHANS] = b1[...]
        sc["small"][0:1, CHANS:] = b1[...]
        sc["small"][1:2, :CHANS] = b2[...]
        sc["small"][1:2, CHANS:] = b2[...]
        natural = lax.broadcasted_iota(jnp.int32, (cols, cols), 0)
        placed = lax.broadcasted_iota(jnp.int32, (cols, cols), 1)
        eighth = (natural >> 3) & 3
        upper = eighth >> 1
        goal = upper * half + (natural >> 5) * 2 * STEP + ((eighth ^ upper) & 1) * STEP
        goal = goal + (natural & 7)
        move = jnp.where(placed == goal, 1.0, 0.0).astype(BF16)
        tiles = cols // LANES
        ones_row = [mask_v[pl.ds(column * tiles + tile, 1), :] for tile in range(tiles)]
        ones_row = jnp.concatenate(ones_row, axis=1).astype(F32)
        top = lax.broadcasted_iota(jnp.int32, (2 * STEP, cols), 0) == 0
        ones_row = jnp.where(top, jnp.broadcast_to(ones_row, (2 * STEP, cols)), 0.0).astype(BF16)
        sc["colm"][...] = dot_tn(ones_row, jnp.ones((2 * STEP, LANES), BF16))
        sc["colp"][...] = jnp.broadcast_to(dot_nn(ones_row, move)[0:1], (BINS, cols))
        sc["binsp"][0] = dot_nn(bins[...].astype(F32).astype(BF16), move)
        for ref in (sc["acc_b"], sc["acc_h"], sc["acc_e"]):
            ref[...] = jnp.zeros(ref.shape, F32)
        for ref in (sc["own_a"], sc["own_b"]):
            ref[CONV_ROWS:, :] = jnp.zeros((ref.shape[0] - CONV_ROWS, LANES), BF16)

    def valid(line):
        return mask_s[row * rows + line].astype(F32)

    def pair_mask(kind, at):
        one, two = lines(kind, at)
        return sc["colm"][...] * jnp.where(lane_low, valid(one), valid(two))

    def conv_steps(field, body, sent=None, after=None):
        for part in EDGE_PARTS:
            first = part == EDGE_PARTS[0]
            starts = (part[0], part[0] + STEP)
            place_cols(field, (part, MIDDLE_PART) if first else (part,), starts)

            @pl.loop(*part, unroll=4)
            def _(at):
                body(MIDDLE, at)

        if sent is not None:
            send_halo(sent, MIDDLE_PART)
        if after is not None:
            after(MIDDLE_PART)
        for part in EDGE_PARTS:
            place_rows(field, part)

            @pl.loop(*part, unroll=4)
            def _(at):
                body(EDGE, at)

            if sent is not None:
                send_halo(sent, part)
            if after is not None:
                after(part)

    with jax.named_scope("conv1"):

        def conv1_body(kind, at):
            place = kind * STEP + at
            inner = conv(PAIR, 0, kind, at) + sc["small"][0:1, :]
            power = jnp.exp(jnp.minimum(inner, 0.0))
            value = jnp.where(inner > 0, inner, power - 1.0)
            sc["sl1"][place] = jnp.where(inner > 0, 1.0, power)
            publish(ACT, kind, at, value)

        conv_steps(PAIR, conv1_body, ACT)

    def mirror_source(block, group, part):
        return sc["hid"].at[
            pl.ds(group * STEP, STEP), pl.ds(block * rows + part * 2 * STEP, 2 * STEP)
        ]

    def mirror_target(at, group, part):
        return sc["mirror"].at[at, pl.ds(group * STEP, STEP), pl.ds(part * 2 * STEP, 2 * STEP)]

    def mirror_copy(block, at, group, part):
        piece = 2 * group + part
        return pltpu.make_async_remote_copy(
            src_ref=mirror_source(block, group, part),
            dst_ref=mirror_target(at, group, part),
            send_sem=sc["mir_send"].at[block, piece],
            recv_sem=sc["mir_recv"].at[at, piece],
            device_id=partner(block),
            device_id_type=MESH,
        )

    def mirror_own(block, group, part):
        return pltpu.make_async_copy(
            mirror_source(block, group, part),
            mirror_target(block, group, part),
            sc["mir_own"].at[2 * group + part],
        )

    def relayed(group, part, block):
        return relays and (group + part + block) % 2 == 1

    def relay_copy(block, group, part):
        return pltpu.make_async_remote_copy(
            src_ref=mirror_source(block, group, part),
            dst_ref=sc["relay"].at[block, group],
            send_sem=sc["mir_send"].at[block, 2 * group + part],
            recv_sem=sc["relay_recv"].at[block, group],
            device_id=(row, 1 - column),
            device_id_type=MESH,
        )

    def relay_forward(block, group, part):
        return pltpu.make_async_remote_copy(
            src_ref=sc["relay"].at[block, group],
            dst_ref=mirror_target(slot, group, part),
            send_sem=sc["relay_send"].at[block, group],
            recv_sem=sc["mir_recv"].at[slot, 2 * group + part],
            device_id=(count * (1 - column) + block, column),
            device_id_type=MESH,
        )

    def row_groups(eighths):
        return [rows * block + STEP * at for block in range(count) for at in eighths]

    def gathered(value, starts):
        return jnp.concatenate([value[start : start + STEP] for start in starts], axis=0)

    def send_mirror(group):
        for part in range(2):
            for block in range(count):

                @pl.when(meets_self(block))
                def _():
                    mirror_own(block, group, part).start()

                if relayed(group, part, block):

                    @pl.when(jnp.logical_not(own_group))
                    def _():
                        relay_copy(block, group, part).start()

                    @pl.when(own_group & (slot != block))
                    def _():
                        mirror_copy(block, slot, group, part).start()

                else:

                    @pl.when(jnp.logical_not(meets_self(block)))
                    def _():
                        mirror_copy(block, slot, group, part).start()

    with jax.named_scope("conv2"):

        def conv2_body(kind, at):
            place = kind * STEP + at
            outer = conv(ACT, 1, kind, at) + sc["small"][1:2, :]
            total = qa[PAIR, place].astype(F32) + outer
            power = jnp.exp(jnp.minimum(total, 0.0))
            keep = pair_mask(kind, at)
            hidden = keep * jnp.where(total > 0, total, power - 1.0)
            sc["sl2"][place] = keep * jnp.where(total > 0, 1.0, power)
            sc["hid"][place] = gathered(hidden, row_groups(PLACES)).astype(BF16)
            order = row_groups(PLACES[0:4:2]) + row_groups(PLACES[1:4:2])
            sc["hidp"][place] = gathered(hidden, order).astype(BF16)

        def conv2_after(part):
            if part == MIDDLE_PART:
                send_mirror(MIDDLE)
            if part == EDGE_PARTS[-1]:
                send_mirror(EDGE)

        conv_steps(ACT, conv2_body, None, conv2_after)

    def relay_pieces():
        for group in (MIDDLE, EDGE):
            for part in range(2):
                for block in range(count):
                    if relayed(group, part, block):
                        yield block, group, part

    if relays:

        @pl.when(own_group)
        def _():
            for piece in relay_pieces():
                relay_copy(*piece).wait_recv()
                relay_forward(*piece).start()

    with jax.named_scope("bins"):
        total = jnp.zeros((rows, cols), F32)
        for block in range(count):

            @pl.when(jnp.logical_not(meets_self(block)))
            def _():
                bins_copy(block, block).wait()

            part = move[block * rows : (block + 1) * rows]
            total = total + dot_nn(sc["bins_in"][block][:, :rows], part)
        sc["binsp"][1] = total

    bin_ids = lax.broadcasted_iota(jnp.int32, (BINS, cols), 0).astype(F32)

    def mirrored(line):
        parts = [sc["m32"][block, pl.ds(line, pairs, stride=rows), :] for block in range(count)]
        return jnp.concatenate(parts, axis=0).astype(BF16)

    for group in range(groups):
        with jax.named_scope("wait_mirror"):
            for sender in range(groups):
                for block in range(count):

                    @pl.when(jnp.logical_not(meets_self(block)))
                    def _():
                        mirror_copy(block, block, sender, group).wait()

                    @pl.when(meets_self(block))
                    def _():
                        mirror_own(block, sender, group).wait()

            @pl.loop(0, pairs, unroll=2)
            def _(at):
                for block in range(count):
                    start = pl.multiple_of(at * rows + group * 2 * STEP, 2 * STEP)
                    sc["m32"][block, pl.ds(start, 2 * STEP), :] = sc["mirror"][
                        block, at, group * 2 * STEP : (group + 1) * 2 * STEP, :
                    ].astype(F32)

        with jax.named_scope("head"):

            @pl.loop(0, STEP, unroll=4)
            def _(at):
                place = group * STEP + at
                own = dot_nt(sc["wb"][...], sc["hidp"][place])
                errors = []
                for part, line in enumerate(lines(group, at)):
                    other = dot_nt(sc["wb"][...], mirrored((2 * group + part) * STEP + at))
                    other = jnp.concatenate([other[:BINS], other[BINS:]], axis=1)
                    logits = own[part * BINS : (part + 1) * BINS] + other + sc["hbias"][...]
                    peak = jnp.max(logits, axis=0, keepdims=True)
                    powered = jnp.exp(logits - peak)
                    scale = 1.0 / jnp.sum(powered, axis=0, keepdims=True)
                    hits = jnp.where(sc["binsp"][0, pl.ds(line, 1), :] == bin_ids, 0.5, 0.0)
                    hits += jnp.where(sc["binsp"][1, pl.ds(line, 1), :] == bin_ids, 0.5, 0.0)
                    errors.append(sc["colp"][...] * valid(line) * (powered * scale - hits))
                sc["acc_e"][...] += errors[0] + errors[1]
                error = jnp.concatenate(errors, axis=0)
                coarse = error.astype(BF16)
                fine = (error - coarse.astype(F32)).astype(BF16)
                stack = jnp.concatenate([coarse, fine], axis=0)
                sc["acc_h"][...] += dot_nn(stack, sc["hidp"][place])
                slope = dot_tn(stack, sc["wb2"][...])
                order = []
                for block in range(count):
                    for eighth in range(4):
                        upper = eighth >> 1
                        first = (eighth ^ upper) & 1
                        order.append(upper * half + block * 2 * STEP + first * STEP)
                value = gathered(slope, order) * sc["sl2"][place]
                sc["og"][place] = value
                sc["grad"][place] = value.astype(BF16)
                sc["acc_b"][1] += column_sums(value)
                publish(OUTER, group, at, value)

        for part in EDGE_PARTS if group == EDGE else (MIDDLE_PART,):
            send_halo(OUTER, part)

    def near_one(kind, tag, step):
        tall = sc["slots_" + tag].shape[1]
        peer = lax.rem(spot + step, near)
        return pltpu.make_async_remote_copy(
            src_ref=sc["own_" + tag].at[pl.ds(pl.multiple_of(peer * tall, 16), tall)],
            dst_ref=sc["slots_" + tag].at[step],
            send_sem=sc["near_send"].at[kind, 0, step],
            recv_sem=sc["near_recv"].at[kind, 0, step],
            device_id=near_device(peer),
            device_id_type=MESH,
        )

    def far_one(kind, tag, step):
        return pltpu.make_async_remote_copy(
            src_ref=sc["mid_" + tag].at[tier],
            dst_ref=sc["mid_" + tag].at[tier],
            send_sem=sc["far_send"].at[kind, step],
            recv_sem=sc["far_recv"].at[kind, step],
            device_id=far_device(lax.rem(tier + step, far)),
            device_id_type=MESH,
        )

    def near_two(kind, tag, step):
        return pltpu.make_async_remote_copy(
            src_ref=sc["all_" + tag].at[spot],
            dst_ref=sc["all_" + tag].at[spot],
            send_sem=sc["near_send"].at[kind, 1, step],
            recv_sem=sc["near_recv"].at[kind, 1, step],
            device_id=near_device(lax.rem(spot + step, near)),
            device_id_type=MESH,
        )

    def pack_taps(own):
        turned = {name: jnp.transpose(sc["t_" + name][...]) for name in ("edge", "middle")}
        for across in range(TAPS):
            for down in range(TAPS):
                sides = [0.0, 0.0]
                for name, start, part in block_places(down, across):
                    sides[part] = sides[part] + turned[name][start : start + CHANS]
                total = sides[0] + pltpu.roll(sides[1], CHANS, 1)
                packed = jnp.where(
                    halves_mask((CHANS // 2, LANES)),
                    total[: CHANS // 2],
                    pltpu.roll(total[CHANS // 2 :], CHANS, 1),
                )
                start = (down * TAPS + across) * (CHANS // 2)
                own[start : start + CHANS // 2, :] = packed.astype(BF16)

    def two_rows(parts):
        value = jnp.sum(parts, axis=0, keepdims=True)
        coarse = value.astype(BF16).astype(F32)
        at = lax.broadcasted_iota(jnp.int32, (2 * STEP, LANES), 0)
        return jnp.where(at == 0, coarse, jnp.where(at == 1, value - coarse, 0.0)).astype(BF16)

    def start_sum(kind, tag):
        for step in range(1, near):
            near_one(kind, tag, step).start()

    def middle_sum(kind, tag):
        for step in range(1, near):
            near_one(kind, tag, step).wait()
        tall = sc["slots_" + tag].shape[1]
        total = sc["own_" + tag][pl.ds(pl.multiple_of(spot * tall, 16), tall), :].astype(F32)
        for step in range(1, near):
            total = total + sc["slots_" + tag][step].astype(F32)
        sc["mid_" + tag][tier] = total.astype(BF16)
        for step in range(1, far):
            far_one(kind, tag, step).start()

    def late_sum(kind, tag):
        for step in range(1, far):
            far_one(kind, tag, step).wait()
        total = sc["mid_" + tag][0].astype(F32)
        for level in range(1, far):
            total = total + sc["mid_" + tag][level].astype(F32)
        sc["all_" + tag][spot] = total.astype(BF16)
        for step in range(1, near):
            near_two(kind, tag, step).start()

    def end_sum(kind, tag, out):
        for step in range(1, near):
            near_two(kind, tag, step).wait()
        out[...] = sc["all_" + tag][...]

    if relays:

        @pl.when(own_group)
        def _():
            for piece in relay_pieces():
                relay_forward(*piece).wait_send()

    with jax.named_scope("taps2"):
        add_taps(ACT, MIDDLE)
        add_taps(ACT, EDGE)
        pack_taps(sc["own_b"])
        both = sc["acc_h"][: 2 * BINS, :] + sc["acc_h"][2 * BINS :, :]
        both = both[:BINS] + pltpu.roll(both[BINS:], CHANS, 1)
        tally = jnp.sum(sc["acc_e"][...], axis=1, keepdims=True)
        coarse = tally.astype(BF16).astype(F32)
        lane = lax.broadcasted_iota(jnp.int32, (BINS, LANES), 1)
        sides = jnp.where(
            lane < CHANS + CHANS // 2,
            jnp.broadcast_to(coarse, (BINS, LANES)),
            jnp.broadcast_to(tally - coarse, (BINS, LANES)),
        )
        both = jnp.where(lane < CHANS, both, sides)
        both = jnp.concatenate([both, jnp.zeros((8, LANES), F32)], axis=0)
        sc["own_b"][CONV_ROWS : CONV_ROWS + BINS + 8, :] = both.astype(BF16)
        start = CONV_ROWS + BINS + 8
        sc["own_b"][start : start + 16, :] = two_rows(sc["acc_b"][1])
        start_sum(1, "b")

    with jax.named_scope("convt2"):

        def convt2_body(kind, at):
            place = kind * STEP + at
            value = conv(OUTER, 2, kind, at) * sc["sl1"][place]
            sc["grad"][place] = value.astype(BF16)
            sc["acc_b"][0] += column_sums(value)
            publish(INNER, kind, at, value)

        def convt2_after(part):
            if part == MIDDLE_PART:
                add_taps(PAIR, MIDDLE)
                middle_sum(1, "b")

        conv_steps(OUTER, convt2_body, INNER, convt2_after)

    with jax.named_scope("taps1"):
        add_taps(PAIR, EDGE)
        pack_taps(sc["own_a"])
        sc["own_a"][CONV_ROWS : CONV_ROWS + 16, :] = two_rows(sc["acc_b"][0])
        start_sum(0, "a")
    with jax.named_scope("convt1"):

        def convt1_body(kind, at):
            place = kind * STEP + at
            one, two = lines(kind, at)
            value = sc["og"][place] + conv(INNER, 3, kind, at)
            for tile in range(cols // LANES):
                turned = jnp.transpose(value[tile * LANES : (tile + 1) * LANES])
                sc["p32"][tile, pl.ds(one, CHANS, stride=rows), :] = turned[:CHANS]
                sc["p32"][tile, pl.ds(two, CHANS, stride=rows), :] = turned[CHANS:]

        def convt1_after(part):
            if part == MIDDLE_PART:
                middle_sum(0, "a")
                late_sum(1, "b")
            if part == EDGE_PARTS[1]:
                late_sum(0, "a")

        conv_steps(INNER, convt1_body, None, convt1_after)

        @pl.loop(0, CHANS, unroll=4)
        def _(chan):
            for tile in range(cols // LANES):
                out_pair[chan, :, tile * LANES : (tile + 1) * LANES] = sc["p32"][
                    tile, pl.ds(chan * rows, rows), :
                ].astype(BF16)

    with jax.named_scope("end_sums"):
        end_sum(1, "b", out_b)
        end_sum(0, "a", out_a)


def finish_kernel(pair, sums_a, sums_b, mask_v, out_pair, c1w, c1b, c2w, c2b, hgw, hgb):
    out_pair[...] = pair[...]
    scale = 1.0 / jnp.sum(mask_v[...].astype(F32))
    for sums, weight, bias, extra in ((sums_a, c1w, c1b, 0), (sums_b, c2w, c2b, BINS + 8)):
        for tap in range(TAPS * TAPS):
            start = tap * (CHANS // 2)
            value = sums[start : start + CHANS // 2, :].astype(F32) * scale
            weight[tap // TAPS, tap % TAPS, : CHANS // 2, :] = value[:, :CHANS]
            weight[tap // TAPS, tap % TAPS, CHANS // 2 :, :] = value[:, CHANS:]
        start = CONV_ROWS + extra
        total = sums[start : start + 16, :].astype(F32)
        total = jnp.sum(total, axis=0, keepdims=True) * scale
        bias[...] = total[:, :CHANS] + total[:, CHANS:]
    head = sums_b[CONV_ROWS : CONV_ROWS + BINS + 8, :].astype(F32)[:BINS] * scale
    nbins = hgw.shape[0]
    hgw[...] = head[:nbins, :CHANS]
    head = jnp.concatenate([head, jnp.zeros((LANES - BINS, LANES), F32)], axis=0)
    head = jnp.transpose(head)
    middle = CHANS + CHANS // 2
    hgb[...] = head[CHANS : CHANS + 1, :nbins] + head[middle : middle + 1, :nbins]


def on_device(pair, w1, b1, w2, b2, hw, hb, bins, mask):
    nrow = lax.axis_size("ri")
    ncol = lax.axis_size("rj")
    rows, cols = bins.shape
    nbins = hw.shape[1]
    near = GROUP * ncol
    rows_a = chunk_rows(CONV_ROWS + 16, near)
    rows_b = chunk_rows(CONV_ROWS + BINS + 24, near)
    items = scratch_list(rows, cols, nrow, ncol)
    vmem = pl.BlockSpec(memory_space=pltpu.VMEM)
    smem = pl.BlockSpec(memory_space=pltpu.SMEM)
    mask_v = mask.reshape(-1, LANES)
    params = dict(vmem_limit_bytes=56 * 1024 * 1024)
    grad_pair, sums_a, sums_b = pl.pallas_call(
        functools.partial(mega_kernel, tuple(items), nrow, ncol),
        out_shape=[
            jax.ShapeDtypeStruct((CHANS, rows, cols), BF16),
            jax.ShapeDtypeStruct((near, rows_a, LANES), BF16),
            jax.ShapeDtypeStruct((near, rows_b, LANES), BF16),
        ],
        in_specs=[vmem, smem] + [vmem] * 8,
        out_specs=[vmem] * 3,
        scratch_shapes=list(items.values()),
        compiler_params=pltpu.CompilerParams(collective_id=0, has_side_effects=True, **params),
    )(
        pair, mask, mask_v, w1, b1.reshape(1, -1), w2, b2.reshape(1, -1), hw.T, hb.reshape(1, -1), bins
    )
    shape = (TAPS, TAPS, CHANS, CHANS)
    outs = pl.pallas_call(
        finish_kernel,
        out_shape=[
            jax.ShapeDtypeStruct((CHANS, rows, cols), BF16),
            jax.ShapeDtypeStruct(shape, F32),
            jax.ShapeDtypeStruct((1, CHANS), F32),
            jax.ShapeDtypeStruct(shape, F32),
            jax.ShapeDtypeStruct((1, CHANS), F32),
            jax.ShapeDtypeStruct((nbins, CHANS), F32),
            jax.ShapeDtypeStruct((1, nbins), F32),
        ],
        in_specs=[vmem] * 4,
        out_specs=[vmem] * 7,
        compiler_params=pltpu.CompilerParams(**params),
    )(grad_pair, sums_a.reshape(-1, LANES), sums_b.reshape(-1, LANES), mask_v)
    gp, c1w, c1b, c2w, c2b, hgw, hgb = outs
    return gp, c1w, c1b.reshape(-1), c2w, c2b.reshape(-1), hgw.T, hgb.reshape(-1)


def solution(mesh):
    return jax.shard_map(
        on_device,
        mesh=mesh,
        in_specs=(P(None, "ri", "rj"), P(), P(), P(), P(), P(), P(), P("ri", "rj"), P()),
        out_specs=(P(None, "ri", "rj"), P(), P(), P(), P(), P(), P()),
        check_vma=False,
    )
```

```python
import functools

import jax
import jax.numpy as jnp
from jax import lax
from jax.experimental import pallas as pl
from jax.experimental.pallas import tpu as pltpu
from jax.sharding import PartitionSpec as P

TAPS = 3
STEP = 8
CHANS = 64
LANES = 128
BINS = 40
MESH = pl.DeviceIdType.MESH
F32 = jnp.float32
BF16 = jnp.bfloat16
PAIR, ACT, OUTER, INNER = range(4)
EDGE_PARTS = ((0, 4), (4, 8))
MIDDLE_PART = (8, 16)
SIDES = ((-1, 0), (1, 0), (-1, -1), (-1, 1), (1, -1), (1, 1), (0, -1), (0, 1))
MESSAGES = tuple((side, part) for part in EDGE_PARTS for side in SIDES) + tuple(
    (side, MIDDLE_PART) for side in SIDES if side[0] == 0
)
EDGE, MIDDLE = 0, 1
OWN_BLOCKS = ((1, 4), (2, 3))
HALO_BLOCKS = (0, 5)
PLACES = (0, 3, 1, 2)
GROUP = 2
CONV_ROWS = TAPS * TAPS * CHANS // 2


def dot_nt(a, b):
    return lax.dot_general(a, b, (((1,), (1,)), ((), ())), preferred_element_type=F32)


def dot_tn(a, b):
    return lax.dot_general(a, b, (((0,), (0,)), ((), ())), preferred_element_type=F32)


def dot_nn(a, b):
    return jnp.dot(a, b, preferred_element_type=F32)


def halves_mask(shape):
    return lax.broadcasted_iota(jnp.int32, shape, len(shape) - 1) < CHANS


def chunk_rows(used, chunks):
    return -(-used // (16 * chunks)) * 16


def block_places(down, across):
    found = []
    for name, outs in (("edge", OWN_BLOCKS[EDGE]), ("middle", OWN_BLOCKS[MIDDLE])):
        for part, block in enumerate(outs):
            source = block + down - 1
            flat = OWN_BLOCKS[EDGE] + OWN_BLOCKS[MIDDLE]
            if source in flat:
                start = across * 2 * LANES + flat.index(source) * CHANS
            else:
                start = TAPS * 2 * LANES + across * LANES + HALO_BLOCKS.index(source) * CHANS
            found.append((name, start, part))
    return found


def scratch_list(rows, cols, nrow, ncol):
    pairs = rows // 2
    count = cols // rows
    near = GROUP * ncol
    far = nrow // GROUP
    rows_a = chunk_rows(CONV_ROWS + 16, near)
    rows_b = chunk_rows(CONV_ROWS + BINS + 24, near)
    dma = pltpu.SemaphoreType.DMA
    items = dict(
        p32=pltpu.VMEM((cols // LANES, CHANS * rows, LANES), F32),
        qa=pltpu.VMEM((4, pairs + STEP, cols, LANES), BF16),
        qb=pltpu.VMEM((4, pairs + STEP, cols + 2 * STEP, LANES), BF16),
        up=pltpu.VMEM((4, STEP, cols // 2, LANES), BF16),
        down=pltpu.VMEM((4, STEP, cols // 2, LANES), BF16),
        left=pltpu.VMEM((4, pairs, 2 * STEP, LANES), BF16),
        right=pltpu.VMEM((4, pairs, 2 * STEP, LANES), BF16),
        rows_in=pltpu.VMEM((4, 2, STEP, cols // 2, LANES), BF16),
        cols_in=pltpu.VMEM((4, 2, pairs, 2 * STEP, LANES), BF16),
        corner_in=pltpu.VMEM((4, 4, STEP, 2 * STEP, LANES), BF16),
        sl1=pltpu.VMEM((pairs, cols, LANES), F32),
        sl2=pltpu.VMEM((pairs, cols, LANES), F32),
        og=pltpu.VMEM((pairs, cols, LANES), F32),
        hid=pltpu.VMEM((pairs, cols, LANES), BF16),
        hidp=pltpu.VMEM((pairs, cols, LANES), BF16),
        grad=pltpu.VMEM((pairs, cols, LANES), BF16),
        mirror=pltpu.VMEM((count, pairs, rows, LANES), BF16),
        m32=pltpu.VMEM((count, pairs * rows, LANES), F32),
        binsend=pltpu.VMEM((cols, LANES), BF16),
        bins_in=pltpu.VMEM((count, rows, LANES), BF16),
        binsp=pltpu.VMEM((2, rows, cols), F32),
        w_edge=pltpu.VMEM((4, TAPS * 3 * LANES, LANES), BF16),
        w_middle=pltpu.VMEM((4, TAPS * 2 * LANES, LANES), BF16),
        wb=pltpu.VMEM((2 * BINS, LANES), BF16),
        wb2=pltpu.VMEM((4 * BINS, LANES), BF16),
        hwp=pltpu.VMEM((BINS, CHANS), F32),
        small=pltpu.VMEM((8, LANES), F32),
        hbias=pltpu.VMEM((BINS, cols), F32),
        colm=pltpu.VMEM((cols, LANES), F32),
        colp=pltpu.VMEM((BINS, cols), F32),
        t_edge=pltpu.VMEM((LANES, TAPS * 3 * LANES), F32),
        t_middle=pltpu.VMEM((LANES, TAPS * 2 * LANES), F32),
        acc_b=pltpu.VMEM((2, 8, LANES), F32),
        acc_h=pltpu.VMEM((4 * BINS, LANES), F32),
        acc_e=pltpu.VMEM((BINS, cols), F32),
        own_a=pltpu.VMEM((near * rows_a, LANES), BF16),
        own_b=pltpu.VMEM((near * rows_b, LANES), BF16),
        slots_a=pltpu.VMEM((near, rows_a, LANES), BF16),
        slots_b=pltpu.VMEM((near, rows_b, LANES), BF16),
        mid_a=pltpu.VMEM((far, rows_a, LANES), BF16),
        mid_b=pltpu.VMEM((far, rows_b, LANES), BF16),
        all_a=pltpu.VMEM((near, rows_a, LANES), BF16),
        all_b=pltpu.VMEM((near, rows_b, LANES), BF16),
        halo_send=dma((4, len(MESSAGES))),
        halo_recv=dma((4, len(MESSAGES))),
        mir_send=dma((count, 4)),
        mir_recv=dma((count, 4)),
        mir_own=dma((4,)),
        relay=pltpu.VMEM((count, 2, STEP, 2 * STEP, LANES), BF16),
        relay_recv=dma((count, 2)),
        relay_send=dma((count, 2)),
        bin_send=dma((count,)),
        bin_recv=dma((count,)),
        near_send=dma((2, 2, near)),
        near_recv=dma((2, 2, near)),
        far_send=dma((2, far)),
        far_recv=dma((2, far)),
    )
    return items


def mega_kernel(
    names, nrow, ncol,
    pair, mask_s, mask_v, w1, b1, w2, b2, hw, hb, bins, out_pair, out_a, out_b, *scratch
):
    sc = dict(zip(names, scratch))
    rows, cols = bins.shape
    pairs = rows // 2
    groups = pairs // STEP
    count = cols // rows
    half = cols // 2
    near = GROUP * ncol
    far = nrow // GROUP
    row = lax.axis_index("ri")
    column = lax.axis_index("rj")
    slot = lax.rem(row, count)
    far_column = lax.div(row, count)
    own_group = far_column == column
    relays = ncol == 2
    spot = lax.rem(row, GROUP) + GROUP * column
    tier = lax.div(row, GROUP)
    barrier = pltpu.get_barrier_semaphore()

    qa, qb = sc["qa"], sc["qb"]

    def near_device(place):
        return (tier * GROUP + lax.rem(place, GROUP), lax.div(place, GROUP))

    def far_device(level):
        return (level * GROUP + lax.rem(row, GROUP), column)

    def side_exists(side):
        dr, dc = side
        there = None
        for step, here, size in ((dr, row, nrow), (dc, column, ncol)):
            if step:
                one = here > 0 if step < 0 else here < size - 1
                there = one if there is None else jnp.logical_and(there, one)
        return there

    def side_device(side):
        return (row + side[0], column + side[1])

    def meets_self(block):
        return jnp.logical_and(own_group, slot == block)

    def partner(block):
        return (count * column + block, far_column)

    def signal(device):
        pl.semaphore_signal(barrier, inc=1, device_id=device, device_id_type=MESH)

    for side in SIDES:

        @pl.when(side_exists(side))
        def _():
            signal(side_device(side))

    for block in range(count):

        @pl.when(jnp.logical_not(meets_self(block)))
        def _():
            signal(partner(block))

    if relays:

        @pl.when(jnp.logical_not(own_group))
        def _():
            for block in range(count):
                signal((count * column + block, column))

    @pl.loop(1, near)
    def _(step):
        signal(near_device(lax.rem(spot + step, near)))

    @pl.loop(1, far)
    def _(step):
        signal(far_device(lax.rem(tier + step, far)))

    @pl.loop(0, CHANS, unroll=4)
    def _(chan):
        for tile in range(cols // LANES):
            sc["p32"][tile, pl.ds(chan * rows, rows), :] = pair[
                chan, :, tile * LANES : (tile + 1) * LANES
            ].astype(F32)

    lane_low = halves_mask((1, LANES))
    zero8 = jnp.zeros((STEP, LANES), F32)
    low = halves_mask((half, LANES))

    def publish(field, kind, at, value):
        place = kind * STEP + at
        qa[field, place] = value.astype(BF16)
        qb[field, place] = jnp.concatenate([zero8, value, zero8], axis=0).astype(BF16)
        sc["left"][field, place] = value[: 2 * STEP].astype(BF16)
        sc["right"][field, place] = value[cols - 2 * STEP :].astype(BF16)
        if kind == EDGE:
            turned = pltpu.roll(value, CHANS, 1)
            sc["up"][field, at] = jnp.where(low, value[:half], turned[half:]).astype(BF16)
            sc["down"][field, at] = jnp.where(low, turned[:half], value[half:]).astype(BF16)

    def halo_source(field, message):
        (dr, dc), (start, stop) = message
        if dc == 0:
            return sc["up" if dr < 0 else "down"].at[field, pl.ds(start, stop - start)]
        return sc["left" if dc < 0 else "right"].at[field, pl.ds(start, stop - start)]

    def halo_target(field, message):
        (dr, dc), (start, stop) = message
        if dc == 0:
            name, index = "rows_in", 0 if dr < 0 else 1
        elif dr == 0:
            name, index = "cols_in", 0 if dc < 0 else 1
        else:
            name, index = "corner_in", (0 if dr < 0 else 2) + (0 if dc < 0 else 1)
        return sc[name].at[field, index, pl.ds(start, stop - start)]

    def halo_copy(field, message):
        (dr, dc), part = message
        back = ((-dr, -dc), part)
        return pltpu.make_async_remote_copy(
            src_ref=halo_source(field, message),
            dst_ref=halo_target(field, back),
            send_sem=sc["halo_send"].at[field, MESSAGES.index(message)],
            recv_sem=sc["halo_recv"].at[field, MESSAGES.index(back)],
            device_id=side_device((dr, dc)),
            device_id_type=MESH,
        )

    def halo_arrival(field, message):
        index = MESSAGES.index(message)
        return pltpu.make_async_remote_copy(
            src_ref=halo_source(field, message),
            dst_ref=halo_target(field, message),
            send_sem=sc["halo_send"].at[field, index],
            recv_sem=sc["halo_recv"].at[field, index],
            device_id=side_device(message[0]),
            device_id_type=MESH,
        )

    def send_halo(field, part):
        for message in MESSAGES:
            if message[1] == part:

                @pl.when(side_exists(message[0]))
                def _():
                    halo_copy(field, message).start()

    def wait_halo(field, messages):
        for message in messages:

            @pl.when(side_exists(message[0]))
            def _():
                halo_arrival(field, message).wait()

    def place_rows(field, part):
        wait_halo(field, [m for m in MESSAGES if m[1] == part and m[0][0] != 0])

        @pl.loop(*part, unroll=4)
        def _(at):
            above = sc["rows_in"][field, 0, at].astype(F32)
            below = sc["rows_in"][field, 1, at].astype(F32)
            start = jnp.where(low, above, pltpu.roll(below, CHANS, 1))
            rest = jnp.where(low, pltpu.roll(above, CHANS, 1), below)
            wide = jnp.concatenate([start, rest], axis=0)
            qa[field, pairs + at] = wide.astype(BF16)
            edges = []
            for edge in (0, 1):
                upper = sc["corner_in"][field, edge, at].astype(F32)
                lower = sc["corner_in"][field, 2 + edge, at].astype(F32)
                both = pltpu.roll(jnp.where(lane_low, lower, upper), CHANS, 1)
                edges.append(both[STEP:] if edge == 0 else both[:STEP])
            wide = jnp.concatenate([edges[0], wide, edges[1]], axis=0)
            qb[field, pairs + at] = wide.astype(BF16)

    def place_cols(field, parts, starts):
        wait_halo(field, [m for m in MESSAGES if m[0][0] == 0 and m[1] in parts])
        for start in starts:

            @pl.loop(start, start + 4, unroll=4)
            def _(at):
                own = sc["left"][field, at].astype(F32)
                come = sc["cols_in"][field, 0, at].astype(F32)
                both = jnp.concatenate([come[STEP:], own[:STEP]], axis=0)
                qb[field, at, : 2 * STEP, :] = both.astype(BF16)
                own = sc["right"][field, at].astype(F32)
                come = sc["cols_in"][field, 1, at].astype(F32)
                both = jnp.concatenate([own[STEP:], come[:STEP]], axis=0)
                qb[field, at, cols:, :] = both.astype(BF16)

    def taps(field, kind, at):
        starts = (at, STEP + at)
        parts = [qb[field, start, :cols, :] for start in starts]
        parts += [qa[field, start] for start in starts]
        parts += [qb[field, start, 2 * STEP :, :] for start in starts]
        if kind == EDGE:
            start = pairs + at
            parts += [qb[field, start, :cols, :], qa[field, start], qb[field, start, 2 * STEP :, :]]
        return jnp.concatenate(parts, axis=1)

    def conv(field, which, kind, at):
        weight = sc["w_edge" if kind == EDGE else "w_middle"]
        return dot_nn(taps(field, kind, at), weight[which])

    def add_taps(field, kind):
        name = "t_edge" if kind == EDGE else "t_middle"
        sc[name][...] = jnp.zeros(sc[name].shape, F32)

        @pl.loop(0, STEP, unroll=8)
        def _(at):
            sc[name][...] += dot_tn(sc["grad"][kind * STEP + at], taps(field, kind, at))

    def lines(kind, at):
        return (kind * STEP + at, rows - STEP * (kind + 1) + at)

    def column_sums(value):
        total = value[:STEP]
        for start in range(STEP, cols, STEP):
            total = total + value[start : start + STEP]
        return total

    def publish_pair(kind):
        @pl.loop(0, STEP, unroll=2)
        def _(at):
            one, two = lines(kind, at)
            value = []
            for tile in range(cols // LANES):
                upper = sc["p32"][tile, pl.ds(one, CHANS, stride=rows), :]
                lower = sc["p32"][tile, pl.ds(two, CHANS, stride=rows), :]
                value.append(jnp.transpose(jnp.concatenate([upper, lower], axis=0)))
            value = jnp.concatenate(value, axis=0)
            publish(PAIR, kind, at, value)

    for message in MESSAGES:

        @pl.when(jnp.logical_not(side_exists(message[0])))
        def _():
            for field in range(4):
                ref = halo_target(field, message)
                ref[...] = jnp.zeros(ref.shape, ref.dtype)

    publish_pair(EDGE)
    wait_count = 0
    for side in SIDES:
        wait_count = wait_count + side_exists(side).astype(jnp.int32)
    wait_count = wait_count + count - own_group.astype(jnp.int32)
    if relays:
        wait_count = wait_count + count * own_group.astype(jnp.int32)
    pl.semaphore_wait(barrier, wait_count + (near - 1) + (far - 1))
    for part in EDGE_PARTS:
        send_halo(PAIR, part)
    publish_pair(MIDDLE)
    send_halo(PAIR, MIDDLE_PART)

    text = bins[...].astype(F32)
    text = jnp.concatenate([text, jnp.zeros((LANES - rows, cols), F32)], axis=0)
    sc["binsend"][...] = jnp.transpose(text).astype(BF16)

    def bins_source(block):
        return sc["binsend"].at[pl.ds(block * rows, rows)]

    def bins_copy(block, at):
        return pltpu.make_async_remote_copy(
            src_ref=bins_source(block),
            dst_ref=sc["bins_in"].at[at],
            send_sem=sc["bin_send"].at[block],
            recv_sem=sc["bin_recv"].at[at],
            device_id=partner(block),
            device_id_type=MESH,
        )

    for block in range(count):

        @pl.when(jnp.logical_not(meets_self(block)))
        def _():
            bins_copy(block, slot).start()

        @pl.when(meets_self(block))
        def _():
            sc["bins_in"][block] = sc["binsend"][pl.ds(block * rows, rows), :]

    with jax.named_scope("weights"):
        for name in ("w_edge", "w_middle"):
            sc[name][...] = jnp.zeros(sc[name].shape, BF16)
        for which, (weight, flip) in enumerate(((w1, False), (w2, False), (w2, True), (w1, True))):
            for across in range(TAPS):
                for down in range(TAPS):
                    if flip:
                        piece = weight[TAPS - 1 - down, TAPS - 1 - across].astype(F32)
                        piece = jnp.transpose(piece).astype(BF16)
                    else:
                        piece = weight[down, across]
                    for name, start, part in block_places(down, across):
                        sc["w_" + name][
                            which, start : start + CHANS, part * CHANS : (part + 1) * CHANS
                        ] = piece
        nbins = hw.shape[0]
        sc["hwp"][...] = jnp.zeros(sc["hwp"].shape, F32)
        sc["hwp"][:nbins, :] = hw[...].astype(F32)
        flat = sc["hwp"][...]
        none = jnp.zeros_like(flat)
        both = jnp.concatenate(
            [jnp.concatenate([flat, none], axis=1), jnp.concatenate([none, flat], axis=1)], axis=0
        )
        sc["wb"][...] = (0.5 * both).astype(BF16)
        sc["wb2"][...] = jnp.concatenate([both, both], axis=0).astype(BF16)
        sc["small"][...] = jnp.full((8, LANES), -1e30, F32)
        sc["small"][0:1, :nbins] = hb[...]
        spread = jnp.broadcast_to(sc["small"][0:1, :], (LANES, LANES))
        spread = jnp.transpose(spread)[:BINS]
        for start in range(0, cols, LANES):
            sc["hbias"][:, start : start + LANES] = spread
        sc["small"][0:1, :CHANS] = b1[...]
        sc["small"][0:1, CHANS:] = b1[...]
        sc["small"][1:2, :CHANS] = b2[...]
        sc["small"][1:2, CHANS:] = b2[...]
        natural = lax.broadcasted_iota(jnp.int32, (cols, cols), 0)
        placed = lax.broadcasted_iota(jnp.int32, (cols, cols), 1)
        eighth = (natural >> 3) & 3
        upper = eighth >> 1
        goal = upper * half + (natural >> 5) * 2 * STEP + ((eighth ^ upper) & 1) * STEP
        goal = goal + (natural & 7)
        move = jnp.where(placed == goal, 1.0, 0.0).astype(BF16)
        tiles = cols // LANES
        ones_row = [mask_v[pl.ds(column * tiles + tile, 1), :] for tile in range(tiles)]
        ones_row = jnp.concatenate(ones_row, axis=1).astype(F32)
        top = lax.broadcasted_iota(jnp.int32, (2 * STEP, cols), 0) == 0
        ones_row = jnp.where(top, jnp.broadcast_to(ones_row, (2 * STEP, cols)), 0.0).astype(BF16)
        sc["colm"][...] = dot_tn(ones_row, jnp.ones((2 * STEP, LANES), BF16))
        sc["colp"][...] = jnp.broadcast_to(dot_nn(ones_row, move)[0:1], (BINS, cols))
        sc["binsp"][0] = dot_nn(bins[...].astype(F32).astype(BF16), move)
        for ref in (sc["acc_b"], sc["acc_h"], sc["acc_e"]):
            ref[...] = jnp.zeros(ref.shape, F32)
        for ref in (sc["own_a"], sc["own_b"]):
            ref[CONV_ROWS:, :] = jnp.zeros((ref.shape[0] - CONV_ROWS, LANES), BF16)

    def valid(line):
        return mask_s[row * rows + line].astype(F32)

    def pair_mask(kind, at):
        one, two = lines(kind, at)
        return sc["colm"][...] * jnp.where(lane_low, valid(one), valid(two))

    def conv_steps(field, body, sent=None, after=None):
        for part in EDGE_PARTS:
            first = part == EDGE_PARTS[0]
            starts = (part[0], part[0] + STEP)
            place_cols(field, (part, MIDDLE_PART) if first else (part,), starts)

            @pl.loop(*part, unroll=4)
            def _(at):
                body(MIDDLE, at)

        if sent is not None:
            send_halo(sent, MIDDLE_PART)
        if after is not None:
            after(MIDDLE_PART)
        for part in EDGE_PARTS:
            place_rows(field, part)

            @pl.loop(*part, unroll=4)
            def _(at):
                body(EDGE, at)

            if sent is not None:
                send_halo(sent, part)
            if after is not None:
                after(part)

    with jax.named_scope("conv1"):

        def conv1_body(kind, at):
            place = kind * STEP + at
            inner = conv(PAIR, 0, kind, at) + sc["small"][0:1, :]
            power = jnp.exp(jnp.minimum(inner, 0.0))
            value = jnp.where(inner > 0, inner, power - 1.0)
            sc["sl1"][place] = jnp.where(inner > 0, 1.0, power)
            publish(ACT, kind, at, value)

        conv_steps(PAIR, conv1_body, ACT)

    def mirror_source(block, group, part):
        return sc["hid"].at[
            pl.ds(group * STEP, STEP), pl.ds(block * rows + part * 2 * STEP, 2 * STEP)
        ]

    def mirror_target(at, group, part):
        return sc["mirror"].at[at, pl.ds(group * STEP, STEP), pl.ds(part * 2 * STEP, 2 * STEP)]

    def mirror_copy(block, at, group, part):
        piece = 2 * group + part
        return pltpu.make_async_remote_copy(
            src_ref=mirror_source(block, group, part),
            dst_ref=mirror_target(at, group, part),
            send_sem=sc["mir_send"].at[block, piece],
            recv_sem=sc["mir_recv"].at[at, piece],
            device_id=partner(block),
            device_id_type=MESH,
        )

    def mirror_own(block, group, part):
        return pltpu.make_async_copy(
            mirror_source(block, group, part),
            mirror_target(block, group, part),
            sc["mir_own"].at[2 * group + part],
        )

    def relayed(group, part, block):
        return relays and (group + part + block) % 2 == 1

    def relay_copy(block, group, part):
        return pltpu.make_async_remote_copy(
            src_ref=mirror_source(block, group, part),
            dst_ref=sc["relay"].at[block, group],
            send_sem=sc["mir_send"].at[block, 2 * group + part],
            recv_sem=sc["relay_recv"].at[block, group],
            device_id=(row, 1 - column),
            device_id_type=MESH,
        )

    def relay_forward(block, group, part):
        return pltpu.make_async_remote_copy(
            src_ref=sc["relay"].at[block, group],
            dst_ref=mirror_target(slot, group, part),
            send_sem=sc["relay_send"].at[block, group],
            recv_sem=sc["mir_recv"].at[slot, 2 * group + part],
            device_id=(count * (1 - column) + block, column),
            device_id_type=MESH,
        )

    def row_groups(eighths):
        return [rows * block + STEP * at for block in range(count) for at in eighths]

    def gathered(value, starts):
        return jnp.concatenate([value[start : start + STEP] for start in starts], axis=0)

    def send_mirror(group):
        for part in range(2):
            for block in range(count):

                @pl.when(meets_self(block))
                def _():
                    mirror_own(block, group, part).start()

                if relayed(group, part, block):

                    @pl.when(jnp.logical_not(own_group))
                    def _():
                        relay_copy(block, group, part).start()

                    @pl.when(own_group & (slot != block))
                    def _():
                        mirror_copy(block, slot, group, part).start()

                else:

                    @pl.when(jnp.logical_not(meets_self(block)))
                    def _():
                        mirror_copy(block, slot, group, part).start()

    with jax.named_scope("conv2"):

        def conv2_body(kind, at):
            place = kind * STEP + at
            outer = conv(ACT, 1, kind, at) + sc["small"][1:2, :]
            total = qa[PAIR, place].astype(F32) + outer
            power = jnp.exp(jnp.minimum(total, 0.0))
            keep = pair_mask(kind, at)
            hidden = keep * jnp.where(total > 0, total, power - 1.0)
            sc["sl2"][place] = keep * jnp.where(total > 0, 1.0, power)
            sc["hid"][place] = gathered(hidden, row_groups(PLACES)).astype(BF16)
            order = row_groups(PLACES[0:4:2]) + row_groups(PLACES[1:4:2])
            sc["hidp"][place] = gathered(hidden, order).astype(BF16)

        def conv2_after(part):
            if part == MIDDLE_PART:
                send_mirror(MIDDLE)
            if part == EDGE_PARTS[-1]:
                send_mirror(EDGE)

        conv_steps(ACT, conv2_body, None, conv2_after)

    def relay_pieces():
        for group in (MIDDLE, EDGE):
            for part in range(2):
                for block in range(count):
                    if relayed(group, part, block):
                        yield block, group, part

    if relays:

        @pl.when(own_group)
        def _():
            for piece in relay_pieces():
                relay_copy(*piece).wait_recv()
                relay_forward(*piece).start()

    with jax.named_scope("bins"):
        total = jnp.zeros((rows, cols), F32)
        for block in range(count):

            @pl.when(jnp.logical_not(meets_self(block)))
            def _():
                bins_copy(block, block).wait()

            part = move[block * rows : (block + 1) * rows]
            total = total + dot_nn(sc["bins_in"][block][:, :rows], part)
        sc["binsp"][1] = total

    bin_ids = lax.broadcasted_iota(jnp.int32, (BINS, cols), 0).astype(F32)

    def mirrored(line):
        parts = [sc["m32"][block, pl.ds(line, pairs, stride=rows), :] for block in range(count)]
        return jnp.concatenate(parts, axis=0).astype(BF16)

    for group in range(groups):
        with jax.named_scope("wait_mirror"):
            for sender in range(groups):
                for block in range(count):

                    @pl.when(jnp.logical_not(meets_self(block)))
                    def _():
                        mirror_copy(block, block, sender, group).wait()

                    @pl.when(meets_self(block))
                    def _():
                        mirror_own(block, sender, group).wait()

            @pl.loop(0, pairs, unroll=2)
            def _(at):
                for block in range(count):
                    start = pl.multiple_of(at * rows + group * 2 * STEP, 2 * STEP)
                    sc["m32"][block, pl.ds(start, 2 * STEP), :] = sc["mirror"][
                        block, at, group * 2 * STEP : (group + 1) * 2 * STEP, :
                    ].astype(F32)

        with jax.named_scope("head"):

            @pl.loop(0, STEP, unroll=4)
            def _(at):
                place = group * STEP + at
                own = dot_nt(sc["wb"][...], sc["hidp"][place])
                errors = []
                for part, line in enumerate(lines(group, at)):
                    other = dot_nt(sc["wb"][...], mirrored((2 * group + part) * STEP + at))
                    other = jnp.concatenate([other[:BINS], other[BINS:]], axis=1)
                    logits = own[part * BINS : (part + 1) * BINS] + other + sc["hbias"][...]
                    peak = jnp.max(logits, axis=0, keepdims=True)
                    powered = jnp.exp(logits - peak)
                    scale = 1.0 / jnp.sum(powered, axis=0, keepdims=True)
                    hits = jnp.where(sc["binsp"][0, pl.ds(line, 1), :] == bin_ids, 0.5, 0.0)
                    hits += jnp.where(sc["binsp"][1, pl.ds(line, 1), :] == bin_ids, 0.5, 0.0)
                    errors.append(sc["colp"][...] * valid(line) * (powered * scale - hits))
                sc["acc_e"][...] += errors[0] + errors[1]
                error = jnp.concatenate(errors, axis=0)
                coarse = error.astype(BF16)
                fine = (error - coarse.astype(F32)).astype(BF16)
                stack = jnp.concatenate([coarse, fine], axis=0)
                sc["acc_h"][...] += dot_nn(stack, sc["hidp"][place])
                slope = dot_tn(stack, sc["wb2"][...])
                order = []
                for block in range(count):
                    for eighth in range(4):
                        upper = eighth >> 1
                        first = (eighth ^ upper) & 1
                        order.append(upper * half + block * 2 * STEP + first * STEP)
                value = gathered(slope, order) * sc["sl2"][place]
                sc["og"][place] = value
                sc["grad"][place] = value.astype(BF16)
                sc["acc_b"][1] += column_sums(value)
                publish(OUTER, group, at, value)

        for part in EDGE_PARTS if group == EDGE else (MIDDLE_PART,):
            send_halo(OUTER, part)

    def near_one(kind, tag, step):
        tall = sc["slots_" + tag].shape[1]
        peer = lax.rem(spot + step, near)
        return pltpu.make_async_remote_copy(
            src_ref=sc["own_" + tag].at[pl.ds(pl.multiple_of(peer * tall, 16), tall)],
            dst_ref=sc["slots_" + tag].at[step],
            send_sem=sc["near_send"].at[kind, 0, step],
            recv_sem=sc["near_recv"].at[kind, 0, step],
            device_id=near_device(peer),
            device_id_type=MESH,
        )

    def far_one(kind, tag, step):
        return pltpu.make_async_remote_copy(
            src_ref=sc["mid_" + tag].at[tier],
            dst_ref=sc["mid_" + tag].at[tier],
            send_sem=sc["far_send"].at[kind, step],
            recv_sem=sc["far_recv"].at[kind, step],
            device_id=far_device(lax.rem(tier + step, far)),
            device_id_type=MESH,
        )

    def near_two(kind, tag, step):
        return pltpu.make_async_remote_copy(
            src_ref=sc["all_" + tag].at[spot],
            dst_ref=sc["all_" + tag].at[spot],
            send_sem=sc["near_send"].at[kind, 1, step],
            recv_sem=sc["near_recv"].at[kind, 1, step],
            device_id=near_device(lax.rem(spot + step, near)),
            device_id_type=MESH,
        )

    def pack_taps(own):
        turned = {name: jnp.transpose(sc["t_" + name][...]) for name in ("edge", "middle")}
        for across in range(TAPS):
            for down in range(TAPS):
                sides = [0.0, 0.0]
                for name, start, part in block_places(down, across):
                    sides[part] = sides[part] + turned[name][start : start + CHANS]
                total = sides[0] + pltpu.roll(sides[1], CHANS, 1)
                packed = jnp.where(
                    halves_mask((CHANS // 2, LANES)),
                    total[: CHANS // 2],
                    pltpu.roll(total[CHANS // 2 :], CHANS, 1),
                )
                start = (down * TAPS + across) * (CHANS // 2)
                own[start : start + CHANS // 2, :] = packed.astype(BF16)

    def two_rows(parts):
        value = jnp.sum(parts, axis=0, keepdims=True)
        coarse = value.astype(BF16).astype(F32)
        at = lax.broadcasted_iota(jnp.int32, (2 * STEP, LANES), 0)
        return jnp.where(at == 0, coarse, jnp.where(at == 1, value - coarse, 0.0)).astype(BF16)

    def start_sum(kind, tag):
        for step in range(1, near):
            near_one(kind, tag, step).start()

    def middle_sum(kind, tag):
        for step in range(1, near):
            near_one(kind, tag, step).wait()
        tall = sc["slots_" + tag].shape[1]
        total = sc["own_" + tag][pl.ds(pl.multiple_of(spot * tall, 16), tall), :].astype(F32)
        for step in range(1, near):
            total = total + sc["slots_" + tag][step].astype(F32)
        sc["mid_" + tag][tier] = total.astype(BF16)
        for step in range(1, far):
            far_one(kind, tag, step).start()

    def late_sum(kind, tag):
        for step in range(1, far):
            far_one(kind, tag, step).wait()
        total = sc["mid_" + tag][0].astype(F32)
        for level in range(1, far):
            total = total + sc["mid_" + tag][level].astype(F32)
        sc["all_" + tag][spot] = total.astype(BF16)
        for step in range(1, near):
            near_two(kind, tag, step).start()

    def end_sum(kind, tag, out):
        for step in range(1, near):
            near_two(kind, tag, step).wait()
        out[...] = sc["all_" + tag][...]

    if relays:

        @pl.when(own_group)
        def _():
            for piece in relay_pieces():
                relay_forward(*piece).wait_send()

    with jax.named_scope("taps2"):
        add_taps(ACT, MIDDLE)
        add_taps(ACT, EDGE)
        pack_taps(sc["own_b"])
        both = sc["acc_h"][: 2 * BINS, :] + sc["acc_h"][2 * BINS :, :]
        both = both[:BINS] + pltpu.roll(both[BINS:], CHANS, 1)
        tally = jnp.sum(sc["acc_e"][...], axis=1, keepdims=True)
        coarse = tally.astype(BF16).astype(F32)
        lane = lax.broadcasted_iota(jnp.int32, (BINS, LANES), 1)
        sides = jnp.where(
            lane < CHANS + CHANS // 2,
            jnp.broadcast_to(coarse, (BINS, LANES)),
            jnp.broadcast_to(tally - coarse, (BINS, LANES)),
        )
        both = jnp.where(lane < CHANS, both, sides)
        both = jnp.concatenate([both, jnp.zeros((8, LANES), F32)], axis=0)
        sc["own_b"][CONV_ROWS : CONV_ROWS + BINS + 8, :] = both.astype(BF16)
        start = CONV_ROWS + BINS + 8
        sc["own_b"][start : start + 16, :] = two_rows(sc["acc_b"][1])
        start_sum(1, "b")

    with jax.named_scope("convt2"):

        def convt2_body(kind, at):
            place = kind * STEP + at
            value = conv(OUTER, 2, kind, at) * sc["sl1"][place]
            sc["grad"][place] = value.astype(BF16)
            sc["acc_b"][0] += column_sums(value)
            publish(INNER, kind, at, value)

        def convt2_after(part):
            if part == MIDDLE_PART:
                add_taps(PAIR, MIDDLE)
                middle_sum(1, "b")

        conv_steps(OUTER, convt2_body, INNER, convt2_after)

    with jax.named_scope("taps1"):
        add_taps(PAIR, EDGE)
        pack_taps(sc["own_a"])
        sc["own_a"][CONV_ROWS : CONV_ROWS + 16, :] = two_rows(sc["acc_b"][0])
        start_sum(0, "a")
    with jax.named_scope("convt1"):

        def convt1_body(kind, at):
            place = kind * STEP + at
            one, two = lines(kind, at)
            value = sc["og"][place] + conv(INNER, 3, kind, at)
            for tile in range(cols // LANES):
                turned = jnp.transpose(value[tile * LANES : (tile + 1) * LANES])
                sc["p32"][tile, pl.ds(one, CHANS, stride=rows), :] = turned[:CHANS]
                sc["p32"][tile, pl.ds(two, CHANS, stride=rows), :] = turned[CHANS:]

        def convt1_after(part):
            if part == MIDDLE_PART:
                middle_sum(0, "a")
                late_sum(1, "b")
            if part == EDGE_PARTS[0]:
                late_sum(0, "a")

        conv_steps(INNER, convt1_body, None, convt1_after)

        @pl.loop(0, CHANS, unroll=4)
        def _(chan):
            for tile in range(cols // LANES):
                out_pair[chan, :, tile * LANES : (tile + 1) * LANES] = sc["p32"][
                    tile, pl.ds(chan * rows, rows), :
                ].astype(BF16)

    with jax.named_scope("end_sums"):
        end_sum(1, "b", out_b)
        end_sum(0, "a", out_a)


def finish_kernel(pair, sums_a, sums_b, mask_v, out_pair, c1w, c1b, c2w, c2b, hgw, hgb):
    out_pair[...] = pair[...]
    scale = 1.0 / jnp.sum(mask_v[...].astype(F32))
    for sums, weight, bias, extra in ((sums_a, c1w, c1b, 0), (sums_b, c2w, c2b, BINS + 8)):
        for tap in range(TAPS * TAPS):
            start = tap * (CHANS // 2)
            value = sums[start : start + CHANS // 2, :].astype(F32) * scale
            weight[tap // TAPS, tap % TAPS, : CHANS // 2, :] = value[:, :CHANS]
            weight[tap // TAPS, tap % TAPS, CHANS // 2 :, :] = value[:, CHANS:]
        start = CONV_ROWS + extra
        total = sums[start : start + 16, :].astype(F32)
        total = jnp.sum(total, axis=0, keepdims=True) * scale
        bias[...] = total[:, :CHANS] + total[:, CHANS:]
    head = sums_b[CONV_ROWS : CONV_ROWS + BINS + 8, :].astype(F32)[:BINS] * scale
    nbins = hgw.shape[0]
    hgw[...] = head[:nbins, :CHANS]
    head = jnp.concatenate([head, jnp.zeros((LANES - BINS, LANES), F32)], axis=0)
    head = jnp.transpose(head)
    middle = CHANS + CHANS // 2
    hgb[...] = head[CHANS : CHANS + 1, :nbins] + head[middle : middle + 1, :nbins]


def on_device(pair, w1, b1, w2, b2, hw, hb, bins, mask):
    nrow = lax.axis_size("ri")
    ncol = lax.axis_size("rj")
    rows, cols = bins.shape
    nbins = hw.shape[1]
    near = GROUP * ncol
    rows_a = chunk_rows(CONV_ROWS + 16, near)
    rows_b = chunk_rows(CONV_ROWS + BINS + 24, near)
    items = scratch_list(rows, cols, nrow, ncol)
    vmem = pl.BlockSpec(memory_space=pltpu.VMEM)
    smem = pl.BlockSpec(memory_space=pltpu.SMEM)
    mask_v = mask.reshape(-1, LANES)
    params = dict(vmem_limit_bytes=56 * 1024 * 1024)
    grad_pair, sums_a, sums_b = pl.pallas_call(
        functools.partial(mega_kernel, tuple(items), nrow, ncol),
        out_shape=[
            jax.ShapeDtypeStruct((CHANS, rows, cols), BF16),
            jax.ShapeDtypeStruct((near, rows_a, LANES), BF16),
            jax.ShapeDtypeStruct((near, rows_b, LANES), BF16),
        ],
        in_specs=[vmem, smem] + [vmem] * 8,
        out_specs=[vmem] * 3,
        scratch_shapes=list(items.values()),
        compiler_params=pltpu.CompilerParams(collective_id=0, has_side_effects=True, **params),
    )(
        pair, mask, mask_v, w1, b1.reshape(1, -1), w2, b2.reshape(1, -1), hw.T, hb.reshape(1, -1), bins
    )
    shape = (TAPS, TAPS, CHANS, CHANS)
    outs = pl.pallas_call(
        finish_kernel,
        out_shape=[
            jax.ShapeDtypeStruct((CHANS, rows, cols), BF16),
            jax.ShapeDtypeStruct(shape, F32),
            jax.ShapeDtypeStruct((1, CHANS), F32),
            jax.ShapeDtypeStruct(shape, F32),
            jax.ShapeDtypeStruct((1, CHANS), F32),
            jax.ShapeDtypeStruct((nbins, CHANS), F32),
            jax.ShapeDtypeStruct((1, nbins), F32),
        ],
        in_specs=[vmem] * 4,
        out_specs=[vmem] * 7,
        compiler_params=pltpu.CompilerParams(**params),
    )(grad_pair, sums_a.reshape(-1, LANES), sums_b.reshape(-1, LANES), mask_v)
    gp, c1w, c1b, c2w, c2b, hgw, hgb = outs
    return gp, c1w, c1b.reshape(-1), c2w, c2b.reshape(-1), hgw.T, hgb.reshape(-1)


def solution(mesh):
    return jax.shard_map(
        on_device,
        mesh=mesh,
        in_specs=(P(None, "ri", "rj"), P(), P(), P(), P(), P(), P(), P("ri", "rj"), P()),
        out_specs=(P(None, "ri", "rj"), P(), P(), P(), P(), P(), P()),
        check_vma=False,
    )
```

```python
import functools

import jax
import jax.numpy as jnp
from jax import lax
from jax.experimental import pallas as pl
from jax.experimental.pallas import tpu as pltpu
from jax.sharding import PartitionSpec as P

TAPS = 3
STEP = 8
CHANS = 64
LANES = 128
BINS = 40
MESH = pl.DeviceIdType.MESH
F32 = jnp.float32
BF16 = jnp.bfloat16
PAIR, ACT, OUTER, INNER = range(4)
EDGE_PARTS = ((0, 4), (4, 8))
MIDDLE_PART = (8, 16)
SIDES = ((-1, 0), (1, 0), (-1, -1), (-1, 1), (1, -1), (1, 1), (0, -1), (0, 1))
MESSAGES = tuple((side, part) for part in EDGE_PARTS for side in SIDES) + tuple(
    (side, MIDDLE_PART) for side in SIDES if side[0] == 0
)
EDGE, MIDDLE = 0, 1
OWN_BLOCKS = ((1, 4), (2, 3))
HALO_BLOCKS = (0, 5)
PLACES = (0, 3, 1, 2)
GROUP = 2
CONV_ROWS = TAPS * TAPS * CHANS // 2


def dot_nt(a, b):
    return lax.dot_general(a, b, (((1,), (1,)), ((), ())), preferred_element_type=F32)


def dot_tn(a, b):
    return lax.dot_general(a, b, (((0,), (0,)), ((), ())), preferred_element_type=F32)


def dot_nn(a, b):
    return jnp.dot(a, b, preferred_element_type=F32)


def halves_mask(shape):
    return lax.broadcasted_iota(jnp.int32, shape, len(shape) - 1) < CHANS


def chunk_rows(used, chunks):
    return -(-used // (16 * chunks)) * 16


def block_places(down, across):
    found = []
    for name, outs in (("edge", OWN_BLOCKS[EDGE]), ("middle", OWN_BLOCKS[MIDDLE])):
        for part, block in enumerate(outs):
            source = block + down - 1
            flat = OWN_BLOCKS[EDGE] + OWN_BLOCKS[MIDDLE]
            if source in flat:
                start = across * 2 * LANES + flat.index(source) * CHANS
            else:
                start = TAPS * 2 * LANES + across * LANES + HALO_BLOCKS.index(source) * CHANS
            found.append((name, start, part))
    return found


def scratch_list(rows, cols, nrow, ncol):
    pairs = rows // 2
    count = cols // rows
    near = GROUP * ncol
    far = nrow // GROUP
    rows_a = chunk_rows(CONV_ROWS + 16, near)
    rows_b = chunk_rows(CONV_ROWS + BINS + 24, near)
    dma = pltpu.SemaphoreType.DMA
    items = dict(
        p32=pltpu.VMEM((cols // LANES, CHANS * rows, LANES), F32),
        qa=pltpu.VMEM((4, pairs + STEP, cols, LANES), BF16),
        qb=pltpu.VMEM((4, pairs + STEP, cols + 2 * STEP, LANES), BF16),
        up=pltpu.VMEM((4, STEP, cols // 2, LANES), BF16),
        down=pltpu.VMEM((4, STEP, cols // 2, LANES), BF16),
        left=pltpu.VMEM((4, pairs, 2 * STEP, LANES), BF16),
        right=pltpu.VMEM((4, pairs, 2 * STEP, LANES), BF16),
        rows_in=pltpu.VMEM((4, 2, STEP, cols // 2, LANES), BF16),
        cols_in=pltpu.VMEM((4, 2, pairs, 2 * STEP, LANES), BF16),
        corner_in=pltpu.VMEM((4, 4, STEP, 2 * STEP, LANES), BF16),
        sl1=pltpu.VMEM((pairs, cols, LANES), F32),
        sl2=pltpu.VMEM((pairs, cols, LANES), F32),
        og=pltpu.VMEM((pairs, cols, LANES), F32),
        hid=pltpu.VMEM((pairs, cols, LANES), BF16),
        hidp=pltpu.VMEM((pairs, cols, LANES), BF16),
        grad=pltpu.VMEM((pairs, cols, LANES), BF16),
        mirror=pltpu.VMEM((count, pairs, rows, LANES), BF16),
        m32=pltpu.VMEM((count, pairs * rows, LANES), F32),
        binsend=pltpu.VMEM((cols, LANES), BF16),
        bins_in=pltpu.VMEM((count, rows, LANES), BF16),
        binsp=pltpu.VMEM((2, rows, cols), F32),
        w_edge=pltpu.VMEM((4, TAPS * 3 * LANES, LANES), BF16),
        w_middle=pltpu.VMEM((4, TAPS * 2 * LANES, LANES), BF16),
        wb=pltpu.VMEM((2 * BINS, LANES), BF16),
        wb2=pltpu.VMEM((4 * BINS, LANES), BF16),
        hwp=pltpu.VMEM((BINS, CHANS), F32),
        small=pltpu.VMEM((8, LANES), F32),
        hbias=pltpu.VMEM((BINS, cols), F32),
        colm=pltpu.VMEM((cols, LANES), F32),
        colp=pltpu.VMEM((BINS, cols), F32),
        t_edge=pltpu.VMEM((LANES, TAPS * 3 * LANES), F32),
        t_middle=pltpu.VMEM((LANES, TAPS * 2 * LANES), F32),
        acc_b=pltpu.VMEM((2, 8, LANES), F32),
        acc_h=pltpu.VMEM((4 * BINS, LANES), F32),
        acc_e=pltpu.VMEM((BINS, cols), F32),
        own_a=pltpu.VMEM((near * rows_a, LANES), BF16),
        own_b=pltpu.VMEM((near * rows_b, LANES), BF16),
        slots_a=pltpu.VMEM((near, rows_a, LANES), BF16),
        slots_b=pltpu.VMEM((near, rows_b, LANES), BF16),
        mid_a=pltpu.VMEM((far, rows_a, LANES), BF16),
        mid_b=pltpu.VMEM((far, rows_b, LANES), BF16),
        all_a=pltpu.VMEM((near, rows_a, LANES), BF16),
        all_b=pltpu.VMEM((near, rows_b, LANES), BF16),
        halo_send=dma((4, len(MESSAGES))),
        halo_recv=dma((4, len(MESSAGES))),
        mir_send=dma((count, 4)),
        mir_recv=dma((count, 4)),
        mir_own=dma((4,)),
        relay=pltpu.VMEM((count, 2, STEP, 2 * STEP, LANES), BF16),
        relay_recv=dma((count, 2)),
        relay_send=dma((count, 2)),
        bin_send=dma((count,)),
        bin_recv=dma((count,)),
        near_send=dma((2, 2, near)),
        near_recv=dma((2, 2, near)),
        far_send=dma((2, far)),
        far_recv=dma((2, far)),
    )
    return items


def mega_kernel(
    names, nrow, ncol,
    pair, mask_s, mask_v, w1, b1, w2, b2, hw, hb, bins, out_pair, out_a, out_b, *scratch
):
    sc = dict(zip(names, scratch))
    rows, cols = bins.shape
    pairs = rows // 2
    groups = pairs // STEP
    count = cols // rows
    half = cols // 2
    near = GROUP * ncol
    far = nrow // GROUP
    row = lax.axis_index("ri")
    column = lax.axis_index("rj")
    slot = lax.rem(row, count)
    far_column = lax.div(row, count)
    own_group = far_column == column
    relays = ncol == 2
    spot = lax.rem(row, GROUP) + GROUP * column
    tier = lax.div(row, GROUP)
    barrier = pltpu.get_barrier_semaphore()

    qa, qb = sc["qa"], sc["qb"]

    def near_device(place):
        return (tier * GROUP + lax.rem(place, GROUP), lax.div(place, GROUP))

    def far_device(level):
        return (level * GROUP + lax.rem(row, GROUP), column)

    def side_exists(side):
        dr, dc = side
        there = None
        for step, here, size in ((dr, row, nrow), (dc, column, ncol)):
            if step:
                one = here > 0 if step < 0 else here < size - 1
                there = one if there is None else jnp.logical_and(there, one)
        return there

    def side_device(side):
        return (row + side[0], column + side[1])

    def meets_self(block):
        return jnp.logical_and(own_group, slot == block)

    def partner(block):
        return (count * column + block, far_column)

    def signal(device):
        pl.semaphore_signal(barrier, inc=1, device_id=device, device_id_type=MESH)

    for side in SIDES:

        @pl.when(side_exists(side))
        def _():
            signal(side_device(side))

    for block in range(count):

        @pl.when(jnp.logical_not(meets_self(block)))
        def _():
            signal(partner(block))

    if relays:

        @pl.when(jnp.logical_not(own_group))
        def _():
            for block in range(count):
                signal((count * column + block, column))

    @pl.loop(1, near)
    def _(step):
        signal(near_device(lax.rem(spot + step, near)))

    @pl.loop(1, far)
    def _(step):
        signal(far_device(lax.rem(tier + step, far)))

    @pl.loop(0, CHANS, unroll=4)
    def _(chan):
        for tile in range(cols // LANES):
            sc["p32"][tile, pl.ds(chan * rows, rows), :] = pair[
                chan, :, tile * LANES : (tile + 1) * LANES
            ].astype(F32)

    lane_low = halves_mask((1, LANES))
    zero8 = jnp.zeros((STEP, LANES), F32)
    low = halves_mask((half, LANES))

    def publish(field, kind, at, value):
        place = kind * STEP + at
        qa[field, place] = value.astype(BF16)
        qb[field, place] = jnp.concatenate([zero8, value, zero8], axis=0).astype(BF16)
        sc["left"][field, place] = value[: 2 * STEP].astype(BF16)
        sc["right"][field, place] = value[cols - 2 * STEP :].astype(BF16)
        if kind == EDGE:
            turned = pltpu.roll(value, CHANS, 1)
            sc["up"][field, at] = jnp.where(low, value[:half], turned[half:]).astype(BF16)
            sc["down"][field, at] = jnp.where(low, turned[:half], value[half:]).astype(BF16)

    def halo_source(field, message):
        (dr, dc), (start, stop) = message
        if dc == 0:
            return sc["up" if dr < 0 else "down"].at[field, pl.ds(start, stop - start)]
        return sc["left" if dc < 0 else "right"].at[field, pl.ds(start, stop - start)]

    def halo_target(field, message):
        (dr, dc), (start, stop) = message
        if dc == 0:
            name, index = "rows_in", 0 if dr < 0 else 1
        elif dr == 0:
            name, index = "cols_in", 0 if dc < 0 else 1
        else:
            name, index = "corner_in", (0 if dr < 0 else 2) + (0 if dc < 0 else 1)
        return sc[name].at[field, index, pl.ds(start, stop - start)]

    def halo_copy(field, message):
        (dr, dc), part = message
        back = ((-dr, -dc), part)
        return pltpu.make_async_remote_copy(
            src_ref=halo_source(field, message),
            dst_ref=halo_target(field, back),
            send_sem=sc["halo_send"].at[field, MESSAGES.index(message)],
            recv_sem=sc["halo_recv"].at[field, MESSAGES.index(back)],
            device_id=side_device((dr, dc)),
            device_id_type=MESH,
        )

    def halo_arrival(field, message):
        index = MESSAGES.index(message)
        return pltpu.make_async_remote_copy(
            src_ref=halo_source(field, message),
            dst_ref=halo_target(field, message),
            send_sem=sc["halo_send"].at[field, index],
            recv_sem=sc["halo_recv"].at[field, index],
            device_id=side_device(message[0]),
            device_id_type=MESH,
        )

    def send_halo(field, part):
        for message in MESSAGES:
            if message[1] == part:

                @pl.when(side_exists(message[0]))
                def _():
                    halo_copy(field, message).start()

    def wait_halo(field, messages):
        for message in messages:

            @pl.when(side_exists(message[0]))
            def _():
                halo_arrival(field, message).wait()

    def place_rows(field, part):
        wait_halo(field, [m for m in MESSAGES if m[1] == part and m[0][0] != 0])

        @pl.loop(*part, unroll=4)
        def _(at):
            above = sc["rows_in"][field, 0, at].astype(F32)
            below = sc["rows_in"][field, 1, at].astype(F32)
            start = jnp.where(low, above, pltpu.roll(below, CHANS, 1))
            rest = jnp.where(low, pltpu.roll(above, CHANS, 1), below)
            wide = jnp.concatenate([start, rest], axis=0)
            qa[field, pairs + at] = wide.astype(BF16)
            edges = []
            for edge in (0, 1):
                upper = sc["corner_in"][field, edge, at].astype(F32)
                lower = sc["corner_in"][field, 2 + edge, at].astype(F32)
                both = pltpu.roll(jnp.where(lane_low, lower, upper), CHANS, 1)
                edges.append(both[STEP:] if edge == 0 else both[:STEP])
            wide = jnp.concatenate([edges[0], wide, edges[1]], axis=0)
            qb[field, pairs + at] = wide.astype(BF16)

    def place_cols(field, parts, starts):
        wait_halo(field, [m for m in MESSAGES if m[0][0] == 0 and m[1] in parts])
        for start in starts:

            @pl.loop(start, start + 4, unroll=4)
            def _(at):
                own = sc["left"][field, at].astype(F32)
                come = sc["cols_in"][field, 0, at].astype(F32)
                both = jnp.concatenate([come[STEP:], own[:STEP]], axis=0)
                qb[field, at, : 2 * STEP, :] = both.astype(BF16)
                own = sc["right"][field, at].astype(F32)
                come = sc["cols_in"][field, 1, at].astype(F32)
                both = jnp.concatenate([own[STEP:], come[:STEP]], axis=0)
                qb[field, at, cols:, :] = both.astype(BF16)

    def taps(field, kind, at):
        starts = (at, STEP + at)
        parts = [qb[field, start, :cols, :] for start in starts]
        parts += [qa[field, start] for start in starts]
        parts += [qb[field, start, 2 * STEP :, :] for start in starts]
        if kind == EDGE:
            start = pairs + at
            parts += [qb[field, start, :cols, :], qa[field, start], qb[field, start, 2 * STEP :, :]]
        return jnp.concatenate(parts, axis=1)

    def conv(field, which, kind, at):
        weight = sc["w_edge" if kind == EDGE else "w_middle"]
        return dot_nn(taps(field, kind, at), weight[which])

    def add_taps(field, kind):
        name = "t_edge" if kind == EDGE else "t_middle"
        sc[name][...] = jnp.zeros(sc[name].shape, F32)

        @pl.loop(0, STEP, unroll=8)
        def _(at):
            sc[name][...] += dot_tn(sc["grad"][kind * STEP + at], taps(field, kind, at))

    def lines(kind, at):
        return (kind * STEP + at, rows - STEP * (kind + 1) + at)

    def column_sums(value):
        total = value[:STEP]
        for start in range(STEP, cols, STEP):
            total = total + value[start : start + STEP]
        return total

    def publish_pair(kind):
        @pl.loop(0, STEP, unroll=2)
        def _(at):
            one, two = lines(kind, at)
            value = []
            for tile in range(cols // LANES):
                upper = sc["p32"][tile, pl.ds(one, CHANS, stride=rows), :]
                lower = sc["p32"][tile, pl.ds(two, CHANS, stride=rows), :]
                value.append(jnp.transpose(jnp.concatenate([upper, lower], axis=0)))
            value = jnp.concatenate(value, axis=0)
            publish(PAIR, kind, at, value)

    for message in MESSAGES:

        @pl.when(jnp.logical_not(side_exists(message[0])))
        def _():
            for field in range(4):
                ref = halo_target(field, message)
                ref[...] = jnp.zeros(ref.shape, ref.dtype)

    publish_pair(EDGE)
    wait_count = 0
    for side in SIDES:
        wait_count = wait_count + side_exists(side).astype(jnp.int32)
    wait_count = wait_count + count - own_group.astype(jnp.int32)
    if relays:
        wait_count = wait_count + count * own_group.astype(jnp.int32)
    pl.semaphore_wait(barrier, wait_count + (near - 1) + (far - 1))
    for part in EDGE_PARTS:
        send_halo(PAIR, part)
    publish_pair(MIDDLE)
    send_halo(PAIR, MIDDLE_PART)

    text = bins[...].astype(F32)
    text = jnp.concatenate([text, jnp.zeros((LANES - rows, cols), F32)], axis=0)
    sc["binsend"][...] = jnp.transpose(text).astype(BF16)

    def bins_source(block):
        return sc["binsend"].at[pl.ds(block * rows, rows)]

    def bins_copy(block, at):
        return pltpu.make_async_remote_copy(
            src_ref=bins_source(block),
            dst_ref=sc["bins_in"].at[at],
            send_sem=sc["bin_send"].at[block],
            recv_sem=sc["bin_recv"].at[at],
            device_id=partner(block),
            device_id_type=MESH,
        )

    for block in range(count):

        @pl.when(jnp.logical_not(meets_self(block)))
        def _():
            bins_copy(block, slot).start()

        @pl.when(meets_self(block))
        def _():
            sc["bins_in"][block] = sc["binsend"][pl.ds(block * rows, rows), :]

    with jax.named_scope("weights"):
        for name in ("w_edge", "w_middle"):
            sc[name][...] = jnp.zeros(sc[name].shape, BF16)
        for which, (weight, flip) in enumerate(((w1, False), (w2, False), (w2, True), (w1, True))):
            for across in range(TAPS):
                for down in range(TAPS):
                    if flip:
                        piece = weight[TAPS - 1 - down, TAPS - 1 - across].astype(F32)
                        piece = jnp.transpose(piece).astype(BF16)
                    else:
                        piece = weight[down, across]
                    for name, start, part in block_places(down, across):
                        sc["w_" + name][
                            which, start : start + CHANS, part * CHANS : (part + 1) * CHANS
                        ] = piece
        nbins = hw.shape[0]
        sc["hwp"][...] = jnp.zeros(sc["hwp"].shape, F32)
        sc["hwp"][:nbins, :] = hw[...].astype(F32)
        flat = sc["hwp"][...]
        none = jnp.zeros_like(flat)
        both = jnp.concatenate(
            [jnp.concatenate([flat, none], axis=1), jnp.concatenate([none, flat], axis=1)], axis=0
        )
        sc["wb"][...] = (0.5 * both).astype(BF16)
        sc["wb2"][...] = jnp.concatenate([both, both], axis=0).astype(BF16)
        sc["small"][...] = jnp.full((8, LANES), -1e30, F32)
        sc["small"][0:1, :nbins] = hb[...]
        spread = jnp.broadcast_to(sc["small"][0:1, :], (LANES, LANES))
        spread = jnp.transpose(spread)[:BINS]
        for start in range(0, cols, LANES):
            sc["hbias"][:, start : start + LANES] = spread
        sc["small"][0:1, :CHANS] = b1[...]
        sc["small"][0:1, CHANS:] = b1[...]
        sc["small"][1:2, :CHANS] = b2[...]
        sc["small"][1:2, CHANS:] = b2[...]
        natural = lax.broadcasted_iota(jnp.int32, (cols, cols), 0)
        placed = lax.broadcasted_iota(jnp.int32, (cols, cols), 1)
        eighth = (natural >> 3) & 3
        upper = eighth >> 1
        goal = upper * half + (natural >> 5) * 2 * STEP + ((eighth ^ upper) & 1) * STEP
        goal = goal + (natural & 7)
        move = jnp.where(placed == goal, 1.0, 0.0).astype(BF16)
        tiles = cols // LANES
        ones_row = [mask_v[pl.ds(column * tiles + tile, 1), :] for tile in range(tiles)]
        ones_row = jnp.concatenate(ones_row, axis=1).astype(F32)
        top = lax.broadcasted_iota(jnp.int32, (2 * STEP, cols), 0) == 0
        ones_row = jnp.where(top, jnp.broadcast_to(ones_row, (2 * STEP, cols)), 0.0).astype(BF16)
        sc["colm"][...] = dot_tn(ones_row, jnp.ones((2 * STEP, LANES), BF16))
        sc["colp"][...] = jnp.broadcast_to(dot_nn(ones_row, move)[0:1], (BINS, cols))
        sc["binsp"][0] = dot_nn(bins[...].astype(F32).astype(BF16), move)
        for ref in (sc["acc_b"], sc["acc_h"], sc["acc_e"]):
            ref[...] = jnp.zeros(ref.shape, F32)
        for ref in (sc["own_a"], sc["own_b"]):
            ref[CONV_ROWS:, :] = jnp.zeros((ref.shape[0] - CONV_ROWS, LANES), BF16)

    def valid(line):
        return mask_s[row * rows + line].astype(F32)

    def pair_mask(kind, at):
        one, two = lines(kind, at)
        return sc["colm"][...] * jnp.where(lane_low, valid(one), valid(two))

    def conv_steps(field, body, sent=None, after=None):
        for part in EDGE_PARTS:
            first = part == EDGE_PARTS[0]
            starts = (part[0], part[0] + STEP)
            place_cols(field, (part, MIDDLE_PART) if first else (part,), starts)

            @pl.loop(*part, unroll=4)
            def _(at):
                body(MIDDLE, at)

            if after is not None and first:
                after(None)

        if sent is not None:
            send_halo(sent, MIDDLE_PART)
        if after is not None:
            after(MIDDLE_PART)
        for part in EDGE_PARTS:
            place_rows(field, part)

            @pl.loop(*part, unroll=4)
            def _(at):
                body(EDGE, at)

            if sent is not None:
                send_halo(sent, part)
            if after is not None:
                after(part)

    with jax.named_scope("conv1"):

        def conv1_body(kind, at):
            place = kind * STEP + at
            inner = conv(PAIR, 0, kind, at) + sc["small"][0:1, :]
            power = jnp.exp(jnp.minimum(inner, 0.0))
            value = jnp.where(inner > 0, inner, power - 1.0)
            sc["sl1"][place] = jnp.where(inner > 0, 1.0, power)
            publish(ACT, kind, at, value)

        conv_steps(PAIR, conv1_body, ACT)

    def mirror_source(block, group, part):
        return sc["hid"].at[
            pl.ds(group * STEP, STEP), pl.ds(block * rows + part * 2 * STEP, 2 * STEP)
        ]

    def mirror_target(at, group, part):
        return sc["mirror"].at[at, pl.ds(group * STEP, STEP), pl.ds(part * 2 * STEP, 2 * STEP)]

    def mirror_copy(block, at, group, part):
        piece = 2 * group + part
        return pltpu.make_async_remote_copy(
            src_ref=mirror_source(block, group, part),
            dst_ref=mirror_target(at, group, part),
            send_sem=sc["mir_send"].at[block, piece],
            recv_sem=sc["mir_recv"].at[at, piece],
            device_id=partner(block),
            device_id_type=MESH,
        )

    def mirror_own(block, group, part):
        return pltpu.make_async_copy(
            mirror_source(block, group, part),
            mirror_target(block, group, part),
            sc["mir_own"].at[2 * group + part],
        )

    def relayed(group, part, block):
        return relays and (group + part + block) % 2 == 1

    def relay_copy(block, group, part):
        return pltpu.make_async_remote_copy(
            src_ref=mirror_source(block, group, part),
            dst_ref=sc["relay"].at[block, group],
            send_sem=sc["mir_send"].at[block, 2 * group + part],
            recv_sem=sc["relay_recv"].at[block, group],
            device_id=(row, 1 - column),
            device_id_type=MESH,
        )

    def relay_forward(block, group, part):
        return pltpu.make_async_remote_copy(
            src_ref=sc["relay"].at[block, group],
            dst_ref=mirror_target(slot, group, part),
            send_sem=sc["relay_send"].at[block, group],
            recv_sem=sc["mir_recv"].at[slot, 2 * group + part],
            device_id=(count * (1 - column) + block, column),
            device_id_type=MESH,
        )

    def row_groups(eighths):
        return [rows * block + STEP * at for block in range(count) for at in eighths]

    def gathered(value, starts):
        return jnp.concatenate([value[start : start + STEP] for start in starts], axis=0)

    def send_mirror(group):
        for part in range(2):
            for block in range(count):

                @pl.when(meets_self(block))
                def _():
                    mirror_own(block, group, part).start()

                if relayed(group, part, block):

                    @pl.when(jnp.logical_not(own_group))
                    def _():
                        relay_copy(block, group, part).start()

                    @pl.when(own_group & (slot != block))
                    def _():
                        mirror_copy(block, slot, group, part).start()

                else:

                    @pl.when(jnp.logical_not(meets_self(block)))
                    def _():
                        mirror_copy(block, slot, group, part).start()

    with jax.named_scope("conv2"):

        def conv2_body(kind, at):
            place = kind * STEP + at
            outer = conv(ACT, 1, kind, at) + sc["small"][1:2, :]
            total = qa[PAIR, place].astype(F32) + outer
            power = jnp.exp(jnp.minimum(total, 0.0))
            keep = pair_mask(kind, at)
            hidden = keep * jnp.where(total > 0, total, power - 1.0)
            sc["sl2"][place] = keep * jnp.where(total > 0, 1.0, power)
            sc["hid"][place] = gathered(hidden, row_groups(PLACES)).astype(BF16)
            order = row_groups(PLACES[0:4:2]) + row_groups(PLACES[1:4:2])
            sc["hidp"][place] = gathered(hidden, order).astype(BF16)

        def conv2_after(part):
            if part == MIDDLE_PART:
                send_mirror(MIDDLE)
            if part == EDGE_PARTS[-1]:
                send_mirror(EDGE)

        conv_steps(ACT, conv2_body, None, conv2_after)

    def relay_pieces():
        for group in (MIDDLE, EDGE):
            for part in range(2):
                for block in range(count):
                    if relayed(group, part, block):
                        yield block, group, part

    if relays:

        @pl.when(own_group)
        def _():
            for piece in relay_pieces():
                relay_copy(*piece).wait_recv()
                relay_forward(*piece).start()

    with jax.named_scope("bins"):
        total = jnp.zeros((rows, cols), F32)
        for block in range(count):

            @pl.when(jnp.logical_not(meets_self(block)))
            def _():
                bins_copy(block, block).wait()

            part = move[block * rows : (block + 1) * rows]
            total = total + dot_nn(sc["bins_in"][block][:, :rows], part)
        sc["binsp"][1] = total

    bin_ids = lax.broadcasted_iota(jnp.int32, (BINS, cols), 0).astype(F32)

    def mirrored(line):
        parts = [sc["m32"][block, pl.ds(line, pairs, stride=rows), :] for block in range(count)]
        return jnp.concatenate(parts, axis=0).astype(BF16)

    for group in range(groups):
        with jax.named_scope("wait_mirror"):
            for sender in range(groups):
                for block in range(count):

                    @pl.when(jnp.logical_not(meets_self(block)))
                    def _():
                        mirror_copy(block, block, sender, group).wait()

                    @pl.when(meets_self(block))
                    def _():
                        mirror_own(block, sender, group).wait()

            @pl.loop(0, pairs, unroll=2)
            def _(at):
                for block in range(count):
                    start = pl.multiple_of(at * rows + group * 2 * STEP, 2 * STEP)
                    sc["m32"][block, pl.ds(start, 2 * STEP), :] = sc["mirror"][
                        block, at, group * 2 * STEP : (group + 1) * 2 * STEP, :
                    ].astype(F32)

        with jax.named_scope("head"):

            @pl.loop(0, STEP, unroll=4)
            def _(at):
                place = group * STEP + at
                own = dot_nt(sc["wb"][...], sc["hidp"][place])
                errors = []
                for part, line in enumerate(lines(group, at)):
                    other = dot_nt(sc["wb"][...], mirrored((2 * group + part) * STEP + at))
                    other = jnp.concatenate([other[:BINS], other[BINS:]], axis=1)
                    logits = own[part * BINS : (part + 1) * BINS] + other + sc["hbias"][...]
                    peak = jnp.max(logits, axis=0, keepdims=True)
                    powered = jnp.exp(logits - peak)
                    scale = 1.0 / jnp.sum(powered, axis=0, keepdims=True)
                    hits = jnp.where(sc["binsp"][0, pl.ds(line, 1), :] == bin_ids, 0.5, 0.0)
                    hits += jnp.where(sc["binsp"][1, pl.ds(line, 1), :] == bin_ids, 0.5, 0.0)
                    errors.append(sc["colp"][...] * valid(line) * (powered * scale - hits))
                sc["acc_e"][...] += errors[0] + errors[1]
                error = jnp.concatenate(errors, axis=0)
                coarse = error.astype(BF16)
                fine = (error - coarse.astype(F32)).astype(BF16)
                stack = jnp.concatenate([coarse, fine], axis=0)
                sc["acc_h"][...] += dot_nn(stack, sc["hidp"][place])
                slope = dot_tn(stack, sc["wb2"][...])
                order = []
                for block in range(count):
                    for eighth in range(4):
                        upper = eighth >> 1
                        first = (eighth ^ upper) & 1
                        order.append(upper * half + block * 2 * STEP + first * STEP)
                value = gathered(slope, order) * sc["sl2"][place]
                sc["og"][place] = value
                sc["grad"][place] = value.astype(BF16)
                sc["acc_b"][1] += column_sums(value)
                publish(OUTER, group, at, value)

        for part in EDGE_PARTS if group == EDGE else (MIDDLE_PART,):
            send_halo(OUTER, part)

    def near_one(kind, tag, step):
        tall = sc["slots_" + tag].shape[1]
        peer = lax.rem(spot + step, near)
        return pltpu.make_async_remote_copy(
            src_ref=sc["own_" + tag].at[pl.ds(pl.multiple_of(peer * tall, 16), tall)],
            dst_ref=sc["slots_" + tag].at[step],
            send_sem=sc["near_send"].at[kind, 0, step],
            recv_sem=sc["near_recv"].at[kind, 0, step],
            device_id=near_device(peer),
            device_id_type=MESH,
        )

    def far_one(kind, tag, step):
        return pltpu.make_async_remote_copy(
            src_ref=sc["mid_" + tag].at[tier],
            dst_ref=sc["mid_" + tag].at[tier],
            send_sem=sc["far_send"].at[kind, step],
            recv_sem=sc["far_recv"].at[kind, step],
            device_id=far_device(lax.rem(tier + step, far)),
            device_id_type=MESH,
        )

    def near_two(kind, tag, step):
        return pltpu.make_async_remote_copy(
            src_ref=sc["all_" + tag].at[spot],
            dst_ref=sc["all_" + tag].at[spot],
            send_sem=sc["near_send"].at[kind, 1, step],
            recv_sem=sc["near_recv"].at[kind, 1, step],
            device_id=near_device(lax.rem(spot + step, near)),
            device_id_type=MESH,
        )

    def pack_taps(own):
        turned = {name: jnp.transpose(sc["t_" + name][...]) for name in ("edge", "middle")}
        for across in range(TAPS):
            for down in range(TAPS):
                sides = [0.0, 0.0]
                for name, start, part in block_places(down, across):
                    sides[part] = sides[part] + turned[name][start : start + CHANS]
                total = sides[0] + pltpu.roll(sides[1], CHANS, 1)
                packed = jnp.where(
                    halves_mask((CHANS // 2, LANES)),
                    total[: CHANS // 2],
                    pltpu.roll(total[CHANS // 2 :], CHANS, 1),
                )
                start = (down * TAPS + across) * (CHANS // 2)
                own[start : start + CHANS // 2, :] = packed.astype(BF16)

    def two_rows(parts):
        value = jnp.sum(parts, axis=0, keepdims=True)
        coarse = value.astype(BF16).astype(F32)
        at = lax.broadcasted_iota(jnp.int32, (2 * STEP, LANES), 0)
        return jnp.where(at == 0, coarse, jnp.where(at == 1, value - coarse, 0.0)).astype(BF16)

    def start_sum(kind, tag):
        for step in range(1, near):
            near_one(kind, tag, step).start()

    def middle_sum(kind, tag):
        for step in range(1, near):
            near_one(kind, tag, step).wait()
        tall = sc["slots_" + tag].shape[1]
        total = sc["own_" + tag][pl.ds(pl.multiple_of(spot * tall, 16), tall), :].astype(F32)
        for step in range(1, near):
            total = total + sc["slots_" + tag][step].astype(F32)
        sc["mid_" + tag][tier] = total.astype(BF16)
        for step in range(1, far):
            far_one(kind, tag, step).start()

    def late_sum(kind, tag):
        for step in range(1, far):
            far_one(kind, tag, step).wait()
        total = sc["mid_" + tag][0].astype(F32)
        for level in range(1, far):
            total = total + sc["mid_" + tag][level].astype(F32)
        sc["all_" + tag][spot] = total.astype(BF16)
        for step in range(1, near):
            near_two(kind, tag, step).start()

    def end_sum(kind, tag, out):
        for step in range(1, near):
            near_two(kind, tag, step).wait()
        out[...] = sc["all_" + tag][...]

    if relays:

        @pl.when(own_group)
        def _():
            for piece in relay_pieces():
                relay_forward(*piece).wait_send()

    with jax.named_scope("taps2"):
        add_taps(ACT, MIDDLE)
        add_taps(ACT, EDGE)
        pack_taps(sc["own_b"])
        both = sc["acc_h"][: 2 * BINS, :] + sc["acc_h"][2 * BINS :, :]
        both = both[:BINS] + pltpu.roll(both[BINS:], CHANS, 1)
        tally = jnp.sum(sc["acc_e"][...], axis=1, keepdims=True)
        coarse = tally.astype(BF16).astype(F32)
        lane = lax.broadcasted_iota(jnp.int32, (BINS, LANES), 1)
        sides = jnp.where(
            lane < CHANS + CHANS // 2,
            jnp.broadcast_to(coarse, (BINS, LANES)),
            jnp.broadcast_to(tally - coarse, (BINS, LANES)),
        )
        both = jnp.where(lane < CHANS, both, sides)
        both = jnp.concatenate([both, jnp.zeros((8, LANES), F32)], axis=0)
        sc["own_b"][CONV_ROWS : CONV_ROWS + BINS + 8, :] = both.astype(BF16)
        start = CONV_ROWS + BINS + 8
        sc["own_b"][start : start + 16, :] = two_rows(sc["acc_b"][1])
        start_sum(1, "b")

    with jax.named_scope("convt2"):

        def convt2_body(kind, at):
            place = kind * STEP + at
            value = conv(OUTER, 2, kind, at) * sc["sl1"][place]
            sc["grad"][place] = value.astype(BF16)
            sc["acc_b"][0] += column_sums(value)
            publish(INNER, kind, at, value)

        def convt2_after(part):
            if part == MIDDLE_PART:
                add_taps(PAIR, MIDDLE)
                middle_sum(1, "b")

        conv_steps(OUTER, convt2_body, INNER, convt2_after)

    with jax.named_scope("taps1"):
        add_taps(PAIR, EDGE)
        pack_taps(sc["own_a"])
        sc["own_a"][CONV_ROWS : CONV_ROWS + 16, :] = two_rows(sc["acc_b"][0])
        start_sum(0, "a")
    with jax.named_scope("convt1"):

        def convt1_body(kind, at):
            place = kind * STEP + at
            one, two = lines(kind, at)
            value = sc["og"][place] + conv(INNER, 3, kind, at)
            for tile in range(cols // LANES):
                turned = jnp.transpose(value[tile * LANES : (tile + 1) * LANES])
                sc["p32"][tile, pl.ds(one, CHANS, stride=rows), :] = turned[:CHANS]
                sc["p32"][tile, pl.ds(two, CHANS, stride=rows), :] = turned[CHANS:]

        def convt1_after(part):
            if part is None:
                middle_sum(0, "a")
            if part == MIDDLE_PART:
                late_sum(1, "b")
            if part == EDGE_PARTS[0]:
                late_sum(0, "a")

        conv_steps(INNER, convt1_body, None, convt1_after)

        @pl.loop(0, CHANS, unroll=4)
        def _(chan):
            for tile in range(cols // LANES):
                out_pair[chan, :, tile * LANES : (tile + 1) * LANES] = sc["p32"][
                    tile, pl.ds(chan * rows, rows), :
                ].astype(BF16)

    with jax.named_scope("end_sums"):
        end_sum(1, "b", out_b)
        end_sum(0, "a", out_a)


def finish_kernel(pair, sums_a, sums_b, mask_v, out_pair, c1w, c1b, c2w, c2b, hgw, hgb):
    out_pair[...] = pair[...]
    scale = 1.0 / jnp.sum(mask_v[...].astype(F32))
    for sums, weight, bias, extra in ((sums_a, c1w, c1b, 0), (sums_b, c2w, c2b, BINS + 8)):
        for tap in range(TAPS * TAPS):
            start = tap * (CHANS // 2)
            value = sums[start : start + CHANS // 2, :].astype(F32) * scale
            weight[tap // TAPS, tap % TAPS, : CHANS // 2, :] = value[:, :CHANS]
            weight[tap // TAPS, tap % TAPS, CHANS // 2 :, :] = value[:, CHANS:]
        start = CONV_ROWS + extra
        total = sums[start : start + 16, :].astype(F32)
        total = jnp.sum(total, axis=0, keepdims=True) * scale
        bias[...] = total[:, :CHANS] + total[:, CHANS:]
    head = sums_b[CONV_ROWS : CONV_ROWS + BINS + 8, :].astype(F32)[:BINS] * scale
    nbins = hgw.shape[0]
    hgw[...] = head[:nbins, :CHANS]
    head = jnp.concatenate([head, jnp.zeros((LANES - BINS, LANES), F32)], axis=0)
    head = jnp.transpose(head)
    middle = CHANS + CHANS // 2
    hgb[...] = head[CHANS : CHANS + 1, :nbins] + head[middle : middle + 1, :nbins]


def on_device(pair, w1, b1, w2, b2, hw, hb, bins, mask):
    nrow = lax.axis_size("ri")
    ncol = lax.axis_size("rj")
    rows, cols = bins.shape
    nbins = hw.shape[1]
    near = GROUP * ncol
    rows_a = chunk_rows(CONV_ROWS + 16, near)
    rows_b = chunk_rows(CONV_ROWS + BINS + 24, near)
    items = scratch_list(rows, cols, nrow, ncol)
    vmem = pl.BlockSpec(memory_space=pltpu.VMEM)
    smem = pl.BlockSpec(memory_space=pltpu.SMEM)
    mask_v = mask.reshape(-1, LANES)
    params = dict(vmem_limit_bytes=56 * 1024 * 1024)
    grad_pair, sums_a, sums_b = pl.pallas_call(
        functools.partial(mega_kernel, tuple(items), nrow, ncol),
        out_shape=[
            jax.ShapeDtypeStruct((CHANS, rows, cols), BF16),
            jax.ShapeDtypeStruct((near, rows_a, LANES), BF16),
            jax.ShapeDtypeStruct((near, rows_b, LANES), BF16),
        ],
        in_specs=[vmem, smem] + [vmem] * 8,
        out_specs=[vmem] * 3,
        scratch_shapes=list(items.values()),
        compiler_params=pltpu.CompilerParams(collective_id=0, has_side_effects=True, **params),
    )(
        pair, mask, mask_v, w1, b1.reshape(1, -1), w2, b2.reshape(1, -1), hw.T, hb.reshape(1, -1), bins
    )
    shape = (TAPS, TAPS, CHANS, CHANS)
    outs = pl.pallas_call(
        finish_kernel,
        out_shape=[
            jax.ShapeDtypeStruct((CHANS, rows, cols), BF16),
            jax.ShapeDtypeStruct(shape, F32),
            jax.ShapeDtypeStruct((1, CHANS), F32),
            jax.ShapeDtypeStruct(shape, F32),
            jax.ShapeDtypeStruct((1, CHANS), F32),
            jax.ShapeDtypeStruct((nbins, CHANS), F32),
            jax.ShapeDtypeStruct((1, nbins), F32),
        ],
        in_specs=[vmem] * 4,
        out_specs=[vmem] * 7,
        compiler_params=pltpu.CompilerParams(**params),
    )(grad_pair, sums_a.reshape(-1, LANES), sums_b.reshape(-1, LANES), mask_v)
    gp, c1w, c1b, c2w, c2b, hgw, hgb = outs
    return gp, c1w, c1b.reshape(-1), c2w, c2b.reshape(-1), hgw.T, hgb.reshape(-1)


def solution(mesh):
    return jax.shard_map(
        on_device,
        mesh=mesh,
        in_specs=(P(None, "ri", "rj"), P(), P(), P(), P(), P(), P(), P("ri", "rj"), P()),
        out_specs=(P(None, "ri", "rj"), P(), P(), P(), P(), P(), P()),
        check_vma=False,
    )
```
